32 devices in a mesh: gx: 4 (over x, core), gy: 8 (over z, y).
Axes of the slice: x: 2, y: 2, z: 4, core: 2. Of those that a mesh axis runs over, the one named last changes fastest.
Arguments:
- adjoint: float32 [2, 256, 768, 128], P(None, 'gx', 'gy'), may hold values from -6 to 6
- medium: bfloat16 [5, 256, 768, 128], P(None, 'gx', 'gy'), may hold values from -4 to 4, as said below
- rotors: float32 [4, 2048], P(None, ('gx', 'gy')), may hold values from -0.5 to 2
- step_size: float32 [], replicated, may hold values from 0.02 to 0.1
- slot_turbine: int32 [6144], P(('gx', 'gy')), may hold values from -1 to 2047, as said below
- slot_corner: int32 [3, 6144], P(None, ('gx', 'gy')), may hold values from 0 to 112, as said below
- moved_rotors: int32 [128], P(('gx', 'gy')), may hold values from 0 to 63, as said below
- new_brick: int32 [128, 1], P(('gx', 'gy')), may hold values from 0 to 31; in each aligned block of 128 rows (0 to 127, 128 to 255, ...) at most 8 rows name the same one
Outputs:
- adjoint_out: float32 [2, 256, 768, 128], P(None, 'gx', 'gy')
- step_taken: float32 [2, 2048], P(None, ('gx', 'gy'))
- incoming: bfloat16 [256, 2048], P(('gx', 'gy'))
The draws below stay inside these ranges and needn't reach their ends.
Inputs may be any that keep to these rules, and one draw needn't show every extreme that they name: `slot_turbine`: entries are global turbine numbers or -1 for an empty slot. Every turbine is listed exactly once over all bricks. A brick lists at most 192 turbines, and some brick lists exactly 192. `slot_corner`: every listed block of 8 x 16 x 16 cells lies inside its brick. `moved_rotors`: the 4 entries of one owner are distinct. `new_brick`: over all moved rotors, no brick is named more than 8 times, a bound that some block reaches. `medium`: viscosity in 0.1 to 1, velocity in 0.2 to 1, dissipation in 0.1 to 1, coupling in -0.3 to 0.3, source in -4 to 4.
All inputs are finite; a program needn't handle non-finite values.
Results may differ from the reference program's by a relative error of at most 0.001.
Values may be sent and summed in bfloat16 or wider, within the bound.
A program may use at most 256 MiB of HBM per device.

```python
import math
import jax
import jax.numpy as jnp
import numpy as np
from jax import lax

CX = 64
CY = 96
CZ = 128
TURB_DEV = 64
MOVED_DEV = 4
KX = 8
KY = 16
KZ = 16
SWEEPS = 2
RECV = 8
BRICKS = 32
NX = 256
NY = 768
NZ = 128
TURBINES = 2048
SLOTS = 192
MOVED = 128
N_GX = 4
N_GY = 8


def loguniform_field(key, shape, low, high):
    return jnp.exp(jax.random.uniform(key, shape, jnp.float32, math.log(low), math.log(high)))


def draw_medium(key, part):
    shape = (NX, NY, NZ)
    keys = [jax.random.fold_in(key, 100 + index) for index in range(5)]
    viscous = loguniform_field(keys[0], shape, 0.1, 1.0)
    velocity = jax.random.uniform(keys[1], shape, jnp.float32, 0.2, 1.0)
    reaction = loguniform_field(keys[2], shape, 0.1, 1.0)
    coupling = jax.random.uniform(keys[3], shape, jnp.float32, -0.3, 0.3)
    source = jnp.clip(jax.random.normal(keys[4], shape, jnp.float32), -4.0, 4.0)
    return jnp.stack([viscous, velocity, reaction, coupling, source]).astype(jnp.bfloat16)


def draw_rotors(key, part):
    keys = [jax.random.fold_in(key, 200 + index) for index in range(4)]
    shape = (TURBINES,)
    offset_x = jax.random.uniform(keys[0], shape, jnp.float32, -0.5, 0.5)
    offset_y = jax.random.uniform(keys[1], shape, jnp.float32, -0.5, 0.5)
    yaw_angle = jax.random.uniform(keys[2], shape, jnp.float32, -0.5, 0.5)
    thrust = loguniform_field(keys[3], shape, 0.5, 2.0)
    return jnp.stack([offset_x, offset_y, yaw_angle, thrust])


def draw_slot_turbine(key, part):
    key_rank = jax.random.fold_in(key, 11)
    key_ids = jax.random.fold_in(key, 12)
    ordering = jax.random.permutation(key_rank, BRICKS)
    rank_of = jnp.zeros((BRICKS,), jnp.int32).at[ordering].set(jnp.arange(BRICKS, dtype=jnp.int32))
    counts = jnp.where(rank_of < BRICKS // 4, 3 * TURB_DEV, jnp.where(rank_of < BRICKS // 2, TURB_DEV, 0)).astype(jnp.int32)
    starts = jnp.cumsum(counts) - counts
    slot_number = jnp.arange(SLOTS, dtype=jnp.int32)
    filled = slot_number[None, :] < counts[:, None]
    flat_index = jnp.clip(starts[:, None] + slot_number[None, :], 0, TURBINES - 1)
    numbers = jax.random.permutation(key_ids, TURBINES).astype(jnp.int32)
    table = jnp.where(filled, numbers[flat_index], -1)
    return table.reshape(BRICKS * SLOTS).astype(jnp.int32)


def draw_slot_corner(key, part):
    shape = (BRICKS * SLOTS,)
    corner_x = jax.random.randint(jax.random.fold_in(key, 21), shape, 0, CX - KX + 1)
    corner_y = jax.random.randint(jax.random.fold_in(key, 22), shape, 0, CY - KY + 1)
    corner_z = jax.random.randint(jax.random.fold_in(key, 23), shape, 0, CZ - KZ + 1)
    return jnp.stack([corner_x, corner_y, corner_z]).astype(jnp.int32)


def draw_moved_rotors(key, part):
    keys = jax.random.split(jax.random.fold_in(key, 300), BRICKS)

    def choose_some(owner_key):
        return jax.random.permutation(owner_key, TURB_DEV)[:MOVED_DEV]
    return jax.vmap(choose_some)(keys).reshape(MOVED).astype(jnp.int32)


def level_of(own_key, dims, cuts, low, high):
    def one(dim, parts):
        steps = jax.random.uniform(jax.random.fold_in(jax.random.fold_in(own_key, 6), dim), (parts,), jnp.float32, low / len(cuts), high / len(cuts))
        return jnp.repeat(jnp.exp(steps), dims[dim] // parts).reshape((-1,) + (1,) * (len(dims) - dim - 1))

    gain = one(*cuts[0])
    for cut in cuts[1:]:
        gain = gain * one(*cut)
    return gain


def deal_out(key, own, number, rows, number_of, top, most, skew):
    ranking = jax.random.permutation(key, number_of)
    crowded, usual = load_shares(number_of, rows * top, most, skew, True), load_shares(number_of, rows * top, most, skew, False)
    places = jnp.arange(number_of)

    def named(sizes, offset_by):
        used = int((sizes > 0).sum())
        fixed = max(1, used // 4)
        moved = fixed + (places - fixed + offset_by * (used - fixed)) % max(1, number_of - fixed)
        return jnp.zeros((number_of,), jnp.int32).at[ranking[jnp.where(places < fixed, places, moved)]].set(jnp.asarray(sizes, jnp.int32))

    sizes = jnp.where(number % 4 == 0, named(crowded, number // 4), named(usual, number - number // 4 - 1))
    mixed = jax.random.permutation(jax.random.fold_in(own, 3), number_of)
    giver, taker = mixed[0:number_of // 2 * 2:2], mixed[1:number_of // 2 * 2:2]
    margin = jnp.minimum(sizes[giver] - 1, most - sizes[taker]) // 2
    margin = jnp.where((giver == ranking[0]) | (taker == ranking[0]) | (sizes[taker] == 0), 0, jnp.maximum(margin, 0))
    moved = jax.random.randint(jax.random.fold_in(own, 4), (number_of // 2,), 0, 1 << 20) % (margin + 1)
    sizes = sizes.at[giver].add(-moved).at[taker].add(moved)
    labels = jnp.searchsorted(jnp.cumsum(sizes), jnp.arange(rows * top), side="right").astype(jnp.int32)
    listing = labels.reshape(top, rows).T
    listing = listing[jax.random.permutation(jax.random.fold_in(own, 1), rows)]
    offset_by = jax.random.randint(jax.random.fold_in(own, 2), (rows, 1), 0, top)
    return jnp.take_along_axis(listing, (jnp.arange(top)[None, :] + offset_by) % top, axis=1)


def load_shares(number_of, total, most, slope, full):
    loads = [(1 << 20) // math.isqrt(standing ** slope) + 1 for standing in range(1, number_of + 1)]
    largest = most if full else min(most, max(-(-total // number_of), total * loads[0] // sum(loads)))
    least = 1 if total - largest >= number_of - 1 else 0
    given, surplus = [largest] + [least] * (number_of - 1), total - largest - least * (number_of - 1)
    while surplus > 0:
        movable = [i for i in range(1, number_of) if given[i] < largest] or [i for i in range(1, number_of) if given[i] < most]
        pool, left = sum([loads[i] for i in movable]), surplus
        for i in movable:
            addition = min(most - given[i], max(1, left * loads[i] // pool), surplus)
            given[i] = given[i] + addition
            surplus = surplus - addition
    return np.array(given)


def noise(key, dims, scale, limit, cuts=(), kind=jnp.bfloat16):
    gain = level_of(key, dims, cuts, -0.22, 0.18) if cuts else 1.0
    values = jax.random.normal(key, dims, jnp.float32) * scale * gain
    return jnp.minimum(jnp.maximum(values, -limit), limit).astype(kind)


def setup_inputs(seed: int = 0) -> dict:
    seeds = jax.random.split(jax.random.key(seed), 9)
    adjoint = noise(seeds[0], (2, NX, NY, NZ), 1.0, 6.0, ((1, 4), (2, 8)), jnp.float32)
    medium = draw_medium(jax.random.fold_in(seeds[8], 71), 0)
    rotors = draw_rotors(jax.random.fold_in(seeds[8], 71), 0)
    step_size = jnp.clip(jnp.exp(jax.random.uniform(seeds[3], (), jnp.float32, math.log(0.02), math.log(0.1))), 0.02, 0.1)
    slot_turbine = draw_slot_turbine(jax.random.fold_in(seeds[8], 71), 0)
    slot_corner = draw_slot_corner(jax.random.fold_in(seeds[8], 71), 0)
    moved_rotors = draw_moved_rotors(jax.random.fold_in(seeds[8], 71), 0)
    new_brick_keys = jax.random.split(jax.random.fold_in(seeds[7], 1), MOVED // MOVED)
    new_brick_turns = jax.random.permutation(jax.random.fold_in(seeds[7], 3), MOVED // MOVED)
    new_brick = jax.vmap(lambda own, number: deal_out(jax.random.fold_in(seeds[7], 2), own, number, MOVED, BRICKS, 1, RECV, 2))(new_brick_keys, new_brick_turns).reshape((MOVED, 1))
    return {"adjoint": adjoint, "medium": medium, "rotors": rotors, "step_size": step_size, "slot_turbine": slot_turbine, "slot_corner": slot_corner, "moved_rotors": moved_rotors, "new_brick": new_brick}


TAU = 0.05
SIGMA_AXIAL = 1.5
SIGMA_RADIAL = 4.0


def relax_cells(padded, viscous, velocity, reaction, coupling, source):
    fluxes = viscous[None] * padded
    side_sum = fluxes[:, 2:, 1:-1] + fluxes[:, :-2, 1:-1] + fluxes[:, 1:-1, 2:] + fluxes[:, 1:-1, :-2]
    centre = padded[:, 1:-1, 1:-1]
    inner_flux = fluxes[:, 1:-1, 1:-1]
    zero_layer = jnp.zeros_like(inner_flux[..., :1])
    vertical = jnp.concatenate([inner_flux[..., 1:], zero_layer], axis=-1) + jnp.concatenate([zero_layer, inner_flux[..., :-1]], axis=-1)
    carried = velocity[None, 2:, 1:-1] * padded[:, 2:, 1:-1]
    diagonal = 6.0 * viscous[1:-1, 1:-1] + velocity[1:-1, 1:-1] + reaction
    image_k = diagonal * centre[0] + coupling * centre[1] - side_sum[0] - vertical[0] - carried[0]
    image_e = (diagonal + reaction) * centre[1] + coupling * centre[0] - side_sum[1] - vertical[1] - carried[1]
    return jnp.stack([centre[0] + TAU * (source - image_k), centre[1] - TAU * image_e])


def disk_shape(sub_x, sub_y, yaw_angle, thrust):
    axis_x = jnp.arange(KX).astype(jnp.float32) + 0.5 - KX / 2.0
    axis_y = jnp.arange(KY).astype(jnp.float32) + 0.5 - KY / 2.0
    axis_z = jnp.arange(KZ).astype(jnp.float32) + 0.5 - KZ / 2.0
    delta_x = axis_x[None, :, None, None] - sub_x[:, None, None, None]
    delta_y = axis_y[None, None, :, None] - sub_y[:, None, None, None]
    height = axis_z[None, None, None, :]
    cosine = jnp.cos(yaw_angle)[:, None, None, None]
    sine_yaw = jnp.sin(yaw_angle)[:, None, None, None]
    along_axis = cosine * delta_x + sine_yaw * delta_y
    across = cosine * delta_y - sine_yaw * delta_x
    kernel = thrust[:, None, None, None] * jnp.exp(-along_axis * along_axis / (2.0 * SIGMA_AXIAL * SIGMA_AXIAL) - (across * across + height * height) / (2.0 * SIGMA_RADIAL * SIGMA_RADIAL))
    return kernel, along_axis, across, cosine, sine_yaw


def disk_slopes(blocks, sub_x, sub_y, yaw_angle, thrust):
    kernel, along_axis, across, cosine, sine_yaw = disk_shape(sub_x, sub_y, yaw_angle, thrust)
    axial_part = along_axis / (SIGMA_AXIAL * SIGMA_AXIAL)
    radial_part = across / (SIGMA_RADIAL * SIGMA_RADIAL)
    slope_x = kernel * (axial_part * cosine - radial_part * sine_yaw)
    slope_y = kernel * (axial_part * sine_yaw + radial_part * cosine)
    return jnp.stack([jnp.sum(blocks * slope_x, axis=(1, 2, 3)), jnp.sum(blocks * slope_y, axis=(1, 2, 3))])


def reference(adjoint, medium, rotors, step_size, slot_turbine, slot_corner, moved_rotors, new_brick):
    coefficients = medium.astype(jnp.float32)
    plane_pad = ((1, 1), (1, 1), (0, 0))
    viscous = jnp.pad(coefficients[0], plane_pad)
    velocity = jnp.pad(coefficients[1], plane_pad)
    current = adjoint
    for repeat in range(SWEEPS):
        padded = jnp.pad(current, ((0, 0), (1, 1), (1, 1), (0, 0)))
        current = relax_cells(padded, viscous, velocity, coefficients[2], coefficients[3], coefficients[4])
    weights = current[0]
    bricks = N_GX * N_GY
    slot_brick = jnp.arange(bricks * SLOTS, dtype=jnp.int32) // SLOTS
    first_x = ((slot_brick // N_GY) * CX + slot_corner[0]).astype(jnp.int32)
    first_y = ((slot_brick % N_GY) * CY + slot_corner[1]).astype(jnp.int32)
    first_z = slot_corner[2].astype(jnp.int32)

    def cut_block(start_x, start_y, start_z):
        return lax.dynamic_slice(weights, (start_x, start_y, start_z), (KX, KY, KZ))

    blocks = jax.vmap(cut_block)(first_x, first_y, first_z)
    occupied = slot_turbine >= 0
    safe_ids = jnp.maximum(slot_turbine, 0)
    rotor_data = rotors[:, safe_ids]
    slopes = disk_slopes(blocks, rotor_data[0], rotor_data[1], rotor_data[2], rotor_data[3])
    slopes = jnp.where(occupied[None, :], slopes, jnp.zeros_like(slopes))
    gradient = jnp.zeros((2, TURBINES), jnp.float32).at[:, safe_ids].add(slopes)
    step_taken = jnp.clip(-step_size * gradient, -0.5, 0.5)
    owners = jnp.arange(MOVED, dtype=jnp.int32) // MOVED_DEV
    turbine = owners * TURB_DEV + moved_rotors
    sub_x = rotors[0, turbine] + step_taken[0, turbine]
    sub_y = rotors[1, turbine] + step_taken[1, turbine]
    kernel = disk_shape(sub_x, sub_y, rotors[2, turbine], rotors[3, turbine])[0]
    values = kernel.reshape(MOVED, KX * KY * KZ).astype(jnp.bfloat16)
    target = new_brick[:, 0]
    position = jnp.arange(MOVED, dtype=jnp.int32)
    earlier = position[:, None] > position[None, :]
    slot_rank = jnp.sum(((target[:, None] == target[None, :]) & earlier).astype(jnp.int32), axis=1).astype(jnp.int32)
    row_index = (target * RECV + slot_rank).astype(jnp.int32)
    incoming = jnp.zeros((bricks * RECV, KX * KY * KZ), jnp.bfloat16).at[row_index].set(values)
    return current, step_taken, incoming
```

```python
import functools

import jax
import jax.numpy as jnp
import numpy as np
from jax import lax
from jax.experimental import pallas as pl
from jax.experimental.pallas import tpu as pltpu
from jax.sharding import PartitionSpec as P

KX = 8
KY = 16
KZ = 16
SWEEPS = 2
RECV = 8
EDGE = 16
CHUNK = 8
STRIP = 16
LANES = 128
BATCH = 16


TAU = 0.05
SIGMA_AXIAL = 1.5
SIGMA_RADIAL = 4.0
MESH = pl.DeviceIdType.MESH


def sweep_first(med, src, fb):
    part, mid = pl.ds(0, src.shape[2]), pl.ds(8, src.shape[2])
    viscous = med[0, 0, part].astype(jnp.float32)
    for c in range(2):
        fb[c, 1, mid] = viscous * src[c, 0, part]


def sweep_plane(med, src, dst, keep, fb, x, fresh, more=True):
    rows, depth = src.shape[2:]
    col = lax.broadcasted_iota(jnp.int32, (STRIP, depth), 1)
    bottom, top = col == 0, col == depth - 1
    if more:
        for start in range(0, rows, STRIP):
            part = pl.ds(start, STRIP)
            viscous = med[0, x + 1, part].astype(jnp.float32)
            for c in range(2):
                fb[c, x + 2, pl.ds(8 + start, STRIP)] = viscous * src[c, x + 1, part]
    for start in range(0, rows, STRIP):
        part, mid = pl.ds(start, STRIP), pl.ds(8 + start, STRIP)
        below, above = pl.ds(7 + start, STRIP), pl.ds(9 + start, STRIP)
        coupling = med[3, x, part].astype(jnp.float32)
        if more:
            pull = med[0, x + 1, part].astype(jnp.float32) + med[1, x + 1, part].astype(jnp.float32)
        if fresh:
            scaled = TAU * med[2, x, part].astype(jnp.float32)
            viscous = med[0, x, part].astype(jnp.float32)
            first = 1.0 - TAU * (6.0 * viscous + med[1, x, part].astype(jnp.float32)) - scaled
            kept = first, first - scaled
            keep[0, x, part], keep[1, x, part] = kept
        else:
            kept = keep[0, x, part], keep[1, x, part]
        values = src[0, x, part], src[1, x, part]
        for c in range(2):
            flux = fb[c, x + 1, mid]
            total = fb[c, x, mid] + jnp.where(bottom, 0.0, pltpu.roll(flux, 1, 1))
            total = total + jnp.where(top, 0.0, pltpu.roll(flux, depth - 1, 1))
            if more:
                total = total + pull * src[c, x + 1, part]
            total = total + (fb[c, x + 1, below] + fb[c, x + 1, above])
            total = total - coupling * values[1 - c]
            if c == 0:
                total = total + med[4, x, part].astype(jnp.float32)
            dst[c, x, part] = kept[c] * values[c] + TAU * total


def pack_tables(me, rotors, listed, moved, target, pack):
    turb_dev, slots, moved_dev = rotors.shape[1], listed.shape[1], moved.shape[1]
    pack[...] = jnp.full(pack.shape, -1.0, jnp.float32)
    own = pl.ds(0, turb_dev)
    pack[0:2, own] = rotors[0:2]
    pack[2:3, own] = jnp.cos(rotors[2:3])
    pack[3:4, own] = jnp.sin(rotors[2:3])
    pack[4:5, own] = rotors[3:4]
    for group in range(-(-slots // LANES)):
        size = min(LANES, slots - group * LANES)
        pack[5 + group : 6 + group, pl.ds(0, size)] = listed[
            :, pl.ds(group * LANES, size)
        ].astype(jnp.float32)
    full = pack[...]
    lane = lax.broadcasted_iota(jnp.int32, full.shape, 1)
    field = lax.broadcasted_iota(jnp.int32, full.shape, 0) + 2
    line = jnp.full((1, LANES), -1.0, jnp.float32)
    chosen, wanted = moved[...].astype(jnp.float32), target[...].astype(jnp.float32)
    for j in range(moved_dev):
        local = chosen[:, j : j + 1]
        picked = jnp.sum(
            jnp.where(lane.astype(jnp.float32) == local, full, 0.0), axis=1, keepdims=True
        )
        here = (lane == moved_dev * field + j) & (field < 7)
        spread = jnp.sum(jnp.where(here, picked, 0.0), axis=0, keepdims=True)
        place = lane[0:1]
        for f in range(2, 7):
            line = jnp.where(place == moved_dev * f + j, spread, line)
        line = jnp.where(place == j, wanted[:, j : j + 1], line)
        number = (me * turb_dev).astype(jnp.float32) + local
        line = jnp.where(place == moved_dev + j, number, line)
    pack[7:8] = line


def greet(sizes):
    n_gx, n_gy = sizes
    gx, gy = lax.axis_index("gx"), lax.axis_index("gy")
    barrier = pltpu.get_barrier_semaphore()
    for j in range(1, n_gy):
        pl.semaphore_signal(
            barrier, inc=1, device_id=(gx, lax.rem(gy + j, n_gy)), device_id_type=MESH
        )
    for j in range(1, n_gx):
        pl.semaphore_signal(
            barrier, inc=1, device_id=(lax.rem(gx + j, n_gx), gy), device_id_type=MESH
        )
    return n_gx + n_gy - 2


def spread_y(sizes, own, every, ssem, rsem):
    n_gy = sizes[1]
    gx, gy = lax.axis_index("gx"), lax.axis_index("gy")
    return [
        pltpu.make_async_remote_copy(
            src_ref=own,
            dst_ref=every.at[gx * n_gy + gy],
            send_sem=ssem.at[j],
            recv_sem=rsem.at[j],
            device_id=(gx, lax.rem(gy + j, n_gy)),
            device_id_type=MESH,
        )
        for j in range(1, n_gy)
    ]


def spread_x(sizes, every, ssem, rsem):
    n_gx, n_gy = sizes
    gx, gy = lax.axis_index("gx"), lax.axis_index("gy")
    block = every.at[pl.ds(gx * n_gy, n_gy)]
    return [
        pltpu.make_async_remote_copy(
            src_ref=block,
            dst_ref=block,
            send_sem=ssem.at[n_gy + j],
            recv_sem=rsem.at[n_gy + j],
            device_id=(lax.rem(gx + j, n_gx), gy),
            device_id_type=MESH,
        )
        for j in range(1, n_gx)
    ]


def relax_kernel(
    sizes,
    rotors_hbm,
    listed_hbm,
    moved_hbm,
    target_hbm,
    q_hbm,
    med_hbm,
    q,
    every,
    rotors,
    listed,
    moved,
    target,
    med,
    q1,
    keep,
    fb,
    xs,
    xr,
    ys,
    yr,
    pack,
    table,
    small_sem,
    edge_sem,
    in_sem,
    ssem,
    rsem,
    tsend,
    trecv,
):
    n_gx, n_gy = sizes
    _, count, width, depth = q.shape
    chunks = count // CHUNK
    gx, gy = lax.axis_index("gx"), lax.axis_index("gy")
    x_lo, x_hi = lax.rem(gx + n_gx - 1, n_gx), lax.rem(gx + 1, n_gx)
    y_lo, y_hi = lax.rem(gy + n_gy - 1, n_gy), lax.rem(gy + 1, n_gy)
    peers = ((x_lo, gy), (x_hi, gy), (gx, y_lo), (gx, y_hi))
    q_mid, mid = pl.ds(8, width - 16), pl.ds(EDGE, width - 2 * EDGE)
    q_edges = (pl.ds(0, 8), pl.ds(width - 8, 8))
    edges = (pl.ds(0, EDGE), pl.ds(width - EDGE, EDGE))

    def fetch(which, planes, rows, sem):
        src, dst = (q_hbm.at[:], q.at[:]) if which is None else (med_hbm.at[which], med.at[which])
        return pltpu.make_async_copy(src.at[:, planes, rows], dst.at[:, planes, rows], sem)

    whole, end, every_plane = pl.ds(0, width), pl.ds(count - 1, 1), pl.ds(0, count)
    viscous, others = pl.ds(0, 1), pl.ds(1, 4)
    edge_in = []
    for i in range(2):
        edge_in.append(fetch(None, every_plane, q_edges[i], edge_sem.at[i, 0]))
        edge_in.append(fetch(viscous, every_plane, edges[i], edge_sem.at[i, 1]))
    end_in = [
        fetch(None, end, q_mid, edge_sem.at[2, 0]),
        fetch(viscous, end, mid, edge_sem.at[2, 1]),
    ]

    def chunk_in(i, size=CHUNK):
        part, all_of_it = pl.ds(i * CHUNK, size), pl.ds(i * CHUNK, CHUNK)
        return (
            fetch(None, part, q_mid, in_sem.at[i, 0]),
            fetch(viscous, part, mid, in_sem.at[i, 1]),
            fetch(others, all_of_it, whole, in_sem.at[i, 2]),
        )

    last_in = chunk_in(chunks - 1, CHUNK - 1)
    small = [
        pltpu.make_async_copy(rotors_hbm, rotors, small_sem.at[0]),
        pltpu.make_async_copy(listed_hbm, listed, small_sem.at[1]),
        pltpu.make_async_copy(moved_hbm, moved, small_sem.at[2]),
        pltpu.make_async_copy(target_hbm, target, small_sem.at[3]),
    ]
    for copy in edge_in + small:
        copy.start()
    for copy in chunk_in(0):
        copy.start()
    for copy in end_in:
        copy.start()

    @pl.loop(1, chunks - 1)
    def _(i):
        for copy in chunk_in(i):
            copy.start()

    for copy in last_in:
        copy.start()

    barrier = pltpu.get_barrier_semaphore()
    me = gx * n_gy + gy

    met = greet(sizes)
    blank = jnp.zeros((8, depth), jnp.float32)

    @pl.loop(0, count + 2, unroll=2)
    def _(x):
        for c in range(2):
            fb[c, x, pl.ds(0, 8)] = blank
            fb[c, x, pl.ds(8 + width, 8)] = blank

    for c in range(2):
        fb[c, 0, pl.ds(8, width)] = jnp.zeros((width, depth), jnp.float32)
    for copy in small:
        copy.wait()
    pack_tables(me, rotors, listed, moved, target, pack)
    pl.semaphore_wait(barrier, met)

    def remote(turn, side, src, dst):
        return pltpu.make_async_remote_copy(
            src_ref=src.at[turn, side % 2],
            dst_ref=dst.at[turn, side % 2],
            send_sem=ssem.at[turn, side],
            recv_sem=rsem.at[turn, side],
            device_id=peers[side],
            device_id_type=MESH,
        )

    def exchange_x(turn, src):
        for c in range(2):
            low, high = med[0, 0].astype(jnp.float32), med[0, count - 1].astype(jnp.float32)
            xs[turn, 0, c] = (low + med[1, 0].astype(jnp.float32)) * src[c, 0]
            xs[turn, 1, c] = high * src[c, count - 1]

        copies = [remote(turn, side, xs, xr) for side in (0, 1)]
        for copy in copies:
            copy.start()
        return copies

    def exchange_y(turn, src):
        @pl.loop(0, count, unroll=8)
        def _(x):
            low = med[0, x, pl.ds(0, EDGE)].astype(jnp.float32)[:8]
            high = med[0, x, pl.ds(width - EDGE, EDGE)].astype(jnp.float32)[8:]
            for c in range(2):
                ys[turn, 0, c, pl.ds(x, 1)] = (low * src[c, x, pl.ds(0, 8)])[:1]
                ys[turn, 1, c, pl.ds(x, 1)] = (high * src[c, x, pl.ds(width - 8, 8)])[7:]

        copies = [remote(turn, side, ys, yr) for side in (2, 3)]
        for copy in copies:
            copy.start()
        return copies

    def patch(turn, dst):
        has_hi_x = jnp.where(gx < n_gx - 1, TAU, 0.0)
        has_lo_x = jnp.where(gx > 0, TAU, 0.0)
        has_hi_y = jnp.where(gy < n_gy - 1, TAU, 0.0)
        has_lo_y = jnp.where(gy > 0, TAU, 0.0)
        for c in range(2):
            dst[c, count - 1] = dst[c, count - 1] + has_hi_x * xr[turn, 0, c]
            dst[c, 0] = dst[c, 0] + has_lo_x * xr[turn, 1, c]

        @pl.loop(0, count, unroll=8)
        def _(x):
            for c in range(2):
                last = pl.ds(width - 1, 1)
                first = pl.ds(0, 1)
                dst[c, x, last] = dst[c, x, last] + has_hi_y * yr[turn, 0, c, pl.ds(x, 1)]
                dst[c, x, first] = dst[c, x, first] + has_lo_y * yr[turn, 1, c, pl.ds(x, 1)]

    for copy in edge_in:
        copy.wait()
    copies = exchange_y(0, q)
    for copy in list(chunk_in(0)) + end_in:
        copy.wait()
    copies += exchange_x(0, q)

    table[me] = pack[...]
    along_y = spread_y(sizes, pack, table, tsend, trecv)
    for copy in along_y:
        copy.start()

    def first_sweep(x, more=True):
        sweep_plane(med, q, q1, keep, fb, x, True, more)

    sweep_first(med, q, fb)

    @pl.loop(0, CHUNK - 1, unroll=CHUNK - 1)
    def _(x):
        first_sweep(x)

    @pl.loop(1, chunks)
    def _(i):
        @pl.when(i < chunks - 1)
        def _():
            for copy in chunk_in(i):
                copy.wait()

        @pl.when(i == chunks - 1)
        def _():
            for copy in last_in:
                copy.wait()

        @pl.loop(0, CHUNK, unroll=CHUNK)
        def _(j):
            first_sweep(i * CHUNK - 1 + j)

    first_sweep(count - 1, False)

    for copy in copies:
        copy.wait()
    patch(0, q1)

    copies = exchange_x(1, q1) + exchange_y(1, q1)
    for copy in along_y:
        copy.wait()
    along_x = spread_x(sizes, table, tsend, trecv)
    for copy in along_x:
        copy.start()

    sweep_first(med, q1, fb)

    @pl.loop(0, count - 1, unroll=7)
    def _(x):
        sweep_plane(med, q1, q, keep, fb, x, False)

    sweep_plane(med, q1, q, keep, fb, count - 1, False, False)

    for copy in along_x:
        copy.wait()
    every[...] = table[...]
    for copy in copies:
        copy.wait()
    patch(1, q)


def relax(adjoint, medium, rotors, slot_turbine, moved_rotors, new_brick, sizes):
    n = sizes[0] * sizes[1]
    vmem, hbm = pl.BlockSpec(memory_space=pltpu.VMEM), pl.BlockSpec(memory_space=pltpu.HBM)
    channels, count, width, depth = adjoint.shape
    slots, moved_dev = slot_turbine.shape[0], moved_rotors.shape[0]
    return pl.pallas_call(
        functools.partial(relax_kernel, sizes),
        out_shape=(
            jax.ShapeDtypeStruct(adjoint.shape, jnp.float32),
            jax.ShapeDtypeStruct((n, 8, LANES), jnp.float32),
        ),
        in_specs=[hbm] * 6,
        out_specs=(vmem, vmem),
        scratch_shapes=[
            pltpu.VMEM(rotors.shape, jnp.float32),
            pltpu.VMEM((1, slots), jnp.int32),
            pltpu.VMEM((1, moved_dev), jnp.int32),
            pltpu.VMEM((1, moved_dev), jnp.int32),
            pltpu.VMEM(medium.shape, jnp.bfloat16),
            pltpu.VMEM(adjoint.shape, jnp.float32),
            pltpu.VMEM(adjoint.shape, jnp.float32),
            pltpu.VMEM((channels, count + 2, width + 16, depth), jnp.float32),
            pltpu.VMEM((2, 2, channels, width, depth), jnp.float32),
            pltpu.VMEM((2, 2, channels, width, depth), jnp.float32),
            pltpu.VMEM((2, 2, channels, count, depth), jnp.float32),
            pltpu.VMEM((2, 2, channels, count, depth), jnp.float32),
            pltpu.VMEM((8, LANES), jnp.float32),
            pltpu.VMEM((n, 8, LANES), jnp.float32),
            pltpu.SemaphoreType.DMA((4,)),
            pltpu.SemaphoreType.DMA((3, 2)),
            pltpu.SemaphoreType.DMA((count // CHUNK, 3)),
            pltpu.SemaphoreType.DMA((2, 4)),
            pltpu.SemaphoreType.DMA((2, 4)),
            pltpu.SemaphoreType.DMA((sizes[0] + sizes[1],)),
            pltpu.SemaphoreType.DMA((sizes[0] + sizes[1],)),
        ],
        compiler_params=pltpu.CompilerParams(
            collective_id=0, has_side_effects=True, vmem_limit_bytes=46 * 1024 * 1024
        ),
        name="relax",
    )(
        rotors,
        slot_turbine.reshape(1, slots),
        moved_rotors.reshape(1, moved_dev),
        new_brick.reshape(1, moved_dev),
        adjoint,
        medium,
    )


def z_weights(depth):
    z = np.arange(depth)[:, None] - np.arange(depth)[None, :]
    height = z + 0.5 - KZ / 2.0
    values = np.exp(-(height**2) / (2.0 * SIGMA_RADIAL**2)) * ((z >= 0) & (z < KZ))
    values = values.astype(np.float32)
    high = values.astype(jnp.bfloat16)
    low = (values - high.astype(np.float32)).astype(jnp.bfloat16)
    return np.block([[high, low], [high, np.zeros_like(low)]])


def weigh_kernel(
    sizes,
    turb_dev,
    corner_hbm,
    profile_hbm,
    table,
    q,
    out_hbm,
    conv,
    coef,
    place,
    corner,
    profile,
    small_sem,
    out_sem,
):
    _, count, width, depth = q.shape
    n, slots = table.shape[0], corner.shape[1]
    groups = -(-slots // LANES)
    me = lax.axis_index("gx") * sizes[1] + lax.axis_index("gy")

    small = [
        pltpu.make_async_copy(profile_hbm, profile, small_sem.at[0]),
        pltpu.make_async_copy(corner_hbm, corner, small_sem.at[1]),
    ]
    write = pltpu.make_async_copy(q, out_hbm, out_sem)
    for copy in small:
        copy.start()
    write.start()

    own = table[me]
    lane = lax.broadcasted_iota(jnp.int32, (1, LANES), 1)
    for group in range(groups):
        turbine = jnp.maximum(own[5 + group : 6 + group], 0.0).astype(jnp.int32)
        owner, local = lax.div(turbine, turb_dev), lax.rem(turbine, turb_dev)
        owner = jnp.broadcast_to(owner, (8, LANES))
        local = jnp.broadcast_to(local, (8, LANES))

        def gather(d, fields):
            found = jnp.take_along_axis(table[d], local, axis=1, mode="promise_in_bounds")
            return jnp.where(owner == d, found, fields)

        fields = lax.fori_loop(0, n, gather, jnp.zeros((8, LANES), jnp.float32), unroll=4)
        sub_x, sub_y, cosine, sine, thrust = [fields[i : i + 1] for i in range(5)]
        cell_y = lax.broadcasted_iota(jnp.int32, (KY, LANES), 0).astype(jnp.float32)
        delta_y = cell_y + (0.5 - KY / 2.0) - sub_y
        for a in range(KX):
            delta_x = (a + 0.5 - KX / 2.0) - sub_x
            along = cosine * delta_x + sine * delta_y
            across = cosine * delta_y - sine * delta_x
            kernel = thrust * jnp.exp(
                -along * along / (2.0 * SIGMA_AXIAL * SIGMA_AXIAL)
                - across * across / (2.0 * SIGMA_RADIAL * SIGMA_RADIAL)
            )
            axial = along * (1.0 / (SIGMA_AXIAL * SIGMA_AXIAL))
            radial = across * (1.0 / (SIGMA_RADIAL * SIGMA_RADIAL))
            coef[0, group, a] = kernel * (axial * cosine - radial * sine)
            coef[1, group, a] = kernel * (axial * sine + radial * cosine)

    for copy in small:
        copy.wait()
    for group in range(groups):
        size = min(LANES, slots - group * LANES)
        part = pl.ds(group * LANES, size)
        first_x = jnp.minimum(corner[0:1, part], count - KX)
        first_y = jnp.minimum(corner[1:2, part], width - KY)
        first_z = jnp.minimum(corner[2:3, part], depth - KZ)
        place[group : group + 1, pl.ds(0, size)] = first_x * width + first_y
        place[groups + group : groups + group + 1, pl.ds(0, size)] = (
            lane[:, :size] - first_z
        ) & (LANES - 1)

    @pl.loop(0, count // BATCH)
    def _(i):
        pieces = []
        for j in range(BATCH):
            plane = q[0, i * BATCH + j]
            high = plane.astype(jnp.bfloat16)
            low = (plane - high.astype(jnp.float32)).astype(jnp.bfloat16)
            pieces.append(jnp.concatenate([high, low], axis=1))
        both = jnp.dot(
            jnp.concatenate(pieces, axis=0), profile[...], preferred_element_type=jnp.float32
        )
        rows = BATCH * width
        conv[pl.ds(pl.multiple_of(i * rows, 8), rows)] = both[:, :depth] + both[:, depth:]

    write.wait()


def weigh(state, table, slot_corner, turb_dev, sizes):
    _, count, width, depth = state.shape
    slots = slot_corner.shape[1]
    groups = -(-slots // LANES)
    vmem, hbm = pl.BlockSpec(memory_space=pltpu.VMEM), pl.BlockSpec(memory_space=pltpu.HBM)
    profile = jnp.asarray(z_weights(depth))
    return pl.pallas_call(
        functools.partial(weigh_kernel, sizes, turb_dev),
        out_shape=(
            jax.ShapeDtypeStruct(state.shape, jnp.float32),
            jax.ShapeDtypeStruct((count * width, depth), jnp.float32),
            jax.ShapeDtypeStruct((2, groups, KX, KY, LANES), jnp.float32),
            jax.ShapeDtypeStruct((2 * groups, LANES), jnp.int32),
        ),
        in_specs=[hbm, hbm, vmem, vmem],
        out_specs=(hbm, vmem, vmem, vmem),
        scratch_shapes=[
            pltpu.VMEM(slot_corner.shape, jnp.int32),
            pltpu.VMEM(profile.shape, jnp.bfloat16),
            pltpu.SemaphoreType.DMA((2,)),
            pltpu.SemaphoreType.DMA,
        ],
        compiler_params=pltpu.CompilerParams(vmem_limit_bytes=8 * 1024 * 1024),
        name="weigh",
    )(slot_corner, profile, table, state)


def plan_rows(sizes, moved_dev, table, plan):
    n = sizes[0] * sizes[1]
    me = lax.axis_index("gx") * sizes[1] + lax.axis_index("gy")
    lines = table[:, 7]
    lane = lax.broadcasted_iota(jnp.int32, lines.shape, 1)
    mine = jnp.where((lines == me.astype(jnp.float32)) & (lane < moved_dev), 1.0, 0.0)

    def earlier(size, row, col):
        less = lax.broadcasted_iota(jnp.int32, (size, size), row) < lax.broadcasted_iota(
            jnp.int32, (size, size), col
        )
        return jnp.where(less, 1.0, 0.0).astype(jnp.bfloat16)

    rank = jnp.sum(
        jnp.dot(
            earlier(n, 1, 0), mine.astype(jnp.bfloat16), preferred_element_type=jnp.float32
        ),
        axis=1,
        keepdims=True,
    ) + jnp.dot(
        mine.astype(jnp.bfloat16), earlier(LANES, 0, 1), preferred_element_type=jnp.float32
    )
    shifted = [jnp.ones_like(lines)]
    shifted += [pltpu.roll(lines, LANES - moved_dev * f, 1) for f in range(1, 7)]
    chosen = [jnp.where(rank == float(slot), mine, 0.0) for slot in range(RECV)]
    for i, values in enumerate(shifted):
        parts = [jnp.sum(pick * values, axis=0, keepdims=True) for pick in chosen]
        total = jnp.sum(jnp.concatenate(parts, axis=0), axis=1, keepdims=True)
        plan[i] = jnp.broadcast_to(total, (RECV, LANES))


def share_kernel(
    sizes,
    slots,
    width,
    moved_dev,
    conv,
    coef,
    place_vmem,
    table,
    out,
    plan,
    mine,
    every,
    place,
    place_sem,
    ssem,
    rsem,
):
    fetch = pltpu.make_async_copy(place_vmem, place, place_sem)
    fetch.start()
    met = greet(sizes)
    fetch.wait()
    groups = -(-slots // LANES)
    lane = lax.broadcasted_iota(jnp.int32, (KY, LANES), 1)
    for group in range(groups):

        def collect(slot, blocks):
            base, shift = place[group, slot], place[groups + group, slot]
            here = lane == slot
            return tuple(
                jnp.where(here, pltpu.roll(conv[pl.ds(base + a * width, KY)], shift, 1), old)
                for a, old in enumerate(blocks)
            )

        size = min(LANES, slots - group * LANES)
        blank = jnp.zeros((KY, LANES), jnp.float32)
        blocks = lax.fori_loop(0, size, collect, (blank,) * KX, unroll=16)
        for i in range(2):
            total = blocks[0] * coef[i, group, 0]
            for a in range(1, KX):
                total = total + blocks[a] * coef[i, group, a]
            row = i * groups + group
            mine[row : row + 1] = jnp.sum(total, axis=0, keepdims=True)

    every[lax.axis_index("gx") * sizes[1] + lax.axis_index("gy")] = mine[...]
    pl.semaphore_wait(pltpu.get_barrier_semaphore(), met)
    along_y = spread_y(sizes, mine, every, ssem, rsem)
    for copy in along_y:
        copy.start()
    plan_rows(sizes, moved_dev, table, plan)
    for copy in along_y:
        copy.wait()
    along_x = spread_x(sizes, every, ssem, rsem)
    for copy in along_x:
        copy.start()
    for copy in along_x:
        copy.wait()
    out[...] = every[...]


def finish_kernel(sizes, groups, step_size, every, table, plan, step_out, incoming):
    n = sizes[0] * sizes[1]
    me = lax.axis_index("gx") * sizes[1] + lax.axis_index("gy")
    turb_dev = step_out.shape[1]
    valid, wanted, sub_x, sub_y, cosine, sine, thrust = [plan[i] for i in range(7)]
    own = (
        me * turb_dev + lax.broadcasted_iota(jnp.int32, (turb_dev, LANES), 0)
    ).astype(jnp.float32)
    targets = jnp.concatenate([own, wanted], axis=0)

    def collect(d, carry):
        sum_x, sum_y = carry
        for group in range(groups):
            hit = targets == table[d, pl.ds(5 + group, 1)]
            sum_x = jnp.where(hit, every[d, pl.ds(group, 1)], sum_x)
            sum_y = jnp.where(hit, every[d, pl.ds(groups + group, 1)], sum_y)
        return sum_x, sum_y

    zero = jnp.zeros((turb_dev + RECV, LANES), jnp.float32)
    sums = lax.fori_loop(0, n, collect, (zero, zero), unroll=2)
    step = step_size[0]
    taken = [
        jnp.clip(-step * jnp.sum(part, axis=1, keepdims=True), -0.5, 0.5) for part in sums
    ]
    flip = lax.broadcasted_iota(jnp.int32, (turb_dev, turb_dev), 0) == lax.broadcasted_iota(
        jnp.int32, (turb_dev, turb_dev), 1
    )
    for i in range(2):
        step_out[i : i + 1] = jnp.sum(
            jnp.where(flip, taken[i][:turb_dev], 0.0), axis=0, keepdims=True
        )
    cells = KX * KY * KZ
    cell = lax.broadcasted_iota(jnp.int32, (RECV, cells), 1)
    ex = (cell // (KY * KZ)).astype(jnp.float32) + 0.5 - KX / 2.0
    ey = lax.rem(cell // KZ, KY).astype(jnp.float32) + 0.5 - KY / 2.0
    ez = lax.rem(cell, KZ).astype(jnp.float32) + 0.5 - KZ / 2.0
    column = slice(0, 1)
    delta_x = ex - (sub_x[:, column] + taken[0][turb_dev:])
    delta_y = ey - (sub_y[:, column] + taken[1][turb_dev:])
    cosine, sine = cosine[:, column], sine[:, column]
    along = cosine * delta_x + sine * delta_y
    across = cosine * delta_y - sine * delta_x
    kernel = thrust[:, column] * jnp.exp(
        -along * along / (2.0 * SIGMA_AXIAL * SIGMA_AXIAL)
        - (across * across + ez * ez) / (2.0 * SIGMA_RADIAL * SIGMA_RADIAL)
    )
    incoming[...] = jnp.where(valid[:, column] > 0, kernel, 0.0).astype(jnp.bfloat16)


def finish(step_size, conv, coef, place, table, slots, width, turb_dev, moved_dev, sizes):
    n = sizes[0] * sizes[1]
    groups = -(-slots // LANES)
    vmem = pl.BlockSpec(memory_space=pltpu.VMEM)

    every, plan = pl.pallas_call(
        functools.partial(share_kernel, sizes, slots, width, moved_dev),
        out_shape=(
            jax.ShapeDtypeStruct((n, 2 * groups, LANES), jnp.float32),
            jax.ShapeDtypeStruct((7, RECV, LANES), jnp.float32),
        ),
        in_specs=[vmem] * 4,
        out_specs=(vmem, vmem),
        scratch_shapes=[
            pltpu.VMEM((2 * groups, LANES), jnp.float32),
            pltpu.VMEM((n, 2 * groups, LANES), jnp.float32),
            pltpu.SMEM(place.shape, jnp.int32),
            pltpu.SemaphoreType.DMA,
            pltpu.SemaphoreType.DMA((sizes[0] + sizes[1],)),
            pltpu.SemaphoreType.DMA((sizes[0] + sizes[1],)),
        ],
        compiler_params=pltpu.CompilerParams(
            collective_id=1, has_side_effects=True, vmem_limit_bytes=8 * 1024 * 1024
        ),
        name="share",
    )(conv, coef, place, table)
    return pl.pallas_call(
        functools.partial(finish_kernel, sizes, groups),
        out_shape=(
            jax.ShapeDtypeStruct((2, turb_dev), jnp.float32),
            jax.ShapeDtypeStruct((RECV, KX * KY * KZ), jnp.bfloat16),
        ),
        in_specs=[pl.BlockSpec(memory_space=pltpu.SMEM), vmem, vmem, vmem],
        out_specs=(vmem, vmem),
        compiler_params=pltpu.CompilerParams(vmem_limit_bytes=8 * 1024 * 1024),
        name="finish",
    )(step_size, every, table, plan)


def body(
    sizes, adjoint, medium, rotors, step_size, slot_turbine, slot_corner, moved_rotors, new_brick
):
    turb_dev, slots = rotors.shape[1], slot_turbine.shape[0]
    state, table = relax(adjoint, medium, rotors, slot_turbine, moved_rotors, new_brick, sizes)
    state, conv, coef, place = weigh(state, table, slot_corner, turb_dev, sizes)
    step_taken, incoming = finish(
        step_size.reshape(1),
        conv,
        coef,
        place,
        table,
        slots,
        adjoint.shape[2],
        turb_dev,
        moved_rotors.shape[0],
        sizes,
    )
    return (state, step_taken, incoming)


def solution(mesh):
    sizes = (mesh.shape["gx"], mesh.shape["gy"])
    return jax.shard_map(
        functools.partial(body, sizes),
        mesh=mesh,
        in_specs=(
            P(None, "gx", "gy", None),
            P(None, "gx", "gy", None),
            P(None, ("gx", "gy")),
            P(),
            P(("gx", "gy")),
            P(None, ("gx", "gy")),
            P(("gx", "gy")),
            P(("gx", "gy"), None),
        ),
        out_specs=(P(None, "gx", "gy", None), P(None, ("gx", "gy")), P(("gx", "gy"), None)),
        check_vma=False,
    )
```

```python
import functools

import jax
import jax.numpy as jnp
import numpy as np
from jax import lax
from jax.experimental import pallas as pl
from jax.experimental.pallas import tpu as pltpu
from jax.sharding import PartitionSpec as P

KX = 8
KY = 16
KZ = 16
SWEEPS = 2
RECV = 8
EDGE = 16
CHUNK = 8
STRIP = 16
LANES = 128
BATCH = 16


TAU = 0.05
SIGMA_AXIAL = 1.5
SIGMA_RADIAL = 4.0
MESH = pl.DeviceIdType.MESH


def strips(rows):
    return [(pl.ds(start, STRIP), pl.ds(8 + start, STRIP)) for start in range(0, rows, STRIP)]


def prepare(med, src, keep, scaled, fb, first, fresh):
    for j in range(CHUNK):
        x = first + j
        for part, mid in strips(src.shape[2]):
            if fresh:
                viscous, velocity, reaction, coupling, source = [
                    TAU * med[i, x, part].astype(jnp.float32) for i in range(5)
                ]
                pull = viscous + velocity
                kept = 1.0 - 5.0 * viscous - (pull + reaction)
                scaled[0, x, part] = viscous
                scaled[1, x, part] = pull
                scaled[2, x, part] = coupling
                scaled[3, x, part] = source
                keep[0, x, part] = kept
                keep[1, x, part] = kept - reaction
            else:
                viscous = scaled[0, x, part]
            for c in range(2):
                fb[c, x + 1, mid] = viscous * src[c, x, part]


def update(src, dst, keep, scaled, fb, first, last):
    rows, depth = src.shape[2:]
    col = lax.broadcasted_iota(jnp.int32, (STRIP, depth), 1)
    bottom, top = col == 0, col == depth - 1
    for start in range(0, rows, STRIP):
        part, mid = pl.ds(start, STRIP), pl.ds(8 + start, STRIP)
        below, above = pl.ds(7 + start, STRIP), pl.ds(9 + start, STRIP)
        values = src[0, first, part], src[1, first, part]
        behind = fb[0, first, mid], fb[1, first, mid]
        for j in range(CHUNK):
            x = first + j
            more = j + 1 < CHUNK or not last
            if more:
                pull = scaled[1, x + 1, part]
                ahead = src[0, x + 1, part], src[1, x + 1, part]
            coupling = scaled[2, x, part]
            here = fb[0, x + 1, mid], fb[1, x + 1, mid]
            for c in range(2):
                near = here[c].astype(jnp.bfloat16)
                zero = jnp.zeros_like(near)
                sides = jnp.where(bottom, zero, pltpu.roll(near, 1, 1))
                sides = sides + jnp.where(top, zero, pltpu.roll(near, depth - 1, 1))
                total = behind[c] + sides.astype(jnp.float32)
                if more:
                    total = total + pull * ahead[c]
                total = total + (fb[c, x + 1, below] + fb[c, x + 1, above])
                total = total - coupling * values[1 - c]
                if c == 0:
                    total = total + scaled[3, x, part]
                dst[c, x, part] = keep[c, x, part] * values[c] + total
            behind = here
            if more:
                values = ahead


def pack_tables(me, rotors, listed, moved, target, step, pack):
    turb_dev, slots, moved_dev = rotors.shape[1], listed.shape[1], moved.shape[1]
    pack[...] = jnp.full(pack.shape, -1.0, jnp.float32)
    own = pl.ds(0, turb_dev)
    pack[0:2, own] = rotors[0:2]
    pack[2:3, own] = jnp.cos(rotors[2:3])
    pack[3:4, own] = jnp.sin(rotors[2:3])
    pack[4:5, own] = rotors[3:4]
    pack[0:1, pl.ds(LANES - 1, 1)] = jnp.full((1, 1), step[...], jnp.float32)
    for group in range(-(-slots // LANES)):
        size = min(LANES, slots - group * LANES)
        pack[5 + group : 6 + group, pl.ds(0, size)] = listed[
            :, pl.ds(group * LANES, size)
        ].astype(jnp.float32)
    full = pack[...]
    lane = lax.broadcasted_iota(jnp.int32, full.shape, 1)
    field = lax.broadcasted_iota(jnp.int32, full.shape, 0) + 2
    line = jnp.full((1, LANES), -1.0, jnp.float32)
    chosen, wanted = moved[...].astype(jnp.float32), target[...].astype(jnp.float32)
    for j in range(moved_dev):
        local = chosen[:, j : j + 1]
        picked = jnp.sum(
            jnp.where(lane.astype(jnp.float32) == local, full, 0.0), axis=1, keepdims=True
        )
        here = (lane == moved_dev * field + j) & (field < 7)
        spread = jnp.sum(jnp.where(here, picked, 0.0), axis=0, keepdims=True)
        place = lane[0:1]
        for f in range(2, 7):
            line = jnp.where(place == moved_dev * f + j, spread, line)
        line = jnp.where(place == j, wanted[:, j : j + 1], line)
        number = (me * turb_dev).astype(jnp.float32) + local
        line = jnp.where(place == moved_dev + j, number, line)
    pack[7:8] = line


def greet(sizes):
    n_gx, n_gy = sizes
    gx, gy = lax.axis_index("gx"), lax.axis_index("gy")
    barrier = pltpu.get_barrier_semaphore()
    for j in range(1, n_gy):
        pl.semaphore_signal(
            barrier, inc=1, device_id=(gx, lax.rem(gy + j, n_gy)), device_id_type=MESH
        )
    for j in range(1, n_gx):
        pl.semaphore_signal(
            barrier, inc=1, device_id=(lax.rem(gx + j, n_gx), gy), device_id_type=MESH
        )
    return n_gx + n_gy - 2


def spread_y(sizes, own, every, ssem, rsem):
    n_gy = sizes[1]
    gx, gy = lax.axis_index("gx"), lax.axis_index("gy")
    return [
        pltpu.make_async_remote_copy(
            src_ref=own,
            dst_ref=every.at[gx * n_gy + gy],
            send_sem=ssem.at[j],
            recv_sem=rsem.at[j],
            device_id=(gx, lax.rem(gy + j, n_gy)),
            device_id_type=MESH,
        )
        for j in range(1, n_gy)
    ]


def spread_x(sizes, every, ssem, rsem):
    n_gx, n_gy = sizes
    gx, gy = lax.axis_index("gx"), lax.axis_index("gy")
    block = every.at[pl.ds(gx * n_gy, n_gy)]
    return [
        pltpu.make_async_remote_copy(
            src_ref=block,
            dst_ref=block,
            send_sem=ssem.at[n_gy + j],
            recv_sem=rsem.at[n_gy + j],
            device_id=(lax.rem(gx + j, n_gx), gy),
            device_id_type=MESH,
        )
        for j in range(1, n_gx)
    ]


def relax_kernel(
    sizes,
    rotors_hbm,
    listed_hbm,
    moved_hbm,
    target_hbm,
    step,
    q_hbm,
    med_hbm,
    q,
    every,
    rotors,
    listed,
    moved,
    target,
    med,
    q1,
    keep,
    scaled,
    fb,
    xs,
    xr,
    ys,
    yr,
    pack,
    table,
    small_sem,
    edge_sem,
    in_sem,
    ssem,
    rsem,
    tsend,
    trecv,
):
    n_gx, n_gy = sizes
    _, count, width, depth = q.shape
    chunks = count // CHUNK
    gx, gy = lax.axis_index("gx"), lax.axis_index("gy")
    x_lo, x_hi = lax.rem(gx + n_gx - 1, n_gx), lax.rem(gx + 1, n_gx)
    y_lo, y_hi = lax.rem(gy + n_gy - 1, n_gy), lax.rem(gy + 1, n_gy)
    peers = ((x_lo, gy), (x_hi, gy), (gx, y_lo), (gx, y_hi))
    q_mid, mid = pl.ds(8, width - 16), pl.ds(EDGE, width - 2 * EDGE)
    q_edges = (pl.ds(0, 8), pl.ds(width - 8, 8))
    edges = (pl.ds(0, EDGE), pl.ds(width - EDGE, EDGE))

    def fetch(which, planes, rows, sem):
        src, dst = (q_hbm.at[:], q.at[:]) if which is None else (med_hbm.at[which], med.at[which])
        return pltpu.make_async_copy(src.at[:, planes, rows], dst.at[:, planes, rows], sem)

    whole, end = pl.ds(0, width), pl.ds(count - 1, 1)
    head, tail = pl.ds(0, CHUNK), pl.ds(CHUNK, count - CHUNK)
    every_field, viscous, others = pl.ds(0, 5), pl.ds(0, 1), pl.ds(1, 4)
    head_in = [
        fetch(None, head, whole, in_sem.at[0, 0]),
        fetch(every_field, head, whole, in_sem.at[0, 1]),
    ]
    edge_in = []
    for i in range(2):
        edge_in.append(fetch(None, tail, q_edges[i], edge_sem.at[i, 0]))
        edge_in.append(fetch(viscous, tail, edges[i], edge_sem.at[i, 1]))
    edge_in += [
        fetch(None, end, q_mid, edge_sem.at[2, 0]),
        fetch(viscous, end, mid, edge_sem.at[2, 1]),
    ]

    def chunk_in(i, size=CHUNK):
        part, all_of_it = pl.ds(i * CHUNK, size), pl.ds(i * CHUNK, CHUNK)
        return (
            fetch(None, part, q_mid, in_sem.at[i, 0]),
            fetch(viscous, part, mid, in_sem.at[i, 1]),
            fetch(others, all_of_it, whole, in_sem.at[i, 2]),
        )

    last_in = chunk_in(chunks - 1, CHUNK - 1)
    small = [
        pltpu.make_async_copy(rotors_hbm, rotors, small_sem.at[0]),
        pltpu.make_async_copy(listed_hbm, listed, small_sem.at[1]),
        pltpu.make_async_copy(moved_hbm, moved, small_sem.at[2]),
        pltpu.make_async_copy(target_hbm, target, small_sem.at[3]),
    ]
    for copy in head_in + edge_in + small:
        copy.start()

    @pl.loop(1, chunks - 1)
    def _(i):
        for copy in chunk_in(i):
            copy.start()

    for copy in last_in:
        copy.start()

    barrier = pltpu.get_barrier_semaphore()
    me = gx * n_gy + gy

    met = greet(sizes)
    blank = jnp.zeros((8, depth), jnp.float32)

    @pl.loop(0, count + 2, unroll=2)
    def _(x):
        for c in range(2):
            fb[c, x, pl.ds(0, 8)] = blank
            fb[c, x, pl.ds(8 + width, 8)] = blank

    for c in range(2):
        fb[c, 0, pl.ds(8, width)] = jnp.zeros((width, depth), jnp.float32)
    for copy in small:
        copy.wait()
    pack_tables(me, rotors, listed, moved, target, step, pack)

    def remote(turn, side, src, dst):
        return pltpu.make_async_remote_copy(
            src_ref=src.at[turn, side % 2],
            dst_ref=dst.at[turn, side % 2],
            send_sem=ssem.at[turn, side],
            recv_sem=rsem.at[turn, side],
            device_id=peers[side],
            device_id_type=MESH,
        )

    def exchange_x(turn, src):
        for c in range(2):
            low, high = med[0, 0].astype(jnp.float32), med[0, count - 1].astype(jnp.float32)
            xs[turn, 0, c] = (low + med[1, 0].astype(jnp.float32)) * src[c, 0]
            xs[turn, 1, c] = high * src[c, count - 1]

        copies = [remote(turn, side, xs, xr) for side in (0, 1)]
        for copy in copies:
            copy.start()
        return copies

    def exchange_y(turn, src):
        @pl.loop(0, count, unroll=8)
        def _(x):
            low = med[0, x, pl.ds(0, EDGE)].astype(jnp.float32)[:8]
            high = med[0, x, pl.ds(width - EDGE, EDGE)].astype(jnp.float32)[8:]
            for c in range(2):
                ys[turn, 0, c, pl.ds(x, 1)] = (low * src[c, x, pl.ds(0, 8)])[:1]
                ys[turn, 1, c, pl.ds(x, 1)] = (high * src[c, x, pl.ds(width - 8, 8)])[7:]

        copies = [remote(turn, side, ys, yr) for side in (2, 3)]
        for copy in copies:
            copy.start()
        return copies

    def patch(turn, dst):
        has_hi_x = jnp.where(gx < n_gx - 1, TAU, 0.0)
        has_lo_x = jnp.where(gx > 0, TAU, 0.0)
        has_hi_y = jnp.where(gy < n_gy - 1, TAU, 0.0)
        has_lo_y = jnp.where(gy > 0, TAU, 0.0)
        for c in range(2):
            dst[c, count - 1] = dst[c, count - 1] + has_hi_x * xr[turn, 0, c]
            dst[c, 0] = dst[c, 0] + has_lo_x * xr[turn, 1, c]

        @pl.loop(0, count, unroll=8)
        def _(x):
            for c in range(2):
                last = pl.ds(width - 1, 1)
                first = pl.ds(0, 1)
                dst[c, x, last] = dst[c, x, last] + has_hi_y * yr[turn, 0, c, pl.ds(x, 1)]
                dst[c, x, first] = dst[c, x, first] + has_lo_y * yr[turn, 1, c, pl.ds(x, 1)]

    for copy in head_in:
        copy.wait()
    prepare(med, q, keep, scaled, fb, 0, True)
    for copy in edge_in:
        copy.wait()
    pl.semaphore_wait(barrier, met)
    copies = exchange_y(0, q) + exchange_x(0, q)

    table[me] = pack[...]
    along_y = spread_y(sizes, pack, table, tsend, trecv)
    for copy in along_y:
        copy.start()

    @pl.loop(0, chunks - 1)
    def _(i):
        @pl.when(i + 1 < chunks - 1)
        def _():
            for copy in chunk_in(i + 1):
                copy.wait()

        @pl.when(i + 1 == chunks - 1)
        def _():
            for copy in last_in:
                copy.wait()

        prepare(med, q, keep, scaled, fb, (i + 1) * CHUNK, True)
        update(q, q1, keep, scaled, fb, i * CHUNK, False)

    update(q, q1, keep, scaled, fb, count - CHUNK, True)

    for copy in copies:
        copy.wait()
    patch(0, q1)

    copies = exchange_x(1, q1) + exchange_y(1, q1)
    for copy in along_y:
        copy.wait()
    along_x = spread_x(sizes, table, tsend, trecv)
    for copy in along_x:
        copy.start()

    prepare(med, q1, keep, scaled, fb, 0, False)

    @pl.loop(0, chunks - 1)
    def _(i):
        prepare(med, q1, keep, scaled, fb, (i + 1) * CHUNK, False)
        update(q1, q, keep, scaled, fb, i * CHUNK, False)

    update(q1, q, keep, scaled, fb, count - CHUNK, True)

    for copy in along_x:
        copy.wait()
    every[...] = table[...]
    for copy in copies:
        copy.wait()
    patch(1, q)


def in_hbm(array):
    return pltpu.with_memory_space_constraint(array, pltpu.HBM)


def relax(adjoint, medium, rotors, step_size, slot_turbine, moved_rotors, new_brick, sizes):
    n = sizes[0] * sizes[1]
    vmem, hbm = pl.BlockSpec(memory_space=pltpu.VMEM), pl.BlockSpec(memory_space=pltpu.HBM)
    channels, count, width, depth = adjoint.shape
    slots, moved_dev = slot_turbine.shape[0], moved_rotors.shape[0]
    return pl.pallas_call(
        functools.partial(relax_kernel, sizes),
        out_shape=(
            jax.ShapeDtypeStruct(adjoint.shape, jnp.float32),
            jax.ShapeDtypeStruct((n, 8, LANES), jnp.float32),
        ),
        in_specs=[hbm] * 4 + [pl.BlockSpec(memory_space=pltpu.SMEM)] + [hbm] * 2,
        out_specs=(vmem, vmem),
        scratch_shapes=[
            pltpu.VMEM(rotors.shape, jnp.float32),
            pltpu.VMEM((1, slots), jnp.int32),
            pltpu.VMEM((1, moved_dev), jnp.int32),
            pltpu.VMEM((1, moved_dev), jnp.int32),
            pltpu.VMEM(medium.shape, jnp.bfloat16),
            pltpu.VMEM(adjoint.shape, jnp.float32),
            pltpu.VMEM(adjoint.shape, jnp.float32),
            pltpu.VMEM((4,) + adjoint.shape[1:], jnp.float32),
            pltpu.VMEM((channels, count + 2, width + 16, depth), jnp.float32),
            pltpu.VMEM((2, 2, channels, width, depth), jnp.float32),
            pltpu.VMEM((2, 2, channels, width, depth), jnp.float32),
            pltpu.VMEM((2, 2, channels, count, depth), jnp.float32),
            pltpu.VMEM((2, 2, channels, count, depth), jnp.float32),
            pltpu.VMEM((8, LANES), jnp.float32),
            pltpu.VMEM((n, 8, LANES), jnp.float32),
            pltpu.SemaphoreType.DMA((4,)),
            pltpu.SemaphoreType.DMA((3, 2)),
            pltpu.SemaphoreType.DMA((count // CHUNK, 3)),
            pltpu.SemaphoreType.DMA((2, 4)),
            pltpu.SemaphoreType.DMA((2, 4)),
            pltpu.SemaphoreType.DMA((sizes[0] + sizes[1],)),
            pltpu.SemaphoreType.DMA((sizes[0] + sizes[1],)),
        ],
        compiler_params=pltpu.CompilerParams(
            collective_id=0, has_side_effects=True, vmem_limit_bytes=46 * 1024 * 1024
        ),
        name="relax",
    )(
        in_hbm(rotors),
        in_hbm(slot_turbine.reshape(1, slots)),
        in_hbm(moved_rotors.reshape(1, moved_dev)),
        in_hbm(new_brick.reshape(1, moved_dev)),
        step_size,
        adjoint,
        medium,
    )


def z_weights(depth):
    z = np.arange(depth)[:, None] - np.arange(depth)[None, :]
    height = z + 0.5 - KZ / 2.0
    values = np.exp(-(height**2) / (2.0 * SIGMA_RADIAL**2)) * ((z >= 0) & (z < KZ))
    values = values.astype(np.float32)
    high = values.astype(jnp.bfloat16)
    low = (values - high.astype(np.float32)).astype(jnp.bfloat16)
    return np.block([[high, low], [high, np.zeros_like(low)]])


def weigh_kernel(
    sizes,
    turb_dev,
    corner_hbm,
    profile_hbm,
    table,
    q,
    out_hbm,
    conv,
    rotor,
    place,
    corner,
    profile,
    small_sem,
    out_sem,
):
    _, count, width, depth = q.shape
    n, slots = table.shape[0], corner.shape[1]
    groups = -(-slots // LANES)
    me = lax.axis_index("gx") * sizes[1] + lax.axis_index("gy")

    small = [
        pltpu.make_async_copy(profile_hbm, profile, small_sem.at[0]),
        pltpu.make_async_copy(corner_hbm, corner, small_sem.at[1]),
    ]
    write = pltpu.make_async_copy(q, out_hbm, out_sem)
    for copy in small:
        copy.start()
    write.start()

    own = table[me]
    lane = lax.broadcasted_iota(jnp.int32, (1, LANES), 1)
    for group in range(groups):
        turbine = jnp.maximum(own[5 + group : 6 + group], 0.0).astype(jnp.int32)
        owner, local = lax.div(turbine, turb_dev), lax.rem(turbine, turb_dev)
        owner = jnp.broadcast_to(owner, (8, LANES))
        local = jnp.broadcast_to(local, (8, LANES))

        def gather(d, fields):
            found = jnp.take_along_axis(table[d], local, axis=1, mode="promise_in_bounds")
            return jnp.where(owner == d, found, fields)

        fields = lax.fori_loop(0, n, gather, jnp.zeros((8, LANES), jnp.float32), unroll=4)
        rotor[group] = fields

    for copy in small:
        copy.wait()
    for group in range(groups):
        size = min(LANES, slots - group * LANES)
        part = pl.ds(group * LANES, size)
        first_x = jnp.minimum(corner[0:1, part], count - KX)
        first_y = jnp.minimum(corner[1:2, part], width - KY)
        first_z = jnp.minimum(corner[2:3, part], depth - KZ)
        place[group : group + 1, pl.ds(0, size)] = first_x * width + first_y
        place[groups + group : groups + group + 1, pl.ds(0, size)] = (
            lane[:, :size] - first_z
        ) & (LANES - 1)

    @pl.loop(0, count // BATCH)
    def _(i):
        pieces = []
        for j in range(BATCH):
            plane = q[0, i * BATCH + j]
            high = plane.astype(jnp.bfloat16)
            low = (plane - high.astype(jnp.float32)).astype(jnp.bfloat16)
            pieces.append(jnp.concatenate([high, low], axis=1))
        both = jnp.dot(
            jnp.concatenate(pieces, axis=0), profile[...], preferred_element_type=jnp.float32
        )
        rows = BATCH * width
        conv[pl.ds(pl.multiple_of(i * rows, 8), rows)] = both[:, :depth] + both[:, depth:]

    write.wait()


def weigh(state, table, slot_corner, turb_dev, sizes):
    _, count, width, depth = state.shape
    slots = slot_corner.shape[1]
    groups = -(-slots // LANES)
    vmem, hbm = pl.BlockSpec(memory_space=pltpu.VMEM), pl.BlockSpec(memory_space=pltpu.HBM)
    profile = jnp.asarray(z_weights(depth))
    return pl.pallas_call(
        functools.partial(weigh_kernel, sizes, turb_dev),
        out_shape=(
            jax.ShapeDtypeStruct(state.shape, jnp.float32),
            jax.ShapeDtypeStruct((count * width, depth), jnp.float32),
            jax.ShapeDtypeStruct((groups, 8, LANES), jnp.float32),
            jax.ShapeDtypeStruct((2 * groups, LANES), jnp.int32),
        ),
        in_specs=[hbm, hbm, vmem, vmem],
        out_specs=(hbm, vmem, vmem, vmem),
        scratch_shapes=[
            pltpu.VMEM(slot_corner.shape, jnp.int32),
            pltpu.VMEM(profile.shape, jnp.bfloat16),
            pltpu.SemaphoreType.DMA((2,)),
            pltpu.SemaphoreType.DMA,
        ],
        compiler_params=pltpu.CompilerParams(vmem_limit_bytes=8 * 1024 * 1024),
        name="weigh",
    )(slot_corner, profile, table, state)


def plan_rows(sizes, moved_dev, table, plan):
    n = sizes[0] * sizes[1]
    me = lax.axis_index("gx") * sizes[1] + lax.axis_index("gy")
    lines = table[:, 7]
    lane = lax.broadcasted_iota(jnp.int32, lines.shape, 1)
    mine = jnp.where((lines == me.astype(jnp.float32)) & (lane < moved_dev), 1.0, 0.0)

    def earlier(size, row, col):
        less = lax.broadcasted_iota(jnp.int32, (size, size), row) < lax.broadcasted_iota(
            jnp.int32, (size, size), col
        )
        return jnp.where(less, 1.0, 0.0).astype(jnp.bfloat16)

    rank = jnp.sum(
        jnp.dot(
            earlier(n, 1, 0), mine.astype(jnp.bfloat16), preferred_element_type=jnp.float32
        ),
        axis=1,
        keepdims=True,
    ) + jnp.dot(
        mine.astype(jnp.bfloat16), earlier(LANES, 0, 1), preferred_element_type=jnp.float32
    )
    shifted = [jnp.ones_like(lines)]
    shifted += [pltpu.roll(lines, LANES - moved_dev * f, 1) for f in range(1, 7)]
    chosen = [jnp.where(rank == float(slot), mine, 0.0) for slot in range(RECV)]
    for i, values in enumerate(shifted):
        parts = [jnp.sum(pick * values, axis=0, keepdims=True) for pick in chosen]
        total = jnp.sum(jnp.concatenate(parts, axis=0), axis=1, keepdims=True)
        plan[i] = jnp.broadcast_to(total, (RECV, LANES))


def share_kernel(
    sizes,
    slots,
    width,
    moved_dev,
    conv,
    rotor,
    place_vmem,
    table,
    out,
    plan,
    mine,
    every,
    place,
    place_sem,
    ssem,
    rsem,
):
    n, n_gy = sizes[0] * sizes[1], sizes[1]
    me = lax.axis_index("gx") * n_gy + lax.axis_index("gy")
    barrier = pltpu.get_barrier_semaphore()
    fetch = pltpu.make_async_copy(place_vmem, place, place_sem)
    fetch.start()

    def other(d):
        number = lax.rem(me + d, n)
        return lax.div(number, n_gy), lax.rem(number, n_gy)

    @pl.loop(1, n)
    def _(d):
        pl.semaphore_signal(barrier, inc=1, device_id=other(d), device_id_type=MESH)

    fetch.wait()
    groups = -(-slots // LANES)
    lane = lax.broadcasted_iota(jnp.int32, (KY, LANES), 1)
    for group in range(groups):

        def collect(slot, blocks):
            base, shift = place[group, slot], place[groups + group, slot]
            here = lane == slot
            return tuple(
                jnp.where(here, pltpu.roll(conv[pl.ds(base + a * width, KY)], shift, 1), old)
                for a, old in enumerate(blocks)
            )

        size = min(LANES, slots - group * LANES)
        blank = jnp.zeros((KY, LANES), jnp.float32)
        blocks = lax.fori_loop(0, size, collect, (blank,) * KX, unroll=16)
        fields = rotor[group]
        sub_x, sub_y, cosine, sine, thrust = [fields[i : i + 1] for i in range(5)]
        cell_y = lax.broadcasted_iota(jnp.int32, (KY, LANES), 0).astype(jnp.float32)
        delta_y = cell_y + (0.5 - KY / 2.0) - sub_y
        totals = [jnp.zeros((KY, LANES), jnp.float32)] * 2
        for a in range(KX):
            delta_x = (a + 0.5 - KX / 2.0) - sub_x
            along = cosine * delta_x + sine * delta_y
            across = cosine * delta_y - sine * delta_x
            kernel = thrust * jnp.exp(
                -along * along / (2.0 * SIGMA_AXIAL * SIGMA_AXIAL)
                - across * across / (2.0 * SIGMA_RADIAL * SIGMA_RADIAL)
            )
            weighted = kernel * blocks[a]
            axial = along * (1.0 / (SIGMA_AXIAL * SIGMA_AXIAL))
            radial = across * (1.0 / (SIGMA_RADIAL * SIGMA_RADIAL))
            totals[0] = totals[0] + weighted * (axial * cosine - radial * sine)
            totals[1] = totals[1] + weighted * (axial * sine + radial * cosine)
        for i in range(2):
            row = i * groups + group
            mine[row : row + 1] = jnp.sum(totals[i], axis=0, keepdims=True)

    every[me] = mine[...]
    pl.semaphore_wait(barrier, n - 1)

    @pl.loop(1, n)
    def _(d):
        pltpu.make_async_remote_copy(
            src_ref=mine,
            dst_ref=every.at[me],
            send_sem=ssem,
            recv_sem=rsem,
            device_id=other(d),
            device_id_type=MESH,
        ).start()

    plan_rows(sizes, moved_dev, table, plan)
    rest = every.at[pl.ds(0, n - 1)]
    total = pltpu.make_async_remote_copy(
        src_ref=rest,
        dst_ref=rest,
        send_sem=ssem,
        recv_sem=rsem,
        device_id=other(1),
        device_id_type=MESH,
    )
    total.wait()
    out[...] = every[...]


def finish_kernel(sizes, groups, every, table, plan, step_out, incoming):
    n = sizes[0] * sizes[1]
    me = lax.axis_index("gx") * sizes[1] + lax.axis_index("gy")
    turb_dev = step_out.shape[1]
    valid, wanted, sub_x, sub_y, cosine, sine, thrust = [plan[i] for i in range(7)]
    own = (
        me * turb_dev + lax.broadcasted_iota(jnp.int32, (turb_dev, LANES), 0)
    ).astype(jnp.float32)
    targets = jnp.concatenate([own, wanted], axis=0)

    def collect(d, carry):
        sum_x, sum_y = carry
        for group in range(groups):
            hit = targets == table[d, pl.ds(5 + group, 1)]
            sum_x = jnp.where(hit, every[d, pl.ds(group, 1)], sum_x)
            sum_y = jnp.where(hit, every[d, pl.ds(groups + group, 1)], sum_y)
        return sum_x, sum_y

    zero = jnp.zeros((turb_dev + RECV, LANES), jnp.float32)
    sums = lax.fori_loop(0, n, collect, (zero, zero), unroll=2)
    step = table[0, 0:1, LANES - 1 : LANES]
    taken = [
        jnp.clip(-step * jnp.sum(part, axis=1, keepdims=True), -0.5, 0.5) for part in sums
    ]
    flip = lax.broadcasted_iota(jnp.int32, (turb_dev, turb_dev), 0) == lax.broadcasted_iota(
        jnp.int32, (turb_dev, turb_dev), 1
    )
    for i in range(2):
        step_out[i : i + 1] = jnp.sum(
            jnp.where(flip, taken[i][:turb_dev], 0.0), axis=0, keepdims=True
        )
    cells = KX * KY * KZ
    cell = lax.broadcasted_iota(jnp.int32, (RECV, cells), 1)
    ex = (cell // (KY * KZ)).astype(jnp.float32) + 0.5 - KX / 2.0
    ey = lax.rem(cell // KZ, KY).astype(jnp.float32) + 0.5 - KY / 2.0
    ez = lax.rem(cell, KZ).astype(jnp.float32) + 0.5 - KZ / 2.0
    column = slice(0, 1)
    delta_x = ex - (sub_x[:, column] + taken[0][turb_dev:])
    delta_y = ey - (sub_y[:, column] + taken[1][turb_dev:])
    cosine, sine = cosine[:, column], sine[:, column]
    along = cosine * delta_x + sine * delta_y
    across = cosine * delta_y - sine * delta_x
    kernel = thrust[:, column] * jnp.exp(
        -along * along / (2.0 * SIGMA_AXIAL * SIGMA_AXIAL)
        - (across * across + ez * ez) / (2.0 * SIGMA_RADIAL * SIGMA_RADIAL)
    )
    incoming[...] = jnp.where(valid[:, column] > 0, kernel, 0.0).astype(jnp.bfloat16)


def finish(conv, rotor, place, table, slots, width, turb_dev, moved_dev, sizes):
    n = sizes[0] * sizes[1]
    groups = -(-slots // LANES)
    vmem = pl.BlockSpec(memory_space=pltpu.VMEM)

    every, plan = pl.pallas_call(
        functools.partial(share_kernel, sizes, slots, width, moved_dev),
        out_shape=(
            jax.ShapeDtypeStruct((n, 2 * groups, LANES), jnp.float32),
            jax.ShapeDtypeStruct((7, RECV, LANES), jnp.float32),
        ),
        in_specs=[vmem] * 4,
        out_specs=(vmem, vmem),
        scratch_shapes=[
            pltpu.VMEM((2 * groups, LANES), jnp.float32),
            pltpu.VMEM((n, 2 * groups, LANES), jnp.float32),
            pltpu.SMEM(place.shape, jnp.int32),
            pltpu.SemaphoreType.DMA,
            pltpu.SemaphoreType.DMA,
            pltpu.SemaphoreType.DMA,
        ],
        compiler_params=pltpu.CompilerParams(
            collective_id=1, has_side_effects=True, vmem_limit_bytes=8 * 1024 * 1024
        ),
        name="share",
    )(conv, rotor, place, table)
    return pl.pallas_call(
        functools.partial(finish_kernel, sizes, groups),
        out_shape=(
            jax.ShapeDtypeStruct((2, turb_dev), jnp.float32),
            jax.ShapeDtypeStruct((RECV, KX * KY * KZ), jnp.bfloat16),
        ),
        in_specs=[vmem, vmem, vmem],
        out_specs=(vmem, vmem),
        compiler_params=pltpu.CompilerParams(vmem_limit_bytes=8 * 1024 * 1024),
        name="finish",
    )(every, table, plan)


def body(
    sizes, adjoint, medium, rotors, step_size, slot_turbine, slot_corner, moved_rotors, new_brick
):
    turb_dev, slots = rotors.shape[1], slot_turbine.shape[0]
    state, table = relax(
        adjoint, medium, rotors, step_size, slot_turbine, moved_rotors, new_brick, sizes
    )
    state, conv, rotor, place = weigh(state, table, slot_corner, turb_dev, sizes)
    step_taken, incoming = finish(
        conv,
        rotor,
        place,
        table,
        slots,
        adjoint.shape[2],
        turb_dev,
        moved_rotors.shape[0],
        sizes,
    )
    return (state, step_taken, incoming)


def solution(mesh):
    sizes = (mesh.shape["gx"], mesh.shape["gy"])
    return jax.shard_map(
        functools.partial(body, sizes),
        mesh=mesh,
        in_specs=(
            P(None, "gx", "gy", None),
            P(None, "gx", "gy", None),
            P(None, ("gx", "gy")),
            P(),
            P(("gx", "gy")),
            P(None, ("gx", "gy")),
            P(("gx", "gy")),
            P(("gx", "gy"), None),
        ),
        out_specs=(P(None, "gx", "gy", None), P(None, ("gx", "gy")), P(("gx", "gy"), None)),
        check_vma=False,
    )
```

```python
import functools

import jax
import jax.numpy as jnp
import numpy as np
from jax import lax
from jax.experimental import pallas as pl
from jax.experimental.pallas import tpu as pltpu
from jax.sharding import PartitionSpec as P

KX = 8
KY = 16
KZ = 16
SWEEPS = 2
RECV = 8
EDGE = 16
CHUNK = 8
LONG = 16
STRIP = 16
LANES = 128
BATCH = 16


TAU = 0.05
SIGMA_AXIAL = 1.5
SIGMA_RADIAL = 4.0
MESH = pl.DeviceIdType.MESH


def strips(rows):
    return [(pl.ds(start, STRIP), pl.ds(8 + start, STRIP)) for start in range(0, rows, STRIP)]


def prepare(med, src, keep, scaled, fb, first, fresh, planes=CHUNK):
    for j in range(planes):
        x = first + j
        for part, mid in strips(src.shape[2]):
            if fresh:
                viscous, velocity, reaction, coupling, source = [
                    TAU * med[i, x, part].astype(jnp.float32) for i in range(5)
                ]
                pull = viscous + velocity
                kept = 1.0 - 5.0 * viscous - (pull + reaction)
                scaled[0, x, part] = viscous
                scaled[1, x, part] = pull
                scaled[2, x, part] = coupling
                scaled[3, x, part] = source
                keep[0, x, part] = kept
                keep[1, x, part] = kept - reaction
            else:
                viscous = scaled[0, x, part]
            for c in range(2):
                fb[c, x + 1, mid] = viscous * src[c, x, part]


def update(src, dst, keep, scaled, fb, first, last, planes=CHUNK):
    rows, depth = src.shape[2:]
    col = lax.broadcasted_iota(jnp.int32, (STRIP, depth), 1)
    bottom, top = col == 0, col == depth - 1
    for start in range(0, rows, STRIP):
        part, mid = pl.ds(start, STRIP), pl.ds(8 + start, STRIP)
        below, above = pl.ds(7 + start, STRIP), pl.ds(9 + start, STRIP)
        values = src[0, first, part], src[1, first, part]
        behind = fb[0, first, mid], fb[1, first, mid]
        for j in range(planes):
            x = first + j
            more = j + 1 < planes or not last
            if more:
                pull = scaled[1, x + 1, part]
                ahead = src[0, x + 1, part], src[1, x + 1, part]
            coupling = scaled[2, x, part]
            here = fb[0, x + 1, mid], fb[1, x + 1, mid]
            for c in range(2):
                near = here[c].astype(jnp.bfloat16)
                zero = jnp.zeros_like(near)
                sides = jnp.where(bottom, zero, pltpu.roll(near, 1, 1))
                sides = sides + jnp.where(top, zero, pltpu.roll(near, depth - 1, 1))
                total = behind[c] + sides.astype(jnp.float32)
                if more:
                    total = total + pull * ahead[c]
                total = total + (fb[c, x + 1, below] + fb[c, x + 1, above])
                total = total - coupling * values[1 - c]
                if c == 0:
                    total = total + scaled[3, x, part]
                dst[c, x, part] = keep[c, x, part] * values[c] + total
            behind = here
            if more:
                values = ahead


def pack_tables(me, rotors, listed, moved, target, step, pack):
    turb_dev, slots, moved_dev = rotors.shape[1], listed.shape[1], moved.shape[1]
    pack[...] = jnp.full(pack.shape, -1.0, jnp.float32)
    own = pl.ds(0, turb_dev)
    pack[0:2, own] = rotors[0:2]
    pack[2:3, own] = jnp.cos(rotors[2:3])
    pack[3:4, own] = jnp.sin(rotors[2:3])
    pack[4:5, own] = rotors[3:4]
    pack[0:1, pl.ds(LANES - 1, 1)] = jnp.full((1, 1), step[...], jnp.float32)
    for group in range(-(-slots // LANES)):
        size = min(LANES, slots - group * LANES)
        pack[5 + group : 6 + group, pl.ds(0, size)] = listed[
            :, pl.ds(group * LANES, size)
        ].astype(jnp.float32)
    full = pack[...]
    lane = lax.broadcasted_iota(jnp.int32, full.shape, 1)
    field = lax.broadcasted_iota(jnp.int32, full.shape, 0) + 2
    line = jnp.full((1, LANES), -1.0, jnp.float32)
    chosen, wanted = moved[...].astype(jnp.float32), target[...].astype(jnp.float32)
    for j in range(moved_dev):
        local = chosen[:, j : j + 1]
        picked = jnp.sum(
            jnp.where(lane.astype(jnp.float32) == local, full, 0.0), axis=1, keepdims=True
        )
        here = (lane == moved_dev * field + j) & (field < 7)
        spread = jnp.sum(jnp.where(here, picked, 0.0), axis=0, keepdims=True)
        place = lane[0:1]
        for f in range(2, 7):
            line = jnp.where(place == moved_dev * f + j, spread, line)
        line = jnp.where(place == j, wanted[:, j : j + 1], line)
        number = (me * turb_dev).astype(jnp.float32) + local
        line = jnp.where(place == moved_dev + j, number, line)
    pack[7:8] = line


def greet(sizes):
    n_gx, n_gy = sizes
    gx, gy = lax.axis_index("gx"), lax.axis_index("gy")
    barrier = pltpu.get_barrier_semaphore()
    for j in range(1, n_gy):
        pl.semaphore_signal(
            barrier, inc=1, device_id=(gx, lax.rem(gy + j, n_gy)), device_id_type=MESH
        )
    for j in range(1, n_gx):
        pl.semaphore_signal(
            barrier, inc=1, device_id=(lax.rem(gx + j, n_gx), gy), device_id_type=MESH
        )
    return n_gx + n_gy - 2


def spread_y(sizes, own, every, ssem, rsem):
    n_gy = sizes[1]
    gx, gy = lax.axis_index("gx"), lax.axis_index("gy")
    return [
        pltpu.make_async_remote_copy(
            src_ref=own,
            dst_ref=every.at[gx * n_gy + gy],
            send_sem=ssem.at[j],
            recv_sem=rsem.at[j],
            device_id=(gx, lax.rem(gy + j, n_gy)),
            device_id_type=MESH,
        )
        for j in range(1, n_gy)
    ]


def spread_x(sizes, every, ssem, rsem):
    n_gx, n_gy = sizes
    gx, gy = lax.axis_index("gx"), lax.axis_index("gy")
    block = every.at[pl.ds(gx * n_gy, n_gy)]
    return [
        pltpu.make_async_remote_copy(
            src_ref=block,
            dst_ref=block,
            send_sem=ssem.at[n_gy + j],
            recv_sem=rsem.at[n_gy + j],
            device_id=(lax.rem(gx + j, n_gx), gy),
            device_id_type=MESH,
        )
        for j in range(1, n_gx)
    ]


def relax_kernel(
    sizes,
    rotors_hbm,
    listed_hbm,
    moved_hbm,
    target_hbm,
    step,
    q_hbm,
    med_hbm,
    q,
    every,
    rotors,
    listed,
    moved,
    target,
    med,
    q1,
    keep,
    scaled,
    fb,
    xs,
    xr,
    ys,
    yb,
    yr,
    pack,
    table,
    small_sem,
    edge_sem,
    in_sem,
    ssem,
    rsem,
    tsend,
    trecv,
):
    n_gx, n_gy = sizes
    _, count, width, depth = q.shape
    chunks = count // CHUNK
    gx, gy = lax.axis_index("gx"), lax.axis_index("gy")
    x_lo, x_hi = lax.rem(gx + n_gx - 1, n_gx), lax.rem(gx + 1, n_gx)
    y_lo, y_hi = lax.rem(gy + n_gy - 1, n_gy), lax.rem(gy + 1, n_gy)
    peers = ((x_lo, gy), (x_hi, gy), (gx, y_lo), (gx, y_hi))
    q_mid, mid = pl.ds(8, width - 16), pl.ds(EDGE, width - 2 * EDGE)
    q_edges = (pl.ds(0, 8), pl.ds(width - 8, 8))
    edges = (pl.ds(0, EDGE), pl.ds(width - EDGE, EDGE))

    def fetch(which, planes, rows, sem):
        src, dst = (q_hbm.at[:], q.at[:]) if which is None else (med_hbm.at[which], med.at[which])
        return pltpu.make_async_copy(src.at[:, planes, rows], dst.at[:, planes, rows], sem)

    whole, end = pl.ds(0, width), pl.ds(count - 1, 1)
    head, tail = pl.ds(0, CHUNK), pl.ds(CHUNK, count - CHUNK)
    every_field, viscous, others = pl.ds(0, 5), pl.ds(0, 1), pl.ds(1, 4)
    head_in = [
        fetch(None, head, whole, in_sem.at[0, 0]),
        fetch(every_field, head, whole, in_sem.at[0, 1]),
    ]
    edge_in = []
    for i in range(2):
        edge_in.append(fetch(None, tail, q_edges[i], edge_sem.at[i, 0]))
        edge_in.append(fetch(viscous, tail, edges[i], edge_sem.at[i, 1]))
    edge_in += [
        fetch(None, end, q_mid, edge_sem.at[2, 0]),
        fetch(viscous, end, mid, edge_sem.at[2, 1]),
    ]

    def chunk_in(i, size=CHUNK):
        part, all_of_it = pl.ds(i * CHUNK, size), pl.ds(i * CHUNK, CHUNK)
        return (
            fetch(None, part, q_mid, in_sem.at[i, 0]),
            fetch(viscous, part, mid, in_sem.at[i, 1]),
            fetch(others, all_of_it, whole, in_sem.at[i, 2]),
        )

    last_in = chunk_in(chunks - 1, CHUNK - 1)
    small = [
        pltpu.make_async_copy(rotors_hbm, rotors, small_sem.at[0]),
        pltpu.make_async_copy(listed_hbm, listed, small_sem.at[1]),
        pltpu.make_async_copy(moved_hbm, moved, small_sem.at[2]),
        pltpu.make_async_copy(target_hbm, target, small_sem.at[3]),
    ]
    for copy in head_in + edge_in + small:
        copy.start()

    @pl.loop(1, chunks - 1)
    def _(i):
        for copy in chunk_in(i):
            copy.start()

    for copy in last_in:
        copy.start()

    barrier = pltpu.get_barrier_semaphore()
    me = gx * n_gy + gy

    met = greet(sizes)
    blank = jnp.zeros((8, depth), jnp.float32)

    @pl.loop(0, count + 2, unroll=2)
    def _(x):
        for c in range(2):
            fb[c, x, pl.ds(0, 8)] = blank
            fb[c, x, pl.ds(8 + width, 8)] = blank

    for c in range(2):
        fb[c, 0, pl.ds(8, width)] = jnp.zeros((width, depth), jnp.float32)
    for copy in small:
        copy.wait()
    pack_tables(me, rotors, listed, moved, target, step, pack)

    has_lo_x, has_hi_x, has_lo_y, has_hi_y = gx > 0, gx < n_gx - 1, gy > 0, gy < n_gy - 1
    sends = (has_lo_x, has_hi_x, has_lo_y, has_hi_y)
    receives = (has_hi_x, has_lo_x, has_hi_y, has_lo_y)

    def face(turn, side):
        src, dst = (xs, xr) if side < 2 else (yb, yr)
        return pltpu.make_async_remote_copy(
            src_ref=src.at[turn, side % 2],
            dst_ref=dst.at[turn, side % 2],
            send_sem=ssem.at[turn, side],
            recv_sem=rsem.at[turn, side],
            device_id=peers[side],
            device_id_type=MESH,
        )

    def send(turn, side):
        @pl.when(sends[side])
        def _():
            face(turn, side).start()

    def exchange(turn, src):
        for c in range(2):
            low, high = med[0, 0].astype(jnp.float32), med[0, count - 1].astype(jnp.float32)
            low = (low + med[1, 0].astype(jnp.float32)) * src[c, 0]
            xs[turn, 0, c] = low.astype(jnp.bfloat16)
            xs[turn, 1, c] = (high * src[c, count - 1]).astype(jnp.bfloat16)

        for side in (0, 1):
            send(turn, side)

        @pl.loop(0, count, unroll=8)
        def _(x):
            low = med[0, x, pl.ds(0, EDGE)].astype(jnp.float32)[:8]
            high = med[0, x, pl.ds(width - EDGE, EDGE)].astype(jnp.float32)[8:]
            for c in range(2):
                ys[0, c, pl.ds(x, 1)] = (low * src[c, x, pl.ds(0, 8)])[:1]
                ys[1, c, pl.ds(x, 1)] = (high * src[c, x, pl.ds(width - 8, 8)])[7:]

        for side in (2, 3):
            yb[turn, side - 2] = ys[side - 2].astype(jnp.bfloat16)
            send(turn, side)

    def patch(turn, dst):
        for side in range(4):

            @pl.when(sends[side])
            def _():
                face(turn, side).wait_send()

            @pl.when(receives[side])
            def _():
                face(turn, side).wait_recv()
                if side < 2:
                    x = 0 if side else count - 1
                    for c in range(2):
                        dst[c, x] = dst[c, x] + TAU * xr[turn, side, c].astype(jnp.float32)
                else:
                    ys[side - 2] = TAU * yr[turn, side - 2].astype(jnp.float32)
                    line = pl.ds(0 if side == 3 else width - 1, 1)

                    @pl.loop(0, count, unroll=16)
                    def _(x):
                        for c in range(2):
                            dst[c, x, line] = dst[c, x, line] + ys[side - 2, c, pl.ds(x, 1)]

    for copy in head_in:
        copy.wait()
    prepare(med, q, keep, scaled, fb, 0, True)
    for copy in edge_in:
        copy.wait()
    pl.semaphore_wait(barrier, met)
    exchange(0, q)

    table[me] = pack[...]
    along_y = spread_y(sizes, pack, table, tsend, trecv)
    for copy in along_y:
        copy.start()

    @pl.loop(0, chunks - 1)
    def _(i):
        @pl.when(i + 1 < chunks - 1)
        def _():
            for copy in chunk_in(i + 1):
                copy.wait()

        @pl.when(i + 1 == chunks - 1)
        def _():
            for copy in last_in:
                copy.wait()

        prepare(med, q, keep, scaled, fb, (i + 1) * CHUNK, True)
        update(q, q1, keep, scaled, fb, i * CHUNK, False)

    update(q, q1, keep, scaled, fb, count - CHUNK, True)

    patch(0, q1)
    exchange(1, q1)
    for copy in along_y:
        copy.wait()
    along_x = spread_x(sizes, table, tsend, trecv)
    for copy in along_x:
        copy.start()

    prepare(med, q1, keep, scaled, fb, 0, False, LONG)

    @pl.loop(0, count // LONG - 1)
    def _(i):
        prepare(med, q1, keep, scaled, fb, (i + 1) * LONG, False, LONG)
        update(q1, q, keep, scaled, fb, i * LONG, False, LONG)

    update(q1, q, keep, scaled, fb, count - LONG, True, LONG)

    for copy in along_x:
        copy.wait()
    every[...] = table[...]
    patch(1, q)


def in_hbm(array):
    return pltpu.with_memory_space_constraint(array, pltpu.HBM)


def relax(adjoint, medium, rotors, step_size, slot_turbine, moved_rotors, new_brick, sizes):
    n = sizes[0] * sizes[1]
    vmem, hbm = pl.BlockSpec(memory_space=pltpu.VMEM), pl.BlockSpec(memory_space=pltpu.HBM)
    channels, count, width, depth = adjoint.shape
    slots, moved_dev = slot_turbine.shape[0], moved_rotors.shape[0]
    return pl.pallas_call(
        functools.partial(relax_kernel, sizes),
        out_shape=(
            jax.ShapeDtypeStruct(adjoint.shape, jnp.float32),
            jax.ShapeDtypeStruct((n, 8, LANES), jnp.float32),
        ),
        in_specs=[hbm] * 4 + [pl.BlockSpec(memory_space=pltpu.SMEM)] + [hbm] * 2,
        out_specs=(vmem, vmem),
        scratch_shapes=[
            pltpu.VMEM(rotors.shape, jnp.float32),
            pltpu.VMEM((1, slots), jnp.int32),
            pltpu.VMEM((1, moved_dev), jnp.int32),
            pltpu.VMEM((1, moved_dev), jnp.int32),
            pltpu.VMEM(medium.shape, jnp.bfloat16),
            pltpu.VMEM(adjoint.shape, jnp.float32),
            pltpu.VMEM(adjoint.shape, jnp.float32),
            pltpu.VMEM((4,) + adjoint.shape[1:], jnp.float32),
            pltpu.VMEM((channels, count + 2, width + 16, depth), jnp.float32),
            pltpu.VMEM((2, 2, channels, width, depth), jnp.bfloat16),
            pltpu.VMEM((2, 2, channels, width, depth), jnp.bfloat16),
            pltpu.VMEM((2, channels, count, depth), jnp.float32),
            pltpu.VMEM((2, 2, channels, count, depth), jnp.bfloat16),
            pltpu.VMEM((2, 2, channels, count, depth), jnp.bfloat16),
            pltpu.VMEM((8, LANES), jnp.float32),
            pltpu.VMEM((n, 8, LANES), jnp.float32),
            pltpu.SemaphoreType.DMA((4,)),
            pltpu.SemaphoreType.DMA((3, 2)),
            pltpu.SemaphoreType.DMA((count // CHUNK, 3)),
            pltpu.SemaphoreType.DMA((2, 4)),
            pltpu.SemaphoreType.DMA((2, 4)),
            pltpu.SemaphoreType.DMA((sizes[0] + sizes[1],)),
            pltpu.SemaphoreType.DMA((sizes[0] + sizes[1],)),
        ],
        compiler_params=pltpu.CompilerParams(
            collective_id=0, has_side_effects=True, vmem_limit_bytes=46 * 1024 * 1024
        ),
        name="relax",
    )(
        in_hbm(rotors),
        in_hbm(slot_turbine.reshape(1, slots)),
        in_hbm(moved_rotors.reshape(1, moved_dev)),
        in_hbm(new_brick.reshape(1, moved_dev)),
        step_size,
        adjoint,
        medium,
    )


def z_weights(depth):
    z = np.arange(depth)[:, None] - np.arange(depth)[None, :]
    height = z + 0.5 - KZ / 2.0
    values = np.exp(-(height**2) / (2.0 * SIGMA_RADIAL**2)) * ((z >= 0) & (z < KZ))
    values = values.astype(np.float32)
    high = values.astype(jnp.bfloat16)
    low = (values - high.astype(np.float32)).astype(jnp.bfloat16)
    return np.block([[high, low], [high, np.zeros_like(low)]])


def weigh_kernel(
    sizes,
    turb_dev,
    corner_hbm,
    profile_hbm,
    table,
    q,
    out_hbm,
    conv,
    coef,
    place,
    corner,
    profile,
    small_sem,
    out_sem,
):
    _, count, width, depth = q.shape
    n, slots = table.shape[0], corner.shape[1]
    groups = -(-slots // LANES)
    me = lax.axis_index("gx") * sizes[1] + lax.axis_index("gy")

    small = [
        pltpu.make_async_copy(profile_hbm, profile, small_sem.at[0]),
        pltpu.make_async_copy(corner_hbm, corner, small_sem.at[1]),
    ]
    parts = out_sem.shape[0]
    share = count // parts
    writes = []
    for i in range(parts):
        part = pl.ds(i * share, share)
        writes.append(
            pltpu.make_async_copy(q.at[:, part], out_hbm.at[:, part], out_sem.at[i])
        )
    for copy in small + writes:
        copy.start()

    own = table[me]
    lane = lax.broadcasted_iota(jnp.int32, (1, LANES), 1)
    for group in range(groups):
        turbine = jnp.maximum(own[5 + group : 6 + group], 0.0).astype(jnp.int32)
        owner, local = lax.div(turbine, turb_dev), lax.rem(turbine, turb_dev)
        owner = jnp.broadcast_to(owner, (8, LANES))
        local = jnp.broadcast_to(local, (8, LANES))

        def gather(d, fields):
            found = jnp.take_along_axis(table[d], local, axis=1, mode="promise_in_bounds")
            return jnp.where(owner == d, found, fields)

        fields = lax.fori_loop(0, n, gather, jnp.zeros((8, LANES), jnp.float32), unroll=4)
        sub_x, sub_y, cosine, sine, thrust = [fields[i : i + 1] for i in range(5)]
        cell_y = lax.broadcasted_iota(jnp.int32, (KY, LANES), 0).astype(jnp.float32)
        delta_y = cell_y + (0.5 - KY / 2.0) - sub_y
        for a in range(KX):
            delta_x = (a + 0.5 - KX / 2.0) - sub_x
            along = cosine * delta_x + sine * delta_y
            across = cosine * delta_y - sine * delta_x
            kernel = thrust * jnp.exp(
                -along * along / (2.0 * SIGMA_AXIAL * SIGMA_AXIAL)
                - across * across / (2.0 * SIGMA_RADIAL * SIGMA_RADIAL)
            )
            axial = along * (1.0 / (SIGMA_AXIAL * SIGMA_AXIAL))
            radial = across * (1.0 / (SIGMA_RADIAL * SIGMA_RADIAL))
            coef[0, group, a] = kernel * (axial * cosine - radial * sine)
            coef[1, group, a] = kernel * (axial * sine + radial * cosine)

    for copy in small:
        copy.wait()
    for group in range(groups):
        size = min(LANES, slots - group * LANES)
        part = pl.ds(group * LANES, size)
        first_x = jnp.minimum(corner[0:1, part], count - KX)
        first_y = jnp.minimum(corner[1:2, part], width - KY)
        first_z = jnp.minimum(corner[2:3, part], depth - KZ)
        place[group : group + 1, pl.ds(0, size)] = first_x * width + first_y
        place[groups + group : groups + group + 1, pl.ds(0, size)] = (
            lane[:, :size] - first_z
        ) & (LANES - 1)

    @pl.loop(0, count // BATCH)
    def _(i):
        pieces = []
        for j in range(BATCH):
            plane = q[0, i * BATCH + j]
            high = plane.astype(jnp.bfloat16)
            low = (plane - high.astype(jnp.float32)).astype(jnp.bfloat16)
            pieces.append(jnp.concatenate([high, low], axis=1))
        both = jnp.dot(
            jnp.concatenate(pieces, axis=0), profile[...], preferred_element_type=jnp.float32
        )
        rows = BATCH * width
        conv[pl.ds(pl.multiple_of(i * rows, 8), rows)] = both[:, :depth] + both[:, depth:]

    for copy in writes:
        copy.wait()


def weigh(state, table, slot_corner, turb_dev, sizes):
    _, count, width, depth = state.shape
    slots = slot_corner.shape[1]
    groups = -(-slots // LANES)
    vmem, hbm = pl.BlockSpec(memory_space=pltpu.VMEM), pl.BlockSpec(memory_space=pltpu.HBM)
    profile = jnp.asarray(z_weights(depth))
    return pl.pallas_call(
        functools.partial(weigh_kernel, sizes, turb_dev),
        out_shape=(
            jax.ShapeDtypeStruct(state.shape, jnp.float32),
            jax.ShapeDtypeStruct((count * width, depth), jnp.float32),
            jax.ShapeDtypeStruct((2, groups, KX, KY, LANES), jnp.float32),
            jax.ShapeDtypeStruct((2 * groups, LANES), jnp.int32),
        ),
        in_specs=[hbm, hbm, vmem, vmem],
        out_specs=(hbm, vmem, vmem, vmem),
        scratch_shapes=[
            pltpu.VMEM(slot_corner.shape, jnp.int32),
            pltpu.VMEM(profile.shape, jnp.bfloat16),
            pltpu.SemaphoreType.DMA((2,)),
            pltpu.SemaphoreType.DMA((8,)),
        ],
        compiler_params=pltpu.CompilerParams(vmem_limit_bytes=8 * 1024 * 1024),
        name="weigh",
    )(slot_corner, profile, table, state)


def plan_rows(sizes, moved_dev, table, plan):
    n = sizes[0] * sizes[1]
    me = lax.axis_index("gx") * sizes[1] + lax.axis_index("gy")
    lines = table[:, 7]
    lane = lax.broadcasted_iota(jnp.int32, lines.shape, 1)
    mine = jnp.where((lines == me.astype(jnp.float32)) & (lane < moved_dev), 1.0, 0.0)

    def earlier(size, row, col):
        less = lax.broadcasted_iota(jnp.int32, (size, size), row) < lax.broadcasted_iota(
            jnp.int32, (size, size), col
        )
        return jnp.where(less, 1.0, 0.0).astype(jnp.bfloat16)

    rank = jnp.sum(
        jnp.dot(
            earlier(n, 1, 0), mine.astype(jnp.bfloat16), preferred_element_type=jnp.float32
        ),
        axis=1,
        keepdims=True,
    ) + jnp.dot(
        mine.astype(jnp.bfloat16), earlier(LANES, 0, 1), preferred_element_type=jnp.float32
    )
    shifted = [jnp.ones_like(lines)]
    shifted += [pltpu.roll(lines, LANES - moved_dev * f, 1) for f in range(1, 7)]
    chosen = [jnp.where(rank == float(slot), mine, 0.0) for slot in range(RECV)]
    for i, values in enumerate(shifted):
        parts = [jnp.sum(pick * values, axis=0, keepdims=True) for pick in chosen]
        total = jnp.sum(jnp.concatenate(parts, axis=0), axis=1, keepdims=True)
        plan[i] = jnp.broadcast_to(total, (RECV, LANES))


def share_kernel(
    sizes,
    slots,
    width,
    moved_dev,
    conv,
    coef,
    place_vmem,
    table,
    out,
    plan,
    mine,
    every,
    place,
    place_sem,
    ssem,
    rsem,
):
    n, n_gy = sizes[0] * sizes[1], sizes[1]
    me = lax.axis_index("gx") * n_gy + lax.axis_index("gy")
    barrier = pltpu.get_barrier_semaphore()
    fetch = pltpu.make_async_copy(place_vmem, place, place_sem)
    fetch.start()

    def other(d):
        number = lax.rem(me + d, n)
        return lax.div(number, n_gy), lax.rem(number, n_gy)

    @pl.loop(1, n)
    def _(d):
        pl.semaphore_signal(barrier, inc=1, device_id=other(d), device_id_type=MESH)

    fetch.wait()
    groups = -(-slots // LANES)
    lane = lax.broadcasted_iota(jnp.int32, (KY, LANES), 1)
    for group in range(groups):

        def collect(slot, blocks):
            base, shift = place[group, slot], place[groups + group, slot]
            here = lane == slot
            return tuple(
                jnp.where(here, pltpu.roll(conv[pl.ds(base + a * width, KY)], shift, 1), old)
                for a, old in enumerate(blocks)
            )

        size = min(LANES, slots - group * LANES)
        blank = jnp.zeros((KY, LANES), jnp.float32)
        blocks = lax.fori_loop(0, size, collect, (blank,) * KX, unroll=16)
        for i in range(2):
            total = blocks[0] * coef[i, group, 0]
            for a in range(1, KX):
                total = total + blocks[a] * coef[i, group, a]
            row = i * groups + group
            mine[row : row + 1] = jnp.sum(total, axis=0, keepdims=True)

    every[me] = mine[...]
    pl.semaphore_wait(barrier, n - 1)

    @pl.loop(1, n)
    def _(d):
        pltpu.make_async_remote_copy(
            src_ref=mine,
            dst_ref=every.at[me],
            send_sem=ssem,
            recv_sem=rsem,
            device_id=other(d),
            device_id_type=MESH,
        ).start()

    plan_rows(sizes, moved_dev, table, plan)
    rest = every.at[pl.ds(0, n - 1)]
    total = pltpu.make_async_remote_copy(
        src_ref=rest,
        dst_ref=rest,
        send_sem=ssem,
        recv_sem=rsem,
        device_id=other(1),
        device_id_type=MESH,
    )
    total.wait()
    out[...] = every[...]


def finish_kernel(sizes, groups, every, table, plan, step_out, incoming):
    n = sizes[0] * sizes[1]
    me = lax.axis_index("gx") * sizes[1] + lax.axis_index("gy")
    turb_dev = step_out.shape[1]
    valid, wanted, sub_x, sub_y, cosine, sine, thrust = [plan[i] for i in range(7)]
    own = (
        me * turb_dev + lax.broadcasted_iota(jnp.int32, (turb_dev, LANES), 0)
    ).astype(jnp.float32)
    targets = jnp.concatenate([own, wanted], axis=0)

    def collect(d, carry):
        sum_x, sum_y = carry
        for group in range(groups):
            hit = targets == table[d, pl.ds(5 + group, 1)]
            sum_x = jnp.where(hit, every[d, pl.ds(group, 1)], sum_x)
            sum_y = jnp.where(hit, every[d, pl.ds(groups + group, 1)], sum_y)
        return sum_x, sum_y

    zero = jnp.zeros((turb_dev + RECV, LANES), jnp.float32)
    sums = lax.fori_loop(0, n, collect, (zero, zero), unroll=2)
    step = table[0, 0:1, LANES - 1 : LANES]
    taken = [
        jnp.clip(-step * jnp.sum(part, axis=1, keepdims=True), -0.5, 0.5) for part in sums
    ]
    flip = lax.broadcasted_iota(jnp.int32, (turb_dev, turb_dev), 0) == lax.broadcasted_iota(
        jnp.int32, (turb_dev, turb_dev), 1
    )
    for i in range(2):
        step_out[i : i + 1] = jnp.sum(
            jnp.where(flip, taken[i][:turb_dev], 0.0), axis=0, keepdims=True
        )
    cells = KX * KY * KZ
    cell = lax.broadcasted_iota(jnp.int32, (RECV, cells), 1)
    ex = (cell // (KY * KZ)).astype(jnp.float32) + 0.5 - KX / 2.0
    ey = lax.rem(cell // KZ, KY).astype(jnp.float32) + 0.5 - KY / 2.0
    ez = lax.rem(cell, KZ).astype(jnp.float32) + 0.5 - KZ / 2.0
    column = slice(0, 1)
    delta_x = ex - (sub_x[:, column] + taken[0][turb_dev:])
    delta_y = ey - (sub_y[:, column] + taken[1][turb_dev:])
    cosine, sine = cosine[:, column], sine[:, column]
    along = cosine * delta_x + sine * delta_y
    across = cosine * delta_y - sine * delta_x
    kernel = thrust[:, column] * jnp.exp(
        -along * along / (2.0 * SIGMA_AXIAL * SIGMA_AXIAL)
        - (across * across + ez * ez) / (2.0 * SIGMA_RADIAL * SIGMA_RADIAL)
    )
    incoming[...] = jnp.where(valid[:, column] > 0, kernel, 0.0).astype(jnp.bfloat16)


def finish(conv, coef, place, table, slots, width, turb_dev, moved_dev, sizes):
    n = sizes[0] * sizes[1]
    groups = -(-slots // LANES)
    vmem = pl.BlockSpec(memory_space=pltpu.VMEM)

    every, plan = pl.pallas_call(
        functools.partial(share_kernel, sizes, slots, width, moved_dev),
        out_shape=(
            jax.ShapeDtypeStruct((n, 2 * groups, LANES), jnp.float32),
            jax.ShapeDtypeStruct((7, RECV, LANES), jnp.float32),
        ),
        in_specs=[vmem] * 4,
        out_specs=(vmem, vmem),
        scratch_shapes=[
            pltpu.VMEM((2 * groups, LANES), jnp.float32),
            pltpu.VMEM((n, 2 * groups, LANES), jnp.float32),
            pltpu.SMEM(place.shape, jnp.int32),
            pltpu.SemaphoreType.DMA,
            pltpu.SemaphoreType.DMA,
            pltpu.SemaphoreType.DMA,
        ],
        compiler_params=pltpu.CompilerParams(
            collective_id=1, has_side_effects=True, vmem_limit_bytes=8 * 1024 * 1024
        ),
        name="share",
    )(conv, coef, place, table)
    return pl.pallas_call(
        functools.partial(finish_kernel, sizes, groups),
        out_shape=(
            jax.ShapeDtypeStruct((2, turb_dev), jnp.float32),
            jax.ShapeDtypeStruct((RECV, KX * KY * KZ), jnp.bfloat16),
        ),
        in_specs=[vmem, vmem, vmem],
        out_specs=(vmem, vmem),
        compiler_params=pltpu.CompilerParams(vmem_limit_bytes=8 * 1024 * 1024),
        name="finish",
    )(every, table, plan)


def body(
    sizes, adjoint, medium, rotors, step_size, slot_turbine, slot_corner, moved_rotors, new_brick
):
    turb_dev, slots = rotors.shape[1], slot_turbine.shape[0]
    state, table = relax(
        adjoint, medium, rotors, step_size, slot_turbine, moved_rotors, new_brick, sizes
    )
    state, conv, coef, place = weigh(state, table, slot_corner, turb_dev, sizes)
    step_taken, incoming = finish(
        conv,
        coef,
        place,
        table,
        slots,
        adjoint.shape[2],
        turb_dev,
        moved_rotors.shape[0],
        sizes,
    )
    return (state, step_taken, incoming)


def solution(mesh):
    sizes = (mesh.shape["gx"], mesh.shape["gy"])
    return jax.shard_map(
        functools.partial(body, sizes),
        mesh=mesh,
        in_specs=(
            P(None, "gx", "gy", None),
            P(None, "gx", "gy", None),
            P(None, ("gx", "gy")),
            P(),
            P(("gx", "gy")),
            P(None, ("gx", "gy")),
            P(("gx", "gy")),
            P(("gx", "gy"), None),
        ),
        out_specs=(P(None, "gx", "gy", None), P(None, ("gx", "gy")), P(("gx", "gy"), None)),
        check_vma=False,
    )
```

```python
import functools

import jax
import jax.numpy as jnp
import numpy as np
from jax import lax
from jax.experimental import pallas as pl
from jax.experimental.pallas import tpu as pltpu
from jax.sharding import PartitionSpec as P

KX = 8
KY = 16
KZ = 16
SWEEPS = 2
RECV = 8
EDGE = 16
CHUNK = 8
LONG = 16
STRIP = 16
LANES = 128
BATCH = 16


TAU = 0.05
SIGMA_AXIAL = 1.5
SIGMA_RADIAL = 4.0
MESH = pl.DeviceIdType.MESH


def strips(rows):
    return [(pl.ds(start, STRIP), pl.ds(8 + start, STRIP)) for start in range(0, rows, STRIP)]


def prepare(med, src, keep, scaled, fb, first, fresh, planes=CHUNK):
    for j in range(planes):
        x = first + j
        for part, mid in strips(src.shape[2]):
            if fresh:
                viscous, velocity, reaction, coupling, source = [
                    TAU * med[i, x, part].astype(jnp.float32) for i in range(5)
                ]
                pull = viscous + velocity
                kept = 1.0 - 5.0 * viscous - (pull + reaction)
                scaled[0, x, part] = viscous
                scaled[1, x, part] = pull
                scaled[2, x, part] = coupling
                scaled[3, x, part] = source
                keep[0, x, part] = kept
                keep[1, x, part] = kept - reaction
            else:
                viscous = scaled[0, x, part]
            for c in range(2):
                fb[c, x + 1, mid] = viscous * src[c, x, part]


def update(src, dst, keep, scaled, fb, first, last, planes=CHUNK):
    rows, depth = src.shape[2:]
    col = lax.broadcasted_iota(jnp.int32, (STRIP, depth), 1)
    bottom, top = col == 0, col == depth - 1
    for start in range(0, rows, STRIP):
        part, mid = pl.ds(start, STRIP), pl.ds(8 + start, STRIP)
        below, above = pl.ds(7 + start, STRIP), pl.ds(9 + start, STRIP)
        values = src[0, first, part], src[1, first, part]
        behind = [fb[c, first, mid].astype(jnp.bfloat16) for c in range(2)]
        for j in range(planes):
            x = first + j
            more = j + 1 < planes or not last
            if more:
                pull = scaled[1, x + 1, part]
                ahead = src[0, x + 1, part], src[1, x + 1, part]
            coupling = scaled[2, x, part]
            here = [fb[c, x + 1, mid].astype(jnp.bfloat16) for c in range(2)]
            zero = jnp.zeros_like(here[0])
            for c in range(2):
                sides = jnp.where(bottom, zero, pltpu.roll(here[c], 1, 1))
                sides = sides + jnp.where(top, zero, pltpu.roll(here[c], depth - 1, 1))
                sides = sides + behind[c]
                total = fb[c, x + 1, below] + fb[c, x + 1, above]
                if more:
                    total = total + pull * ahead[c]
                total = total - coupling * values[1 - c]
                if c == 0:
                    total = total + scaled[3, x, part]
                total = total + sides.astype(jnp.float32)
                dst[c, x, part] = keep[c, x, part] * values[c] + total
            behind = here
            if more:
                values = ahead


def pack_tables(me, rotors, listed, moved, target, step, pack):
    turb_dev, slots, moved_dev = rotors.shape[1], listed.shape[1], moved.shape[1]
    pack[...] = jnp.full(pack.shape, -1.0, jnp.float32)
    own = pl.ds(0, turb_dev)
    pack[0:2, own] = rotors[0:2]
    pack[2:3, own] = jnp.cos(rotors[2:3])
    pack[3:4, own] = jnp.sin(rotors[2:3])
    pack[4:5, own] = rotors[3:4]
    pack[0:1, pl.ds(LANES - 1, 1)] = jnp.full((1, 1), step[...], jnp.float32)
    for group in range(-(-slots // LANES)):
        size = min(LANES, slots - group * LANES)
        pack[5 + group : 6 + group, pl.ds(0, size)] = listed[
            :, pl.ds(group * LANES, size)
        ].astype(jnp.float32)
    full = pack[...]
    lane = lax.broadcasted_iota(jnp.int32, full.shape, 1)
    field = lax.broadcasted_iota(jnp.int32, full.shape, 0) + 2
    line = jnp.full((1, LANES), -1.0, jnp.float32)
    chosen, wanted = moved[...].astype(jnp.float32), target[...].astype(jnp.float32)
    for j in range(moved_dev):
        local = chosen[:, j : j + 1]
        picked = jnp.sum(
            jnp.where(lane.astype(jnp.float32) == local, full, 0.0), axis=1, keepdims=True
        )
        here = (lane == moved_dev * field + j) & (field < 7)
        spread = jnp.sum(jnp.where(here, picked, 0.0), axis=0, keepdims=True)
        place = lane[0:1]
        for f in range(2, 7):
            line = jnp.where(place == moved_dev * f + j, spread, line)
        line = jnp.where(place == j, wanted[:, j : j + 1], line)
        number = (me * turb_dev).astype(jnp.float32) + local
        line = jnp.where(place == moved_dev + j, number, line)
    pack[7:8] = line


def greet(sizes):
    n_gx, n_gy = sizes
    gx, gy = lax.axis_index("gx"), lax.axis_index("gy")
    barrier = pltpu.get_barrier_semaphore()
    for j in range(1, n_gy):
        pl.semaphore_signal(
            barrier, inc=1, device_id=(gx, lax.rem(gy + j, n_gy)), device_id_type=MESH
        )
    for j in range(1, n_gx):
        pl.semaphore_signal(
            barrier, inc=1, device_id=(lax.rem(gx + j, n_gx), gy), device_id_type=MESH
        )
    return n_gx + n_gy - 2


def spread_y(sizes, own, every, ssem, rsem):
    n_gy = sizes[1]
    gx, gy = lax.axis_index("gx"), lax.axis_index("gy")
    return [
        pltpu.make_async_remote_copy(
            src_ref=own,
            dst_ref=every.at[gx * n_gy + gy],
            send_sem=ssem.at[j],
            recv_sem=rsem.at[j],
            device_id=(gx, lax.rem(gy + j, n_gy)),
            device_id_type=MESH,
        )
        for j in range(1, n_gy)
    ]


def spread_x(sizes, every, ssem, rsem):
    n_gx, n_gy = sizes
    gx, gy = lax.axis_index("gx"), lax.axis_index("gy")
    block = every.at[pl.ds(gx * n_gy, n_gy)]
    return [
        pltpu.make_async_remote_copy(
            src_ref=block,
            dst_ref=block,
            send_sem=ssem.at[n_gy + j],
            recv_sem=rsem.at[n_gy + j],
            device_id=(lax.rem(gx + j, n_gx), gy),
            device_id_type=MESH,
        )
        for j in range(1, n_gx)
    ]


def relax_kernel(
    sizes,
    rotors_hbm,
    listed_hbm,
    moved_hbm,
    target_hbm,
    step,
    q_hbm,
    med_hbm,
    q,
    every,
    rotors,
    listed,
    moved,
    target,
    med,
    q1,
    keep,
    scaled,
    fb,
    xs,
    xr,
    ys,
    yb,
    yr,
    pack,
    table,
    small_sem,
    edge_sem,
    in_sem,
    ssem,
    rsem,
    tsend,
    trecv,
):
    n_gx, n_gy = sizes
    _, count, width, depth = q.shape
    chunks = count // CHUNK
    gx, gy = lax.axis_index("gx"), lax.axis_index("gy")
    x_lo, x_hi = lax.rem(gx + n_gx - 1, n_gx), lax.rem(gx + 1, n_gx)
    y_lo, y_hi = lax.rem(gy + n_gy - 1, n_gy), lax.rem(gy + 1, n_gy)
    peers = ((x_lo, gy), (x_hi, gy), (gx, y_lo), (gx, y_hi))
    q_mid, mid = pl.ds(8, width - 16), pl.ds(EDGE, width - 2 * EDGE)
    q_edges = (pl.ds(0, 8), pl.ds(width - 8, 8))
    edges = (pl.ds(0, EDGE), pl.ds(width - EDGE, EDGE))

    def fetch(which, planes, rows, sem):
        src, dst = (q_hbm.at[:], q.at[:]) if which is None else (med_hbm.at[which], med.at[which])
        return pltpu.make_async_copy(src.at[:, planes, rows], dst.at[:, planes, rows], sem)

    whole, end = pl.ds(0, width), pl.ds(count - 1, 1)
    head, tail = pl.ds(0, CHUNK), pl.ds(CHUNK, count - CHUNK)
    every_field, viscous, others = pl.ds(0, 5), pl.ds(0, 1), pl.ds(1, 4)
    head_in = [
        fetch(None, head, whole, in_sem.at[0, 0]),
        fetch(every_field, head, whole, in_sem.at[0, 1]),
    ]
    edge_in = []
    for i in range(2):
        edge_in.append(fetch(None, tail, q_edges[i], edge_sem.at[i, 0]))
        edge_in.append(fetch(viscous, tail, edges[i], edge_sem.at[i, 1]))
    edge_in += [
        fetch(None, end, q_mid, edge_sem.at[2, 0]),
        fetch(viscous, end, mid, edge_sem.at[2, 1]),
    ]

    def chunk_in(i, size=CHUNK):
        part, all_of_it = pl.ds(i * CHUNK, size), pl.ds(i * CHUNK, CHUNK)
        return (
            fetch(None, part, q_mid, in_sem.at[i, 0]),
            fetch(viscous, part, mid, in_sem.at[i, 1]),
            fetch(others, all_of_it, whole, in_sem.at[i, 2]),
        )

    last_in = chunk_in(chunks - 1, CHUNK - 1)
    small = [
        pltpu.make_async_copy(rotors_hbm, rotors, small_sem.at[0]),
        pltpu.make_async_copy(listed_hbm, listed, small_sem.at[1]),
        pltpu.make_async_copy(moved_hbm, moved, small_sem.at[2]),
        pltpu.make_async_copy(target_hbm, target, small_sem.at[3]),
    ]
    for copy in head_in + edge_in + small:
        copy.start()

    @pl.loop(1, chunks - 1)
    def _(i):
        for copy in chunk_in(i):
            copy.start()

    for copy in last_in:
        copy.start()

    barrier = pltpu.get_barrier_semaphore()
    me = gx * n_gy + gy

    met = greet(sizes)
    blank = jnp.zeros((8, depth), jnp.float32)

    @pl.loop(0, count + 2, unroll=2)
    def _(x):
        for c in range(2):
            fb[c, x, pl.ds(0, 8)] = blank
            fb[c, x, pl.ds(8 + width, 8)] = blank

    for c in range(2):
        fb[c, 0, pl.ds(8, width)] = jnp.zeros((width, depth), jnp.float32)
    for copy in small:
        copy.wait()
    pack_tables(me, rotors, listed, moved, target, step, pack)

    has_lo_x, has_hi_x, has_lo_y, has_hi_y = gx > 0, gx < n_gx - 1, gy > 0, gy < n_gy - 1
    sends = (has_lo_x, has_hi_x, has_lo_y, has_hi_y)
    receives = (has_hi_x, has_lo_x, has_hi_y, has_lo_y)

    def face(turn, side):
        src, dst = (xs, xr) if side < 2 else (yb, yr)
        return pltpu.make_async_remote_copy(
            src_ref=src.at[turn, side % 2],
            dst_ref=dst.at[turn, side % 2],
            send_sem=ssem.at[turn, side],
            recv_sem=rsem.at[turn, side],
            device_id=peers[side],
            device_id_type=MESH,
        )

    def send(turn, side):
        @pl.when(sends[side])
        def _():
            face(turn, side).start()

    def exchange(turn, src):
        for c in range(2):
            low, high = med[0, 0].astype(jnp.float32), med[0, count - 1].astype(jnp.float32)
            low = (low + med[1, 0].astype(jnp.float32)) * src[c, 0]
            xs[turn, 0, c] = low.astype(jnp.bfloat16)
            xs[turn, 1, c] = (high * src[c, count - 1]).astype(jnp.bfloat16)

        for side in (0, 1):
            send(turn, side)

        @pl.loop(0, count, unroll=8)
        def _(x):
            low = med[0, x, pl.ds(0, EDGE)].astype(jnp.float32)[:8]
            high = med[0, x, pl.ds(width - EDGE, EDGE)].astype(jnp.float32)[8:]
            for c in range(2):
                ys[0, c, pl.ds(x, 1)] = (low * src[c, x, pl.ds(0, 8)])[:1]
                ys[1, c, pl.ds(x, 1)] = (high * src[c, x, pl.ds(width - 8, 8)])[7:]

        for side in (2, 3):
            yb[turn, side - 2] = ys[side - 2].astype(jnp.bfloat16)
            send(turn, side)

    def patch(turn, dst):
        for side in range(4):

            @pl.when(sends[side])
            def _():
                face(turn, side).wait_send()

            @pl.when(receives[side])
            def _():
                face(turn, side).wait_recv()
                if side < 2:
                    x = 0 if side else count - 1
                    for c in range(2):
                        dst[c, x] = dst[c, x] + TAU * xr[turn, side, c].astype(jnp.float32)
                else:
                    ys[side - 2] = TAU * yr[turn, side - 2].astype(jnp.float32)
                    line = pl.ds(0 if side == 3 else width - 1, 1)

                    @pl.loop(0, count, unroll=16)
                    def _(x):
                        for c in range(2):
                            dst[c, x, line] = dst[c, x, line] + ys[side - 2, c, pl.ds(x, 1)]

    for copy in head_in:
        copy.wait()
    prepare(med, q, keep, scaled, fb, 0, True)
    for copy in edge_in:
        copy.wait()
    pl.semaphore_wait(barrier, met)
    exchange(0, q)

    table[me] = pack[...]
    along_y = spread_y(sizes, pack, table, tsend, trecv)
    for copy in along_y:
        copy.start()

    @pl.loop(0, chunks - 1)
    def _(i):
        @pl.when(i + 1 < chunks - 1)
        def _():
            for copy in chunk_in(i + 1):
                copy.wait()

        @pl.when(i + 1 == chunks - 1)
        def _():
            for copy in last_in:
                copy.wait()

        prepare(med, q, keep, scaled, fb, (i + 1) * CHUNK, True)
        update(q, q1, keep, scaled, fb, i * CHUNK, False)

    update(q, q1, keep, scaled, fb, count - CHUNK, True)

    patch(0, q1)
    exchange(1, q1)
    for copy in along_y:
        copy.wait()
    along_x = spread_x(sizes, table, tsend, trecv)
    for copy in along_x:
        copy.start()

    prepare(med, q1, keep, scaled, fb, 0, False, LONG)

    @pl.loop(0, count // LONG - 1)
    def _(i):
        prepare(med, q1, keep, scaled, fb, (i + 1) * LONG, False, LONG)
        update(q1, q, keep, scaled, fb, i * LONG, False, LONG)

    update(q1, q, keep, scaled, fb, count - LONG, True, LONG)

    for copy in along_x:
        copy.wait()
    every[...] = table[...]
    patch(1, q)


def in_hbm(array):
    return pltpu.with_memory_space_constraint(array, pltpu.HBM)


def relax(adjoint, medium, rotors, step_size, slot_turbine, moved_rotors, new_brick, sizes):
    n = sizes[0] * sizes[1]
    vmem, hbm = pl.BlockSpec(memory_space=pltpu.VMEM), pl.BlockSpec(memory_space=pltpu.HBM)
    channels, count, width, depth = adjoint.shape
    slots, moved_dev = slot_turbine.shape[0], moved_rotors.shape[0]
    return pl.pallas_call(
        functools.partial(relax_kernel, sizes),
        out_shape=(
            jax.ShapeDtypeStruct(adjoint.shape, jnp.float32),
            jax.ShapeDtypeStruct((n, 8, LANES), jnp.float32),
        ),
        in_specs=[hbm] * 4 + [pl.BlockSpec(memory_space=pltpu.SMEM)] + [hbm] * 2,
        out_specs=(vmem, vmem),
        scratch_shapes=[
            pltpu.VMEM(rotors.shape, jnp.float32),
            pltpu.VMEM((1, slots), jnp.int32),
            pltpu.VMEM((1, moved_dev), jnp.int32),
            pltpu.VMEM((1, moved_dev), jnp.int32),
            pltpu.VMEM(medium.shape, jnp.bfloat16),
            pltpu.VMEM(adjoint.shape, jnp.float32),
            pltpu.VMEM(adjoint.shape, jnp.float32),
            pltpu.VMEM((4,) + adjoint.shape[1:], jnp.float32),
            pltpu.VMEM((channels, count + 2, width + 16, depth), jnp.float32),
            pltpu.VMEM((2, 2, channels, width, depth), jnp.bfloat16),
            pltpu.VMEM((2, 2, channels, width, depth), jnp.bfloat16),
            pltpu.VMEM((2, channels, count, depth), jnp.float32),
            pltpu.VMEM((2, 2, channels, count, depth), jnp.bfloat16),
            pltpu.VMEM((2, 2, channels, count, depth), jnp.bfloat16),
            pltpu.VMEM((8, LANES), jnp.float32),
            pltpu.VMEM((n, 8, LANES), jnp.float32),
            pltpu.SemaphoreType.DMA((4,)),
            pltpu.SemaphoreType.DMA((3, 2)),
            pltpu.SemaphoreType.DMA((count // CHUNK, 3)),
            pltpu.SemaphoreType.DMA((2, 4)),
            pltpu.SemaphoreType.DMA((2, 4)),
            pltpu.SemaphoreType.DMA((sizes[0] + sizes[1],)),
            pltpu.SemaphoreType.DMA((sizes[0] + sizes[1],)),
        ],
        compiler_params=pltpu.CompilerParams(
            collective_id=0, has_side_effects=True, vmem_limit_bytes=46 * 1024 * 1024
        ),
        name="relax",
    )(
        in_hbm(rotors),
        in_hbm(slot_turbine.reshape(1, slots)),
        in_hbm(moved_rotors.reshape(1, moved_dev)),
        in_hbm(new_brick.reshape(1, moved_dev)),
        step_size,
        adjoint,
        medium,
    )


def z_weights(depth):
    z = np.arange(depth)[:, None] - np.arange(depth)[None, :]
    height = z + 0.5 - KZ / 2.0
    values = np.exp(-(height**2) / (2.0 * SIGMA_RADIAL**2)) * ((z >= 0) & (z < KZ))
    values = values.astype(np.float32)
    high = values.astype(jnp.bfloat16)
    low = (values - high.astype(np.float32)).astype(jnp.bfloat16)
    return np.block([[high, low], [high, np.zeros_like(low)]])


def weigh_kernel(
    sizes,
    turb_dev,
    corner_hbm,
    profile_hbm,
    table,
    q,
    out_hbm,
    conv,
    coef,
    place,
    corner,
    profile,
    small_sem,
    out_sem,
):
    _, count, width, depth = q.shape
    n, slots = table.shape[0], corner.shape[1]
    groups = -(-slots // LANES)
    me = lax.axis_index("gx") * sizes[1] + lax.axis_index("gy")

    small = [
        pltpu.make_async_copy(profile_hbm, profile, small_sem.at[0]),
        pltpu.make_async_copy(corner_hbm, corner, small_sem.at[1]),
    ]
    parts = out_sem.shape[0]
    share = count // parts
    writes = []
    for i in range(parts):
        part = pl.ds(i * share, share)
        writes.append(
            pltpu.make_async_copy(q.at[:, part], out_hbm.at[:, part], out_sem.at[i])
        )
    for copy in small + writes:
        copy.start()

    own = table[me]
    lane = lax.broadcasted_iota(jnp.int32, (1, LANES), 1)
    owners, locals_ = [], []
    for group in range(groups):
        turbine = jnp.maximum(own[5 + group : 6 + group], 0.0).astype(jnp.int32)
        owners.append(jnp.broadcast_to(lax.div(turbine, turb_dev), (8, LANES)))
        locals_.append(jnp.broadcast_to(lax.rem(turbine, turb_dev), (8, LANES)))

    def gather(d, carry):
        rows = table[d]
        return tuple(
            jnp.where(
                owner == d,
                jnp.take_along_axis(rows, local, axis=1, mode="promise_in_bounds"),
                fields,
            )
            for owner, local, fields in zip(owners, locals_, carry)
        )

    blank = jnp.zeros((8, LANES), jnp.float32)
    gathered = lax.fori_loop(0, n, gather, (blank,) * groups, unroll=16)
    for group, fields in enumerate(gathered):
        sub_x, sub_y, cosine, sine, thrust = [fields[i : i + 1] for i in range(5)]
        cell_y = lax.broadcasted_iota(jnp.int32, (KY, LANES), 0).astype(jnp.float32)
        delta_y = cell_y + (0.5 - KY / 2.0) - sub_y
        for a in range(KX):
            delta_x = (a + 0.5 - KX / 2.0) - sub_x
            along = cosine * delta_x + sine * delta_y
            across = cosine * delta_y - sine * delta_x
            kernel = thrust * jnp.exp(
                -along * along / (2.0 * SIGMA_AXIAL * SIGMA_AXIAL)
                - across * across / (2.0 * SIGMA_RADIAL * SIGMA_RADIAL)
            )
            axial = along * (1.0 / (SIGMA_AXIAL * SIGMA_AXIAL))
            radial = across * (1.0 / (SIGMA_RADIAL * SIGMA_RADIAL))
            coef[0, group, a] = kernel * (axial * cosine - radial * sine)
            coef[1, group, a] = kernel * (axial * sine + radial * cosine)

    for copy in small:
        copy.wait()
    for group in range(groups):
        size = min(LANES, slots - group * LANES)
        part = pl.ds(group * LANES, size)
        first_x = jnp.minimum(corner[0:1, part], count - KX)
        first_y = jnp.minimum(corner[1:2, part], width - KY)
        first_z = jnp.minimum(corner[2:3, part], depth - KZ)
        place[group : group + 1, pl.ds(0, size)] = first_x * width + first_y
        place[groups + group : groups + group + 1, pl.ds(0, size)] = (
            lane[:, :size] - first_z
        ) & (LANES - 1)

    @pl.loop(0, count // BATCH)
    def _(i):
        pieces = []
        for j in range(BATCH):
            plane = q[0, i * BATCH + j]
            high = plane.astype(jnp.bfloat16)
            low = (plane - high.astype(jnp.float32)).astype(jnp.bfloat16)
            pieces.append(jnp.concatenate([high, low], axis=1))
        both = jnp.dot(
            jnp.concatenate(pieces, axis=0), profile[...], preferred_element_type=jnp.float32
        )
        rows = BATCH * width
        conv[pl.ds(pl.multiple_of(i * rows, 8), rows)] = both[:, :depth] + both[:, depth:]

    for copy in writes:
        copy.wait()


def weigh(state, table, slot_corner, turb_dev, sizes):
    _, count, width, depth = state.shape
    slots = slot_corner.shape[1]
    groups = -(-slots // LANES)
    vmem, hbm = pl.BlockSpec(memory_space=pltpu.VMEM), pl.BlockSpec(memory_space=pltpu.HBM)
    profile = jnp.asarray(z_weights(depth))
    return pl.pallas_call(
        functools.partial(weigh_kernel, sizes, turb_dev),
        out_shape=(
            jax.ShapeDtypeStruct(state.shape, jnp.float32),
            jax.ShapeDtypeStruct((count * width, depth), jnp.float32),
            jax.ShapeDtypeStruct((2, groups, KX, KY, LANES), jnp.float32),
            jax.ShapeDtypeStruct((2 * groups, LANES), jnp.int32),
        ),
        in_specs=[hbm, hbm, vmem, vmem],
        out_specs=(hbm, vmem, vmem, vmem),
        scratch_shapes=[
            pltpu.VMEM(slot_corner.shape, jnp.int32),
            pltpu.VMEM(profile.shape, jnp.bfloat16),
            pltpu.SemaphoreType.DMA((2,)),
            pltpu.SemaphoreType.DMA((8,)),
        ],
        compiler_params=pltpu.CompilerParams(vmem_limit_bytes=8 * 1024 * 1024),
        name="weigh",
    )(slot_corner, profile, table, state)


def plan_rows(sizes, moved_dev, table, plan):
    n = sizes[0] * sizes[1]
    me = lax.axis_index("gx") * sizes[1] + lax.axis_index("gy")
    lines = table[:, 7]
    lane = lax.broadcasted_iota(jnp.int32, lines.shape, 1)
    mine = jnp.where((lines == me.astype(jnp.float32)) & (lane < moved_dev), 1.0, 0.0)

    def earlier(size, row, col):
        less = lax.broadcasted_iota(jnp.int32, (size, size), row) < lax.broadcasted_iota(
            jnp.int32, (size, size), col
        )
        return jnp.where(less, 1.0, 0.0).astype(jnp.bfloat16)

    rank = jnp.sum(
        jnp.dot(
            earlier(n, 1, 0), mine.astype(jnp.bfloat16), preferred_element_type=jnp.float32
        ),
        axis=1,
        keepdims=True,
    ) + jnp.dot(
        mine.astype(jnp.bfloat16), earlier(LANES, 0, 1), preferred_element_type=jnp.float32
    )
    shifted = [jnp.ones_like(lines)]
    shifted += [pltpu.roll(lines, LANES - moved_dev * f, 1) for f in range(1, 7)]
    chosen = [jnp.where(rank == float(slot), mine, 0.0) for slot in range(RECV)]
    for i, values in enumerate(shifted):
        parts = [jnp.sum(pick * values, axis=0, keepdims=True) for pick in chosen]
        total = jnp.sum(jnp.concatenate(parts, axis=0), axis=1, keepdims=True)
        plan[i] = jnp.broadcast_to(total, (RECV, LANES))


def share_kernel(
    sizes,
    slots,
    width,
    moved_dev,
    conv,
    coef,
    place_vmem,
    table,
    out,
    plan,
    mine,
    every,
    place,
    place_sem,
    ssem,
    rsem,
):
    n, n_gy = sizes[0] * sizes[1], sizes[1]
    me = lax.axis_index("gx") * n_gy + lax.axis_index("gy")
    barrier = pltpu.get_barrier_semaphore()
    fetch = pltpu.make_async_copy(place_vmem, place, place_sem)
    fetch.start()

    def other(d):
        number = lax.rem(me + d, n)
        return lax.div(number, n_gy), lax.rem(number, n_gy)

    @pl.loop(1, n)
    def _(d):
        pl.semaphore_signal(barrier, inc=1, device_id=other(d), device_id_type=MESH)

    fetch.wait()
    groups = -(-slots // LANES)
    lane = lax.broadcasted_iota(jnp.int32, (KY, LANES), 1)
    for group in range(groups):

        def collect(slot, blocks):
            base, shift = place[group, slot], place[groups + group, slot]
            here = lane == slot
            return tuple(
                jnp.where(here, pltpu.roll(conv[pl.ds(base + a * width, KY)], shift, 1), old)
                for a, old in enumerate(blocks)
            )

        size = min(LANES, slots - group * LANES)
        blank = jnp.zeros((KY, LANES), jnp.float32)
        blocks = lax.fori_loop(0, size, collect, (blank,) * KX, unroll=16)
        for i in range(2):
            total = blocks[0] * coef[i, group, 0]
            for a in range(1, KX):
                total = total + blocks[a] * coef[i, group, a]
            row = i * groups + group
            mine[row : row + 1] = jnp.sum(total, axis=0, keepdims=True)

    every[me] = mine[...]
    pl.semaphore_wait(barrier, n - 1)

    @pl.loop(1, n)
    def _(d):
        pltpu.make_async_remote_copy(
            src_ref=mine,
            dst_ref=every.at[me],
            send_sem=ssem,
            recv_sem=rsem,
            device_id=other(d),
            device_id_type=MESH,
        ).start()

    plan_rows(sizes, moved_dev, table, plan)
    rest = every.at[pl.ds(0, n - 1)]
    total = pltpu.make_async_remote_copy(
        src_ref=rest,
        dst_ref=rest,
        send_sem=ssem,
        recv_sem=rsem,
        device_id=other(1),
        device_id_type=MESH,
    )
    total.wait()
    out[...] = every[...]


def finish_kernel(sizes, groups, every, table, plan, step_out, incoming):
    n = sizes[0] * sizes[1]
    me = lax.axis_index("gx") * sizes[1] + lax.axis_index("gy")
    turb_dev = step_out.shape[1]
    valid, wanted, sub_x, sub_y, cosine, sine, thrust = [plan[i] for i in range(7)]
    own = (
        me * turb_dev + lax.broadcasted_iota(jnp.int32, (turb_dev, LANES), 0)
    ).astype(jnp.float32)
    targets = jnp.concatenate([own, wanted], axis=0)

    def collect(d, carry):
        sum_x, sum_y = carry
        for group in range(groups):
            hit = targets == table[d, pl.ds(5 + group, 1)]
            sum_x = jnp.where(hit, every[d, pl.ds(group, 1)], sum_x)
            sum_y = jnp.where(hit, every[d, pl.ds(groups + group, 1)], sum_y)
        return sum_x, sum_y

    zero = jnp.zeros((turb_dev + RECV, LANES), jnp.float32)
    sums = lax.fori_loop(0, n, collect, (zero, zero), unroll=8)
    step = table[0, 0:1, LANES - 1 : LANES]
    taken = [
        jnp.clip(-step * jnp.sum(part, axis=1, keepdims=True), -0.5, 0.5) for part in sums
    ]
    flip = lax.broadcasted_iota(jnp.int32, (turb_dev, turb_dev), 0) == lax.broadcasted_iota(
        jnp.int32, (turb_dev, turb_dev), 1
    )
    for i in range(2):
        step_out[i : i + 1] = jnp.sum(
            jnp.where(flip, taken[i][:turb_dev], 0.0), axis=0, keepdims=True
        )
    cells = KX * KY * KZ
    cell = lax.broadcasted_iota(jnp.int32, (RECV, cells), 1)
    ex = (cell // (KY * KZ)).astype(jnp.float32) + 0.5 - KX / 2.0
    ey = lax.rem(cell // KZ, KY).astype(jnp.float32) + 0.5 - KY / 2.0
    ez = lax.rem(cell, KZ).astype(jnp.float32) + 0.5 - KZ / 2.0
    column = slice(0, 1)
    delta_x = ex - (sub_x[:, column] + taken[0][turb_dev:])
    delta_y = ey - (sub_y[:, column] + taken[1][turb_dev:])
    cosine, sine = cosine[:, column], sine[:, column]
    along = cosine * delta_x + sine * delta_y
    across = cosine * delta_y - sine * delta_x
    kernel = thrust[:, column] * jnp.exp(
        -along * along / (2.0 * SIGMA_AXIAL * SIGMA_AXIAL)
        - (across * across + ez * ez) / (2.0 * SIGMA_RADIAL * SIGMA_RADIAL)
    )
    incoming[...] = jnp.where(valid[:, column] > 0, kernel, 0.0).astype(jnp.bfloat16)


def finish(conv, coef, place, table, slots, width, turb_dev, moved_dev, sizes):
    n = sizes[0] * sizes[1]
    groups = -(-slots // LANES)
    vmem = pl.BlockSpec(memory_space=pltpu.VMEM)

    every, plan = pl.pallas_call(
        functools.partial(share_kernel, sizes, slots, width, moved_dev),
        out_shape=(
            jax.ShapeDtypeStruct((n, 2 * groups, LANES), jnp.float32),
            jax.ShapeDtypeStruct((7, RECV, LANES), jnp.float32),
        ),
        in_specs=[vmem] * 4,
        out_specs=(vmem, vmem),
        scratch_shapes=[
            pltpu.VMEM((2 * groups, LANES), jnp.float32),
            pltpu.VMEM((n, 2 * groups, LANES), jnp.float32),
            pltpu.SMEM(place.shape, jnp.int32),
            pltpu.SemaphoreType.DMA,
            pltpu.SemaphoreType.DMA,
            pltpu.SemaphoreType.DMA,
        ],
        compiler_params=pltpu.CompilerParams(
            collective_id=1, has_side_effects=True, vmem_limit_bytes=8 * 1024 * 1024
        ),
        name="share",
    )(conv, coef, place, table)
    return pl.pallas_call(
        functools.partial(finish_kernel, sizes, groups),
        out_shape=(
            jax.ShapeDtypeStruct((2, turb_dev), jnp.float32),
            jax.ShapeDtypeStruct((RECV, KX * KY * KZ), jnp.bfloat16),
        ),
        in_specs=[vmem, vmem, vmem],
        out_specs=(vmem, vmem),
        compiler_params=pltpu.CompilerParams(vmem_limit_bytes=8 * 1024 * 1024),
        name="finish",
    )(every, table, plan)


def body(
    sizes, adjoint, medium, rotors, step_size, slot_turbine, slot_corner, moved_rotors, new_brick
):
    turb_dev, slots = rotors.shape[1], slot_turbine.shape[0]
    state, table = relax(
        adjoint, medium, rotors, step_size, slot_turbine, moved_rotors, new_brick, sizes
    )
    state, conv, coef, place = weigh(state, table, slot_corner, turb_dev, sizes)
    step_taken, incoming = finish(
        conv,
        coef,
        place,
        table,
        slots,
        adjoint.shape[2],
        turb_dev,
        moved_rotors.shape[0],
        sizes,
    )
    return (state, step_taken, incoming)


def solution(mesh):
    sizes = (mesh.shape["gx"], mesh.shape["gy"])
    return jax.shard_map(
        functools.partial(body, sizes),
        mesh=mesh,
        in_specs=(
            P(None, "gx", "gy", None),
            P(None, "gx", "gy", None),
            P(None, ("gx", "gy")),
            P(),
            P(("gx", "gy")),
            P(None, ("gx", "gy")),
            P(("gx", "gy")),
            P(("gx", "gy"), None),
        ),
        out_specs=(P(None, "gx", "gy", None), P(None, ("gx", "gy")), P(("gx", "gy"), None)),
        check_vma=False,
    )
```

```python
import functools

import jax
import jax.numpy as jnp
import numpy as np
from jax import lax
from jax.experimental import pallas as pl
from jax.experimental.pallas import tpu as pltpu
from jax.sharding import PartitionSpec as P

KX = 8
KY = 16
KZ = 16
SWEEPS = 2
RECV = 8
EDGE = 16
CHUNK = 8
LONG = 16
STRIP = 16
LANES = 128
BATCH = 16


TAU = 0.05
SIGMA_AXIAL = 1.5
SIGMA_RADIAL = 4.0
MESH = pl.DeviceIdType.MESH


def strips(rows):
    return [(pl.ds(start, STRIP), pl.ds(8 + start, STRIP)) for start in range(0, rows, STRIP)]


def prepare(med, src, keep, scaled, fb, first, fresh, planes=CHUNK):
    for j in range(planes):
        x = first + j
        for part, mid in strips(src.shape[2]):
            if fresh:
                viscous, velocity, reaction, coupling, source = [
                    TAU * med[i, x, part].astype(jnp.float32) for i in range(5)
                ]
                pull = viscous + velocity
                kept = 1.0 - 5.0 * viscous - (pull + reaction)
                scaled[0, x, part] = viscous
                scaled[1, x, part] = pull
                scaled[2, x, part] = coupling
                scaled[3, x, part] = source
                keep[0, x, part] = kept
                keep[1, x, part] = kept - reaction
            else:
                viscous = scaled[0, x, part]
            for c in range(2):
                fb[c, x + 1, mid] = viscous * src[c, x, part]


def update(src, dst, keep, scaled, fb, first, last, planes=CHUNK):
    rows, depth = src.shape[2:]
    col = lax.broadcasted_iota(jnp.int32, (STRIP, depth), 1)
    bottom, top = col == 0, col == depth - 1
    for start in range(0, rows, STRIP):
        part, mid = pl.ds(start, STRIP), pl.ds(8 + start, STRIP)
        below, above = pl.ds(7 + start, STRIP), pl.ds(9 + start, STRIP)
        values = src[0, first, part], src[1, first, part]
        behind = [fb[c, first, mid].astype(jnp.bfloat16) for c in range(2)]
        for j in range(planes):
            x = first + j
            more = j + 1 < planes or not last
            if more:
                pull = scaled[1, x + 1, part]
                ahead = src[0, x + 1, part], src[1, x + 1, part]
            coupling = scaled[2, x, part]
            here = [fb[c, x + 1, mid].astype(jnp.bfloat16) for c in range(2)]
            zero = jnp.zeros_like(here[0])
            for c in range(2):
                sides = jnp.where(bottom, zero, pltpu.roll(here[c], 1, 1))
                sides = sides + jnp.where(top, zero, pltpu.roll(here[c], depth - 1, 1))
                sides = sides + behind[c]
                total = fb[c, x + 1, below] + fb[c, x + 1, above]
                if more:
                    total = total + pull * ahead[c]
                total = total - coupling * values[1 - c]
                if c == 0:
                    total = total + scaled[3, x, part]
                total = total + sides.astype(jnp.float32)
                dst[c, x, part] = keep[c, x, part] * values[c] + total
            behind = here
            if more:
                values = ahead


def pack_tables(me, rotors, listed, moved, target, step, pack):
    turb_dev, slots, moved_dev = rotors.shape[1], listed.shape[1], moved.shape[1]
    pack[...] = jnp.full(pack.shape, -1.0, jnp.float32)
    own = pl.ds(0, turb_dev)
    pack[0:2, own] = rotors[0:2]
    pack[2:3, own] = jnp.cos(rotors[2:3])
    pack[3:4, own] = jnp.sin(rotors[2:3])
    pack[4:5, own] = rotors[3:4]
    pack[0:1, pl.ds(LANES - 1, 1)] = jnp.full((1, 1), step[...], jnp.float32)
    for group in range(-(-slots // LANES)):
        size = min(LANES, slots - group * LANES)
        pack[5 + group : 6 + group, pl.ds(0, size)] = listed[
            :, pl.ds(group * LANES, size)
        ].astype(jnp.float32)
    full = pack[...]
    lane = lax.broadcasted_iota(jnp.int32, full.shape, 1)
    field = lax.broadcasted_iota(jnp.int32, full.shape, 0) + 2
    line = jnp.full((1, LANES), -1.0, jnp.float32)
    chosen, wanted = moved[...].astype(jnp.float32), target[...].astype(jnp.float32)
    for j in range(moved_dev):
        local = chosen[:, j : j + 1]
        picked = jnp.sum(
            jnp.where(lane.astype(jnp.float32) == local, full, 0.0), axis=1, keepdims=True
        )
        here = (lane == moved_dev * field + j) & (field < 7)
        spread = jnp.sum(jnp.where(here, picked, 0.0), axis=0, keepdims=True)
        place = lane[0:1]
        for f in range(2, 7):
            line = jnp.where(place == moved_dev * f + j, spread, line)
        line = jnp.where(place == j, wanted[:, j : j + 1], line)
        number = (me * turb_dev).astype(jnp.float32) + local
        line = jnp.where(place == moved_dev + j, number, line)
    pack[7:8] = line


def greet(sizes):
    n_gx, n_gy = sizes
    gx, gy = lax.axis_index("gx"), lax.axis_index("gy")
    barrier = pltpu.get_barrier_semaphore()
    for j in range(1, n_gy):
        pl.semaphore_signal(
            barrier, inc=1, device_id=(gx, lax.rem(gy + j, n_gy)), device_id_type=MESH
        )
    for j in range(1, n_gx):
        pl.semaphore_signal(
            barrier, inc=1, device_id=(lax.rem(gx + j, n_gx), gy), device_id_type=MESH
        )
    return n_gx + n_gy - 2


def spread_y(sizes, own, every, ssem, rsem):
    n_gy = sizes[1]
    gx, gy = lax.axis_index("gx"), lax.axis_index("gy")
    return [
        pltpu.make_async_remote_copy(
            src_ref=own,
            dst_ref=every.at[gx * n_gy + gy],
            send_sem=ssem.at[j],
            recv_sem=rsem.at[j],
            device_id=(gx, lax.rem(gy + j, n_gy)),
            device_id_type=MESH,
        )
        for j in range(1, n_gy)
    ]


def spread_x(sizes, every, ssem, rsem):
    n_gx, n_gy = sizes
    gx, gy = lax.axis_index("gx"), lax.axis_index("gy")
    block = every.at[pl.ds(gx * n_gy, n_gy)]
    return [
        pltpu.make_async_remote_copy(
            src_ref=block,
            dst_ref=block,
            send_sem=ssem.at[n_gy + j],
            recv_sem=rsem.at[n_gy + j],
            device_id=(lax.rem(gx + j, n_gx), gy),
            device_id_type=MESH,
        )
        for j in range(1, n_gx)
    ]


def relax_kernel(
    sizes,
    rotors_hbm,
    listed_hbm,
    moved_hbm,
    target_hbm,
    step,
    q_hbm,
    med_hbm,
    q,
    every,
    rotors,
    listed,
    moved,
    target,
    med,
    q1,
    keep,
    scaled,
    fb,
    xs,
    xr,
    ys,
    yb,
    yr,
    pack,
    table,
    small_sem,
    edge_sem,
    in_sem,
    ssem,
    rsem,
    tsend,
    trecv,
):
    n_gx, n_gy = sizes
    _, count, width, depth = q.shape
    chunks = count // CHUNK
    gx, gy = lax.axis_index("gx"), lax.axis_index("gy")
    x_lo, x_hi = lax.rem(gx + n_gx - 1, n_gx), lax.rem(gx + 1, n_gx)
    y_lo, y_hi = lax.rem(gy + n_gy - 1, n_gy), lax.rem(gy + 1, n_gy)
    peers = ((x_lo, gy), (x_hi, gy), (gx, y_lo), (gx, y_hi))
    q_mid, mid = pl.ds(8, width - 16), pl.ds(EDGE, width - 2 * EDGE)
    q_edges = (pl.ds(0, 8), pl.ds(width - 8, 8))
    edges = (pl.ds(0, EDGE), pl.ds(width - EDGE, EDGE))

    def fetch(which, planes, rows, sem):
        src, dst = (q_hbm.at[:], q.at[:]) if which is None else (med_hbm.at[which], med.at[which])
        return pltpu.make_async_copy(src.at[:, planes, rows], dst.at[:, planes, rows], sem)

    whole, end = pl.ds(0, width), pl.ds(count - 1, 1)
    head, tail = pl.ds(0, CHUNK), pl.ds(CHUNK, count - CHUNK)
    every_field, viscous, others = pl.ds(0, 5), pl.ds(0, 1), pl.ds(1, 4)
    head_in = [
        fetch(None, head, whole, in_sem.at[0, 0]),
        fetch(every_field, head, whole, in_sem.at[0, 1]),
    ]
    edge_in = []
    for i in range(2):
        edge_in.append(fetch(None, tail, q_edges[i], edge_sem.at[i, 0]))
        edge_in.append(fetch(viscous, tail, edges[i], edge_sem.at[i, 1]))
    edge_in += [
        fetch(None, end, q_mid, edge_sem.at[2, 0]),
        fetch(viscous, end, mid, edge_sem.at[2, 1]),
    ]

    def chunk_in(i, size=CHUNK):
        part, all_of_it = pl.ds(i * CHUNK, size), pl.ds(i * CHUNK, CHUNK)
        return (
            fetch(None, part, q_mid, in_sem.at[i, 0]),
            fetch(viscous, part, mid, in_sem.at[i, 1]),
            fetch(others, all_of_it, whole, in_sem.at[i, 2]),
        )

    last_in = chunk_in(chunks - 1, CHUNK - 1)
    small = [
        pltpu.make_async_copy(rotors_hbm, rotors, small_sem.at[0]),
        pltpu.make_async_copy(listed_hbm, listed, small_sem.at[1]),
        pltpu.make_async_copy(moved_hbm, moved, small_sem.at[2]),
        pltpu.make_async_copy(target_hbm, target, small_sem.at[3]),
    ]
    for copy in head_in + edge_in + small:
        copy.start()

    @pl.loop(1, chunks - 1)
    def _(i):
        for copy in chunk_in(i):
            copy.start()

    for copy in last_in:
        copy.start()

    barrier = pltpu.get_barrier_semaphore()
    me = gx * n_gy + gy

    met = greet(sizes)
    blank = jnp.zeros((8, depth), jnp.float32)

    @pl.loop(0, count + 2, unroll=2)
    def _(x):
        for c in range(2):
            fb[c, x, pl.ds(0, 8)] = blank
            fb[c, x, pl.ds(8 + width, 8)] = blank

    for c in range(2):
        fb[c, 0, pl.ds(8, width)] = jnp.zeros((width, depth), jnp.float32)
    for copy in small:
        copy.wait()
    pack_tables(me, rotors, listed, moved, target, step, pack)

    has_lo_x, has_hi_x, has_lo_y, has_hi_y = gx > 0, gx < n_gx - 1, gy > 0, gy < n_gy - 1
    sends = (has_lo_x, has_hi_x, has_lo_y, has_hi_y)
    receives = (has_hi_x, has_lo_x, has_hi_y, has_lo_y)

    def face(turn, side):
        src, dst = (xs, xr) if side < 2 else (yb, yr)
        return pltpu.make_async_remote_copy(
            src_ref=src.at[turn, side % 2],
            dst_ref=dst.at[turn, side % 2],
            send_sem=ssem.at[turn, side],
            recv_sem=rsem.at[turn, side],
            device_id=peers[side],
            device_id_type=MESH,
        )

    def send(turn, side):
        @pl.when(sends[side])
        def _():
            face(turn, side).start()

    def exchange(turn, src):
        for c in range(2):
            low, high = med[0, 0].astype(jnp.float32), med[0, count - 1].astype(jnp.float32)
            low = (low + med[1, 0].astype(jnp.float32)) * src[c, 0]
            xs[turn, 0, c] = low.astype(jnp.bfloat16)
            xs[turn, 1, c] = (high * src[c, count - 1]).astype(jnp.bfloat16)

        for side in (0, 1):
            send(turn, side)

        @pl.loop(0, count, unroll=8)
        def _(x):
            low = med[0, x, pl.ds(0, EDGE)].astype(jnp.float32)[:8]
            high = med[0, x, pl.ds(width - EDGE, EDGE)].astype(jnp.float32)[8:]
            for c in range(2):
                ys[0, c, pl.ds(x, 1)] = (low * src[c, x, pl.ds(0, 8)])[:1]
                ys[1, c, pl.ds(x, 1)] = (high * src[c, x, pl.ds(width - 8, 8)])[7:]

        for side in (2, 3):
            yb[turn, side - 2] = ys[side - 2].astype(jnp.bfloat16)
            send(turn, side)

    def patch(turn, dst):
        for side in range(4):

            @pl.when(sends[side])
            def _():
                face(turn, side).wait_send()

            @pl.when(receives[side])
            def _():
                face(turn, side).wait_recv()
                if side < 2:
                    x = 0 if side else count - 1
                    for c in range(2):
                        dst[c, x] = dst[c, x] + TAU * xr[turn, side, c].astype(jnp.float32)
                else:
                    ys[side - 2] = TAU * yr[turn, side - 2].astype(jnp.float32)
                    line = pl.ds(0 if side == 3 else width - 1, 1)

                    @pl.loop(0, count, unroll=16)
                    def _(x):
                        for c in range(2):
                            dst[c, x, line] = dst[c, x, line] + ys[side - 2, c, pl.ds(x, 1)]

    for copy in head_in:
        copy.wait()
    prepare(med, q, keep, scaled, fb, 0, True)
    for copy in edge_in:
        copy.wait()
    pl.semaphore_wait(barrier, met)
    exchange(0, q)

    table[me] = pack[...]
    along_y = spread_y(sizes, pack, table, tsend, trecv)
    for copy in along_y:
        copy.start()

    @pl.loop(0, chunks - 1)
    def _(i):
        @pl.when(i + 1 < chunks - 1)
        def _():
            for copy in chunk_in(i + 1):
                copy.wait()

        @pl.when(i + 1 == chunks - 1)
        def _():
            for copy in last_in:
                copy.wait()

        prepare(med, q, keep, scaled, fb, (i + 1) * CHUNK, True)
        update(q, q1, keep, scaled, fb, i * CHUNK, False)

    update(q, q1, keep, scaled, fb, count - CHUNK, True)

    patch(0, q1)
    exchange(1, q1)
    for copy in along_y:
        copy.wait()
    along_x = spread_x(sizes, table, tsend, trecv)
    for copy in along_x:
        copy.start()

    prepare(med, q1, keep, scaled, fb, 0, False, LONG)

    @pl.loop(0, count // LONG - 1)
    def _(i):
        prepare(med, q1, keep, scaled, fb, (i + 1) * LONG, False, LONG)
        update(q1, q, keep, scaled, fb, i * LONG, False, LONG)

    update(q1, q, keep, scaled, fb, count - LONG, True, LONG)

    for copy in along_x:
        copy.wait()
    every[...] = table[...]
    patch(1, q)


def in_hbm(array):
    return pltpu.with_memory_space_constraint(array, pltpu.HBM)


def relax(adjoint, medium, rotors, step_size, slot_turbine, moved_rotors, new_brick, sizes):
    n = sizes[0] * sizes[1]
    vmem, hbm = pl.BlockSpec(memory_space=pltpu.VMEM), pl.BlockSpec(memory_space=pltpu.HBM)
    channels, count, width, depth = adjoint.shape
    slots, moved_dev = slot_turbine.shape[0], moved_rotors.shape[0]
    return pl.pallas_call(
        functools.partial(relax_kernel, sizes),
        out_shape=(
            jax.ShapeDtypeStruct(adjoint.shape, jnp.float32),
            jax.ShapeDtypeStruct((n, 8, LANES), jnp.float32),
        ),
        in_specs=[hbm] * 4 + [pl.BlockSpec(memory_space=pltpu.SMEM)] + [hbm] * 2,
        out_specs=(vmem, vmem),
        scratch_shapes=[
            pltpu.VMEM(rotors.shape, jnp.float32),
            pltpu.VMEM((1, slots), jnp.int32),
            pltpu.VMEM((1, moved_dev), jnp.int32),
            pltpu.VMEM((1, moved_dev), jnp.int32),
            pltpu.VMEM(medium.shape, jnp.bfloat16),
            pltpu.VMEM(adjoint.shape, jnp.float32),
            pltpu.VMEM(adjoint.shape, jnp.float32),
            pltpu.VMEM((4,) + adjoint.shape[1:], jnp.float32),
            pltpu.VMEM((channels, count + 2, width + 16, depth), jnp.float32),
            pltpu.VMEM((2, 2, channels, width, depth), jnp.bfloat16),
            pltpu.VMEM((2, 2, channels, width, depth), jnp.bfloat16),
            pltpu.VMEM((2, channels, count, depth), jnp.float32),
            pltpu.VMEM((2, 2, channels, count, depth), jnp.bfloat16),
            pltpu.VMEM((2, 2, channels, count, depth), jnp.bfloat16),
            pltpu.VMEM((8, LANES), jnp.float32),
            pltpu.VMEM((n, 8, LANES), jnp.float32),
            pltpu.SemaphoreType.DMA((4,)),
            pltpu.SemaphoreType.DMA((3, 2)),
            pltpu.SemaphoreType.DMA((count // CHUNK, 3)),
            pltpu.SemaphoreType.DMA((2, 4)),
            pltpu.SemaphoreType.DMA((2, 4)),
            pltpu.SemaphoreType.DMA((sizes[0] + sizes[1],)),
            pltpu.SemaphoreType.DMA((sizes[0] + sizes[1],)),
        ],
        compiler_params=pltpu.CompilerParams(
            collective_id=0, has_side_effects=True, vmem_limit_bytes=46 * 1024 * 1024
        ),
        name="relax",
    )(
        in_hbm(rotors),
        in_hbm(slot_turbine.reshape(1, slots)),
        in_hbm(moved_rotors.reshape(1, moved_dev)),
        in_hbm(new_brick.reshape(1, moved_dev)),
        step_size,
        adjoint,
        medium,
    )


def z_weights(depth):
    z = np.arange(depth)[:, None] - np.arange(depth)[None, :]
    height = z + 0.5 - KZ / 2.0
    values = np.exp(-(height**2) / (2.0 * SIGMA_RADIAL**2)) * ((z >= 0) & (z < KZ))
    values = values.astype(np.float32)
    high = values.astype(jnp.bfloat16)
    low = (values - high.astype(np.float32)).astype(jnp.bfloat16)
    return np.block([[high, low], [high, np.zeros_like(low)]])


def weigh_kernel(
    sizes,
    turb_dev,
    corner_hbm,
    profile_hbm,
    table,
    q,
    out_hbm,
    conv,
    coef,
    place,
    corner,
    profile,
    small_sem,
    out_sem,
):
    _, count, width, depth = q.shape
    n, slots = table.shape[0], corner.shape[1]
    groups = -(-slots // LANES)
    me = lax.axis_index("gx") * sizes[1] + lax.axis_index("gy")

    small = [
        pltpu.make_async_copy(profile_hbm, profile, small_sem.at[0]),
        pltpu.make_async_copy(corner_hbm, corner, small_sem.at[1]),
    ]
    parts = out_sem.shape[0]
    share = count // parts
    writes = []
    for i in range(parts):
        part = pl.ds(i * share, share)
        writes.append(
            pltpu.make_async_copy(q.at[:, part], out_hbm.at[:, part], out_sem.at[i])
        )
    for copy in small + writes:
        copy.start()

    own = table[me]
    lane = lax.broadcasted_iota(jnp.int32, (1, LANES), 1)
    owners, locals_ = [], []
    for group in range(groups):
        turbine = jnp.maximum(own[5 + group : 6 + group], 0.0).astype(jnp.int32)
        owners.append(jnp.broadcast_to(lax.div(turbine, turb_dev), (8, LANES)))
        locals_.append(jnp.broadcast_to(lax.rem(turbine, turb_dev), (8, LANES)))

    def gather(d, carry):
        rows = table[d]
        return tuple(
            jnp.where(
                owner == d,
                jnp.take_along_axis(rows, local, axis=1, mode="promise_in_bounds"),
                fields,
            )
            for owner, local, fields in zip(owners, locals_, carry)
        )

    blank = jnp.zeros((8, LANES), jnp.float32)
    gathered = lax.fori_loop(0, n, gather, (blank,) * groups, unroll=16)
    for group, fields in enumerate(gathered):
        sub_x, sub_y, cosine, sine, thrust = [fields[i : i + 1] for i in range(5)]
        cell_y = lax.broadcasted_iota(jnp.int32, (KY, LANES), 0).astype(jnp.float32)
        delta_y = cell_y + (0.5 - KY / 2.0) - sub_y
        for a in range(KX):
            delta_x = (a + 0.5 - KX / 2.0) - sub_x
            along = cosine * delta_x + sine * delta_y
            across = cosine * delta_y - sine * delta_x
            kernel = thrust * jnp.exp(
                -along * along / (2.0 * SIGMA_AXIAL * SIGMA_AXIAL)
                - across * across / (2.0 * SIGMA_RADIAL * SIGMA_RADIAL)
            )
            axial = along * (1.0 / (SIGMA_AXIAL * SIGMA_AXIAL))
            radial = across * (1.0 / (SIGMA_RADIAL * SIGMA_RADIAL))
            coef[0, group, a] = kernel * (axial * cosine - radial * sine)
            coef[1, group, a] = kernel * (axial * sine + radial * cosine)

    for copy in small:
        copy.wait()
    for group in range(groups):
        size = min(LANES, slots - group * LANES)
        part = pl.ds(group * LANES, size)
        first_x = jnp.minimum(corner[0:1, part], count - KX)
        first_y = jnp.minimum(corner[1:2, part], width - KY)
        first_z = jnp.minimum(corner[2:3, part], depth - KZ)
        place[group : group + 1, pl.ds(0, size)] = first_x * width + first_y
        place[groups + group : groups + group + 1, pl.ds(0, size)] = (
            lane[:, :size] - first_z
        ) & (LANES - 1)

    @pl.loop(0, count // BATCH)
    def _(i):
        pieces = []
        for j in range(BATCH):
            plane = q[0, i * BATCH + j]
            high = plane.astype(jnp.bfloat16)
            low = (plane - high.astype(jnp.float32)).astype(jnp.bfloat16)
            pieces.append(jnp.concatenate([high, low], axis=1))
        both = jnp.dot(
            jnp.concatenate(pieces, axis=0), profile[...], preferred_element_type=jnp.float32
        )
        rows = BATCH * width
        conv[pl.ds(pl.multiple_of(i * rows, 8), rows)] = both[:, :depth] + both[:, depth:]

    for copy in writes:
        copy.wait()


def weigh(state, table, slot_corner, turb_dev, sizes):
    _, count, width, depth = state.shape
    slots = slot_corner.shape[1]
    groups = -(-slots // LANES)
    vmem, hbm = pl.BlockSpec(memory_space=pltpu.VMEM), pl.BlockSpec(memory_space=pltpu.HBM)
    profile = jnp.asarray(z_weights(depth))
    return pl.pallas_call(
        functools.partial(weigh_kernel, sizes, turb_dev),
        out_shape=(
            jax.ShapeDtypeStruct(state.shape, jnp.float32),
            jax.ShapeDtypeStruct((count * width, depth), jnp.float32),
            jax.ShapeDtypeStruct((2, groups, KX, KY, LANES), jnp.float32),
            jax.ShapeDtypeStruct((2 * groups, LANES), jnp.int32),
        ),
        in_specs=[hbm, hbm, vmem, vmem],
        out_specs=(hbm, vmem, vmem, vmem),
        scratch_shapes=[
            pltpu.VMEM(slot_corner.shape, jnp.int32),
            pltpu.VMEM(profile.shape, jnp.bfloat16),
            pltpu.SemaphoreType.DMA((2,)),
            pltpu.SemaphoreType.DMA((8,)),
        ],
        compiler_params=pltpu.CompilerParams(vmem_limit_bytes=8 * 1024 * 1024),
        name="weigh",
    )(slot_corner, profile, table, state)


def plan_rows(sizes, moved_dev, table, plan):
    n = sizes[0] * sizes[1]
    me = lax.axis_index("gx") * sizes[1] + lax.axis_index("gy")
    lines = table[:, 7]
    lane = lax.broadcasted_iota(jnp.int32, lines.shape, 1)
    mine = jnp.where((lines == me.astype(jnp.float32)) & (lane < moved_dev), 1.0, 0.0)

    def earlier(size, row, col):
        less = lax.broadcasted_iota(jnp.int32, (size, size), row) < lax.broadcasted_iota(
            jnp.int32, (size, size), col
        )
        return jnp.where(less, 1.0, 0.0).astype(jnp.bfloat16)

    rank = jnp.sum(
        jnp.dot(
            earlier(n, 1, 0), mine.astype(jnp.bfloat16), preferred_element_type=jnp.float32
        ),
        axis=1,
        keepdims=True,
    ) + jnp.dot(
        mine.astype(jnp.bfloat16), earlier(LANES, 0, 1), preferred_element_type=jnp.float32
    )
    shifted = [jnp.ones_like(lines)]
    shifted += [pltpu.roll(lines, LANES - moved_dev * f, 1) for f in range(1, 7)]
    chosen = [jnp.where(rank == float(slot), mine, 0.0) for slot in range(RECV)]
    for i, values in enumerate(shifted):
        parts = [jnp.sum(pick * values, axis=0, keepdims=True) for pick in chosen]
        total = jnp.sum(jnp.concatenate(parts, axis=0), axis=1, keepdims=True)
        plan[i] = jnp.broadcast_to(total, (RECV, LANES))


def share_kernel(
    sizes,
    slots,
    width,
    moved_dev,
    conv,
    coef,
    place_vmem,
    table,
    out,
    plan,
    mine,
    every,
    place,
    place_sem,
    ssem,
    rsem,
):
    n, n_gy = sizes[0] * sizes[1], sizes[1]
    me = lax.axis_index("gx") * n_gy + lax.axis_index("gy")
    barrier = pltpu.get_barrier_semaphore()
    steps = n - 1 if n <= 32 else 1
    fetch = pltpu.make_async_copy(place_vmem, place, place_sem)
    fetch.start()

    def other(d):
        number = lax.rem(me + d, n)
        return lax.div(number, n_gy), lax.rem(number, n_gy)

    @pl.loop(1, n, unroll=steps)
    def _(d):
        pl.semaphore_signal(barrier, inc=1, device_id=other(d), device_id_type=MESH)

    fetch.wait()
    groups = -(-slots // LANES)
    lane = lax.broadcasted_iota(jnp.int32, (KY, LANES), 1)
    for group in range(groups):

        def collect(slot, blocks):
            base, shift = place[group, slot], place[groups + group, slot]
            here = lane == slot
            return tuple(
                jnp.where(here, pltpu.roll(conv[pl.ds(base + a * width, KY)], shift, 1), old)
                for a, old in enumerate(blocks)
            )

        size = min(LANES, slots - group * LANES)
        blank = jnp.zeros((KY, LANES), jnp.float32)
        blocks = lax.fori_loop(0, size, collect, (blank,) * KX, unroll=32)
        for i in range(2):
            total = blocks[0] * coef[i, group, 0]
            for a in range(1, KX):
                total = total + blocks[a] * coef[i, group, a]
            row = i * groups + group
            mine[row : row + 1] = jnp.sum(total, axis=0, keepdims=True)

    every[me] = mine[...]
    pl.semaphore_wait(barrier, n - 1)

    @pl.loop(1, n, unroll=steps)
    def _(d):
        pltpu.make_async_remote_copy(
            src_ref=mine,
            dst_ref=every.at[me],
            send_sem=ssem,
            recv_sem=rsem,
            device_id=other(d),
            device_id_type=MESH,
        ).start()

    plan_rows(sizes, moved_dev, table, plan)
    rest = every.at[pl.ds(0, n - 1)]
    total = pltpu.make_async_remote_copy(
        src_ref=rest,
        dst_ref=rest,
        send_sem=ssem,
        recv_sem=rsem,
        device_id=other(1),
        device_id_type=MESH,
    )
    total.wait()
    out[...] = every[...]


def finish_kernel(sizes, groups, every, table, plan, step_out, incoming):
    n = sizes[0] * sizes[1]
    me = lax.axis_index("gx") * sizes[1] + lax.axis_index("gy")
    turb_dev = step_out.shape[1]
    valid, wanted, sub_x, sub_y, cosine, sine, thrust = [plan[i] for i in range(7)]
    own = (
        me * turb_dev + lax.broadcasted_iota(jnp.int32, (turb_dev, LANES), 0)
    ).astype(jnp.float32)
    targets = jnp.concatenate([own, wanted], axis=0)

    def collect(d, carry):
        sum_x, sum_y = carry
        for group in range(groups):
            hit = targets == table[d, pl.ds(5 + group, 1)]
            sum_x = jnp.where(hit, every[d, pl.ds(group, 1)], sum_x)
            sum_y = jnp.where(hit, every[d, pl.ds(groups + group, 1)], sum_y)
        return sum_x, sum_y

    zero = jnp.zeros((turb_dev + RECV, LANES), jnp.float32)
    sums = lax.fori_loop(0, n, collect, (zero, zero), unroll=8)
    step = table[0, 0:1, LANES - 1 : LANES]
    taken = [
        jnp.clip(-step * jnp.sum(part, axis=1, keepdims=True), -0.5, 0.5) for part in sums
    ]
    flip = lax.broadcasted_iota(jnp.int32, (turb_dev, turb_dev), 0) == lax.broadcasted_iota(
        jnp.int32, (turb_dev, turb_dev), 1
    )
    for i in range(2):
        step_out[i : i + 1] = jnp.sum(
            jnp.where(flip, taken[i][:turb_dev], 0.0), axis=0, keepdims=True
        )
    cells = KX * KY * KZ
    cell = lax.broadcasted_iota(jnp.int32, (RECV, cells), 1)
    ex = (cell // (KY * KZ)).astype(jnp.float32) + 0.5 - KX / 2.0
    ey = lax.rem(cell // KZ, KY).astype(jnp.float32) + 0.5 - KY / 2.0
    ez = lax.rem(cell, KZ).astype(jnp.float32) + 0.5 - KZ / 2.0
    column = slice(0, 1)
    delta_x = ex - (sub_x[:, column] + taken[0][turb_dev:])
    delta_y = ey - (sub_y[:, column] + taken[1][turb_dev:])
    cosine, sine = cosine[:, column], sine[:, column]
    along = cosine * delta_x + sine * delta_y
    across = cosine * delta_y - sine * delta_x
    kernel = thrust[:, column] * jnp.exp(
        -along * along / (2.0 * SIGMA_AXIAL * SIGMA_AXIAL)
        - (across * across + ez * ez) / (2.0 * SIGMA_RADIAL * SIGMA_RADIAL)
    )
    incoming[...] = jnp.where(valid[:, column] > 0, kernel, 0.0).astype(jnp.bfloat16)


def finish(conv, coef, place, table, slots, width, turb_dev, moved_dev, sizes):
    n = sizes[0] * sizes[1]
    groups = -(-slots // LANES)
    vmem = pl.BlockSpec(memory_space=pltpu.VMEM)

    every, plan = pl.pallas_call(
        functools.partial(share_kernel, sizes, slots, width, moved_dev),
        out_shape=(
            jax.ShapeDtypeStruct((n, 2 * groups, LANES), jnp.float32),
            jax.ShapeDtypeStruct((7, RECV, LANES), jnp.float32),
        ),
        in_specs=[vmem] * 4,
        out_specs=(vmem, vmem),
        scratch_shapes=[
            pltpu.VMEM((2 * groups, LANES), jnp.float32),
            pltpu.VMEM((n, 2 * groups, LANES), jnp.float32),
            pltpu.SMEM(place.shape, jnp.int32),
            pltpu.SemaphoreType.DMA,
            pltpu.SemaphoreType.DMA,
            pltpu.SemaphoreType.DMA,
        ],
        compiler_params=pltpu.CompilerParams(
            collective_id=1, has_side_effects=True, vmem_limit_bytes=8 * 1024 * 1024
        ),
        name="share",
    )(conv, coef, place, table)
    return pl.pallas_call(
        functools.partial(finish_kernel, sizes, groups),
        out_shape=(
            jax.ShapeDtypeStruct((2, turb_dev), jnp.float32),
            jax.ShapeDtypeStruct((RECV, KX * KY * KZ), jnp.bfloat16),
        ),
        in_specs=[vmem, vmem, vmem],
        out_specs=(vmem, vmem),
        compiler_params=pltpu.CompilerParams(vmem_limit_bytes=8 * 1024 * 1024),
        name="finish",
    )(every, table, plan)


def body(
    sizes, adjoint, medium, rotors, step_size, slot_turbine, slot_corner, moved_rotors, new_brick
):
    turb_dev, slots = rotors.shape[1], slot_turbine.shape[0]
    state, table = relax(
        adjoint, medium, rotors, step_size, slot_turbine, moved_rotors, new_brick, sizes
    )
    state, conv, coef, place = weigh(state, table, slot_corner, turb_dev, sizes)
    step_taken, incoming = finish(
        conv,
        coef,
        place,
        table,
        slots,
        adjoint.shape[2],
        turb_dev,
        moved_rotors.shape[0],
        sizes,
    )
    return (state, step_taken, incoming)


def solution(mesh):
    sizes = (mesh.shape["gx"], mesh.shape["gy"])
    return jax.shard_map(
        functools.partial(body, sizes),
        mesh=mesh,
        in_specs=(
            P(None, "gx", "gy", None),
            P(None, "gx", "gy", None),
            P(None, ("gx", "gy")),
            P(),
            P(("gx", "gy")),
            P(None, ("gx", "gy")),
            P(("gx", "gy")),
            P(("gx", "gy"), None),
        ),
        out_specs=(P(None, "gx", "gy", None), P(None, ("gx", "gy")), P(("gx", "gy"), None)),
        check_vma=False,
    )
```

```python
import functools

import jax
import jax.numpy as jnp
import numpy as np
from jax import lax
from jax.experimental import pallas as pl
from jax.experimental.pallas import tpu as pltpu
from jax.sharding import PartitionSpec as P

KX = 8
KY = 16
KZ = 16
SWEEPS = 2
RECV = 8
EDGE = 16
CHUNK = 8
LONG = 16
STRIP = 16
LANES = 128
BATCH = 32


TAU = 0.05
SIGMA_AXIAL = 1.5
SIGMA_RADIAL = 4.0
MESH = pl.DeviceIdType.MESH


def strips(rows):
    return [(pl.ds(start, STRIP), pl.ds(8 + start, STRIP)) for start in range(0, rows, STRIP)]


def prepare(med, src, keep, scaled, fb, first, fresh, planes=CHUNK):
    for j in range(planes):
        x = first + j
        for part, mid in strips(src.shape[2]):
            if fresh:
                viscous, velocity, reaction, coupling, source = [
                    TAU * med[i, x, part].astype(jnp.float32) for i in range(5)
                ]
                pull = viscous + velocity
                kept = 1.0 - 5.0 * viscous - (pull + reaction)
                scaled[0, x, part] = viscous
                scaled[1, x, part] = pull
                scaled[2, x, part] = coupling
                scaled[3, x, part] = source
                keep[0, x, part] = kept
                keep[1, x, part] = kept - reaction
            else:
                viscous = scaled[0, x, part]
            for c in range(2):
                fb[c, x + 1, mid] = viscous * src[c, x, part]


def update(src, dst, keep, scaled, fb, first, last, planes=CHUNK):
    rows, depth = src.shape[2:]
    col = lax.broadcasted_iota(jnp.int32, (STRIP, depth), 1)
    bottom, top = col == 0, col == depth - 1
    for start in range(0, rows, STRIP):
        part, mid = pl.ds(start, STRIP), pl.ds(8 + start, STRIP)
        below, above = pl.ds(7 + start, STRIP), pl.ds(9 + start, STRIP)
        values = src[0, first, part], src[1, first, part]
        behind = [fb[c, first, mid].astype(jnp.bfloat16) for c in range(2)]
        for j in range(planes):
            x = first + j
            more = j + 1 < planes or not last
            if more:
                pull = scaled[1, x + 1, part]
                ahead = src[0, x + 1, part], src[1, x + 1, part]
            coupling = scaled[2, x, part]
            here = [fb[c, x + 1, mid].astype(jnp.bfloat16) for c in range(2)]
            zero = jnp.zeros_like(here[0])
            for c in range(2):
                sides = jnp.where(bottom, zero, pltpu.roll(here[c], 1, 1))
                sides = sides + jnp.where(top, zero, pltpu.roll(here[c], depth - 1, 1))
                sides = sides + behind[c]
                total = fb[c, x + 1, below] + fb[c, x + 1, above]
                if more:
                    total = total + pull * ahead[c]
                total = total - coupling * values[1 - c]
                if c == 0:
                    total = total + scaled[3, x, part]
                total = total + sides.astype(jnp.float32)
                dst[c, x, part] = keep[c, x, part] * values[c] + total
            behind = here
            if more:
                values = ahead


def pack_tables(me, rotors, listed, moved, target, step, pack):
    turb_dev, slots, moved_dev = rotors.shape[1], listed.shape[1], moved.shape[1]
    pack[...] = jnp.full(pack.shape, -1.0, jnp.float32)
    own = pl.ds(0, turb_dev)
    pack[0:2, own] = rotors[0:2]
    pack[2:3, own] = jnp.cos(rotors[2:3])
    pack[3:4, own] = jnp.sin(rotors[2:3])
    pack[4:5, own] = rotors[3:4]
    pack[0:1, pl.ds(LANES - 1, 1)] = jnp.full((1, 1), step[...], jnp.float32)
    for group in range(-(-slots // LANES)):
        size = min(LANES, slots - group * LANES)
        pack[5 + group : 6 + group, pl.ds(0, size)] = listed[
            :, pl.ds(group * LANES, size)
        ].astype(jnp.float32)
    full = pack[...]
    lane = lax.broadcasted_iota(jnp.int32, full.shape, 1)
    field = lax.broadcasted_iota(jnp.int32, full.shape, 0) + 2
    line = jnp.full((1, LANES), -1.0, jnp.float32)
    chosen, wanted = moved[...].astype(jnp.float32), target[...].astype(jnp.float32)
    for j in range(moved_dev):
        local = chosen[:, j : j + 1]
        picked = jnp.sum(
            jnp.where(lane.astype(jnp.float32) == local, full, 0.0), axis=1, keepdims=True
        )
        here = (lane == moved_dev * field + j) & (field < 7)
        spread = jnp.sum(jnp.where(here, picked, 0.0), axis=0, keepdims=True)
        place = lane[0:1]
        for f in range(2, 7):
            line = jnp.where(place == moved_dev * f + j, spread, line)
        line = jnp.where(place == j, wanted[:, j : j + 1], line)
        number = (me * turb_dev).astype(jnp.float32) + local
        line = jnp.where(place == moved_dev + j, number, line)
    pack[7:8] = line


def greet(sizes):
    n_gx, n_gy = sizes
    gx, gy = lax.axis_index("gx"), lax.axis_index("gy")
    barrier = pltpu.get_barrier_semaphore()
    for j in range(1, n_gy):
        pl.semaphore_signal(
            barrier, inc=1, device_id=(gx, lax.rem(gy + j, n_gy)), device_id_type=MESH
        )
    for j in range(1, n_gx):
        pl.semaphore_signal(
            barrier, inc=1, device_id=(lax.rem(gx + j, n_gx), gy), device_id_type=MESH
        )
    return n_gx + n_gy - 2


def spread_y(sizes, own, every, ssem, rsem):
    n_gy = sizes[1]
    gx, gy = lax.axis_index("gx"), lax.axis_index("gy")
    return [
        pltpu.make_async_remote_copy(
            src_ref=own,
            dst_ref=every.at[gx * n_gy + gy],
            send_sem=ssem.at[j],
            recv_sem=rsem.at[j],
            device_id=(gx, lax.rem(gy + j, n_gy)),
            device_id_type=MESH,
        )
        for j in range(1, n_gy)
    ]


def spread_x(sizes, every, ssem, rsem):
    n_gx, n_gy = sizes
    gx, gy = lax.axis_index("gx"), lax.axis_index("gy")
    block = every.at[pl.ds(gx * n_gy, n_gy)]
    return [
        pltpu.make_async_remote_copy(
            src_ref=block,
            dst_ref=block,
            send_sem=ssem.at[n_gy + j],
            recv_sem=rsem.at[n_gy + j],
            device_id=(lax.rem(gx + j, n_gx), gy),
            device_id_type=MESH,
        )
        for j in range(1, n_gx)
    ]


def relax_kernel(
    sizes,
    rotors_hbm,
    listed_hbm,
    moved_hbm,
    target_hbm,
    step,
    q_hbm,
    med_hbm,
    q,
    every,
    rotors,
    listed,
    moved,
    target,
    med,
    q1,
    keep,
    scaled,
    fb,
    xs,
    xr,
    ys,
    yb,
    yr,
    pack,
    table,
    small_sem,
    edge_sem,
    in_sem,
    ssem,
    rsem,
    tsend,
    trecv,
):
    n_gx, n_gy = sizes
    _, count, width, depth = q.shape
    chunks = count // CHUNK
    gx, gy = lax.axis_index("gx"), lax.axis_index("gy")
    x_lo, x_hi = lax.rem(gx + n_gx - 1, n_gx), lax.rem(gx + 1, n_gx)
    y_lo, y_hi = lax.rem(gy + n_gy - 1, n_gy), lax.rem(gy + 1, n_gy)
    peers = ((x_lo, gy), (x_hi, gy), (gx, y_lo), (gx, y_hi))
    q_mid, mid = pl.ds(8, width - 16), pl.ds(EDGE, width - 2 * EDGE)
    q_edges = (pl.ds(0, 8), pl.ds(width - 8, 8))
    edges = (pl.ds(0, EDGE), pl.ds(width - EDGE, EDGE))

    def fetch(which, planes, rows, sem):
        src, dst = (q_hbm.at[:], q.at[:]) if which is None else (med_hbm.at[which], med.at[which])
        return pltpu.make_async_copy(src.at[:, planes, rows], dst.at[:, planes, rows], sem)

    whole, end = pl.ds(0, width), pl.ds(count - 1, 1)
    head, tail = pl.ds(0, CHUNK), pl.ds(CHUNK, count - CHUNK)
    every_field, viscous, others = pl.ds(0, 5), pl.ds(0, 1), pl.ds(1, 4)
    head_in = [
        fetch(None, head, whole, in_sem.at[0, 0]),
        fetch(every_field, head, whole, in_sem.at[0, 1]),
    ]
    edge_in = []
    for i in range(2):
        edge_in.append(fetch(None, tail, q_edges[i], edge_sem.at[i, 0]))
        edge_in.append(fetch(viscous, tail, edges[i], edge_sem.at[i, 1]))
    edge_in += [
        fetch(None, end, q_mid, edge_sem.at[2, 0]),
        fetch(viscous, end, mid, edge_sem.at[2, 1]),
    ]

    def chunk_in(i, size=CHUNK):
        part, all_of_it = pl.ds(i * CHUNK, size), pl.ds(i * CHUNK, CHUNK)
        return (
            fetch(None, part, q_mid, in_sem.at[i, 0]),
            fetch(viscous, part, mid, in_sem.at[i, 1]),
            fetch(others, all_of_it, whole, in_sem.at[i, 2]),
        )

    last_in = chunk_in(chunks - 1, CHUNK - 1)
    small = [
        pltpu.make_async_copy(rotors_hbm, rotors, small_sem.at[0]),
        pltpu.make_async_copy(listed_hbm, listed, small_sem.at[1]),
        pltpu.make_async_copy(moved_hbm, moved, small_sem.at[2]),
        pltpu.make_async_copy(target_hbm, target, small_sem.at[3]),
    ]
    for copy in head_in + edge_in + small:
        copy.start()

    @pl.loop(1, chunks - 1)
    def _(i):
        for copy in chunk_in(i):
            copy.start()

    for copy in last_in:
        copy.start()

    barrier = pltpu.get_barrier_semaphore()
    me = gx * n_gy + gy

    met = greet(sizes)
    blank = jnp.zeros((8, depth), jnp.float32)

    @pl.loop(0, count + 2, unroll=2)
    def _(x):
        for c in range(2):
            fb[c, x, pl.ds(0, 8)] = blank
            fb[c, x, pl.ds(8 + width, 8)] = blank

    for c in range(2):
        fb[c, 0, pl.ds(8, width)] = jnp.zeros((width, depth), jnp.float32)
    for copy in small:
        copy.wait()
    pack_tables(me, rotors, listed, moved, target, step, pack)

    has_lo_x, has_hi_x, has_lo_y, has_hi_y = gx > 0, gx < n_gx - 1, gy > 0, gy < n_gy - 1
    sends = (has_lo_x, has_hi_x, has_lo_y, has_hi_y)
    receives = (has_hi_x, has_lo_x, has_hi_y, has_lo_y)

    def face(turn, side):
        src, dst = (xs, xr) if side < 2 else (yb, yr)
        return pltpu.make_async_remote_copy(
            src_ref=src.at[turn, side % 2],
            dst_ref=dst.at[turn, side % 2],
            send_sem=ssem.at[turn, side],
            recv_sem=rsem.at[turn, side],
            device_id=peers[side],
            device_id_type=MESH,
        )

    def send(turn, side):
        @pl.when(sends[side])
        def _():
            face(turn, side).start()

    def exchange(turn, src):
        for c in range(2):
            low, high = med[0, 0].astype(jnp.float32), med[0, count - 1].astype(jnp.float32)
            low = (low + med[1, 0].astype(jnp.float32)) * src[c, 0]
            xs[turn, 0, c] = low.astype(jnp.bfloat16)
            xs[turn, 1, c] = (high * src[c, count - 1]).astype(jnp.bfloat16)

        for side in (0, 1):
            send(turn, side)

        @pl.loop(0, count, unroll=8)
        def _(x):
            low = med[0, x, pl.ds(0, EDGE)].astype(jnp.float32)[:8]
            high = med[0, x, pl.ds(width - EDGE, EDGE)].astype(jnp.float32)[8:]
            for c in range(2):
                ys[0, c, pl.ds(x, 1)] = (low * src[c, x, pl.ds(0, 8)])[:1]
                ys[1, c, pl.ds(x, 1)] = (high * src[c, x, pl.ds(width - 8, 8)])[7:]

        for side in (2, 3):
            yb[turn, side - 2] = ys[side - 2].astype(jnp.bfloat16)
            send(turn, side)

    def patch(turn, dst):
        for side in range(4):

            @pl.when(sends[side])
            def _():
                face(turn, side).wait_send()

            @pl.when(receives[side])
            def _():
                face(turn, side).wait_recv()
                if side < 2:
                    x = 0 if side else count - 1
                    for c in range(2):
                        dst[c, x] = dst[c, x] + TAU * xr[turn, side, c].astype(jnp.float32)
                else:
                    ys[side - 2] = TAU * yr[turn, side - 2].astype(jnp.float32)
                    line = pl.ds(0 if side == 3 else width - 1, 1)

                    @pl.loop(0, count, unroll=16)
                    def _(x):
                        for c in range(2):
                            dst[c, x, line] = dst[c, x, line] + ys[side - 2, c, pl.ds(x, 1)]

    for copy in head_in:
        copy.wait()
    prepare(med, q, keep, scaled, fb, 0, True)
    for copy in edge_in:
        copy.wait()
    pl.semaphore_wait(barrier, met)
    exchange(0, q)

    table[me] = pack[...]
    along_y = spread_y(sizes, pack, table, tsend, trecv)
    for copy in along_y:
        copy.start()

    @pl.loop(0, chunks - 1)
    def _(i):
        @pl.when(i + 1 < chunks - 1)
        def _():
            for copy in chunk_in(i + 1):
                copy.wait()

        @pl.when(i + 1 == chunks - 1)
        def _():
            for copy in last_in:
                copy.wait()

        prepare(med, q, keep, scaled, fb, (i + 1) * CHUNK, True)
        update(q, q1, keep, scaled, fb, i * CHUNK, False)

    update(q, q1, keep, scaled, fb, count - CHUNK, True)

    patch(0, q1)
    exchange(1, q1)
    for copy in along_y:
        copy.wait()
    along_x = spread_x(sizes, table, tsend, trecv)
    for copy in along_x:
        copy.start()

    prepare(med, q1, keep, scaled, fb, 0, False, LONG)

    @pl.loop(0, count // LONG - 1)
    def _(i):
        prepare(med, q1, keep, scaled, fb, (i + 1) * LONG, False, LONG)
        update(q1, q, keep, scaled, fb, i * LONG, False, LONG)

    update(q1, q, keep, scaled, fb, count - LONG, True, LONG)

    for copy in along_x:
        copy.wait()
    every[...] = table[...]
    patch(1, q)


def in_hbm(array):
    return pltpu.with_memory_space_constraint(array, pltpu.HBM)


def relax(adjoint, medium, rotors, step_size, slot_turbine, moved_rotors, new_brick, sizes):
    n = sizes[0] * sizes[1]
    vmem, hbm = pl.BlockSpec(memory_space=pltpu.VMEM), pl.BlockSpec(memory_space=pltpu.HBM)
    channels, count, width, depth = adjoint.shape
    slots, moved_dev = slot_turbine.shape[0], moved_rotors.shape[0]
    return pl.pallas_call(
        functools.partial(relax_kernel, sizes),
        out_shape=(
            jax.ShapeDtypeStruct(adjoint.shape, jnp.float32),
            jax.ShapeDtypeStruct((n, 8, LANES), jnp.float32),
        ),
        in_specs=[hbm] * 4 + [pl.BlockSpec(memory_space=pltpu.SMEM)] + [hbm] * 2,
        out_specs=(vmem, vmem),
        scratch_shapes=[
            pltpu.VMEM(rotors.shape, jnp.float32),
            pltpu.VMEM((1, slots), jnp.int32),
            pltpu.VMEM((1, moved_dev), jnp.int32),
            pltpu.VMEM((1, moved_dev), jnp.int32),
            pltpu.VMEM(medium.shape, jnp.bfloat16),
            pltpu.VMEM(adjoint.shape, jnp.float32),
            pltpu.VMEM(adjoint.shape, jnp.float32),
            pltpu.VMEM((4,) + adjoint.shape[1:], jnp.float32),
            pltpu.VMEM((channels, count + 2, width + 16, depth), jnp.float32),
            pltpu.VMEM((2, 2, channels, width, depth), jnp.bfloat16),
            pltpu.VMEM((2, 2, channels, width, depth), jnp.bfloat16),
            pltpu.VMEM((2, channels, count, depth), jnp.float32),
            pltpu.VMEM((2, 2, channels, count, depth), jnp.bfloat16),
            pltpu.VMEM((2, 2, channels, count, depth), jnp.bfloat16),
            pltpu.VMEM((8, LANES), jnp.float32),
            pltpu.VMEM((n, 8, LANES), jnp.float32),
            pltpu.SemaphoreType.DMA((4,)),
            pltpu.SemaphoreType.DMA((3, 2)),
            pltpu.SemaphoreType.DMA((count // CHUNK, 3)),
            pltpu.SemaphoreType.DMA((2, 4)),
            pltpu.SemaphoreType.DMA((2, 4)),
            pltpu.SemaphoreType.DMA((sizes[0] + sizes[1],)),
            pltpu.SemaphoreType.DMA((sizes[0] + sizes[1],)),
        ],
        compiler_params=pltpu.CompilerParams(
            collective_id=0, has_side_effects=True, vmem_limit_bytes=46 * 1024 * 1024
        ),
        name="relax",
    )(
        in_hbm(rotors),
        in_hbm(slot_turbine.reshape(1, slots)),
        in_hbm(moved_rotors.reshape(1, moved_dev)),
        in_hbm(new_brick.reshape(1, moved_dev)),
        step_size,
        adjoint,
        medium,
    )


def z_weights(depth):
    z = np.arange(depth)[:, None] - np.arange(depth)[None, :]
    height = z + 0.5 - KZ / 2.0
    values = np.exp(-(height**2) / (2.0 * SIGMA_RADIAL**2)) * ((z >= 0) & (z < KZ))
    values = values.astype(np.float32)
    high = values.astype(jnp.bfloat16)
    low = (values - high.astype(np.float32)).astype(jnp.bfloat16)
    return np.block([[high, low], [high, np.zeros_like(low)]])


def weigh_kernel(
    sizes,
    turb_dev,
    corner_hbm,
    profile_hbm,
    table,
    q,
    out_hbm,
    conv,
    coef,
    place,
    corner,
    profile,
    small_sem,
    out_sem,
):
    _, count, width, depth = q.shape
    n, slots = table.shape[0], corner.shape[1]
    groups = -(-slots // LANES)
    me = lax.axis_index("gx") * sizes[1] + lax.axis_index("gy")

    small = [
        pltpu.make_async_copy(profile_hbm, profile, small_sem.at[0]),
        pltpu.make_async_copy(corner_hbm, corner, small_sem.at[1]),
    ]
    parts = out_sem.shape[0]
    share = count // parts
    writes = []
    for i in range(parts):
        part = pl.ds(i * share, share)
        writes.append(
            pltpu.make_async_copy(q.at[:, part], out_hbm.at[:, part], out_sem.at[i])
        )
    for copy in small + writes:
        copy.start()

    own = table[me]
    lane = lax.broadcasted_iota(jnp.int32, (1, LANES), 1)
    owners, locals_ = [], []
    for group in range(groups):
        turbine = jnp.maximum(own[5 + group : 6 + group], 0.0).astype(jnp.int32)
        owners.append(jnp.broadcast_to(lax.div(turbine, turb_dev), (8, LANES)))
        locals_.append(jnp.broadcast_to(lax.rem(turbine, turb_dev), (8, LANES)))

    def gather(d, carry):
        rows = table[d]
        return tuple(
            jnp.where(
                owner == d,
                jnp.take_along_axis(rows, local, axis=1, mode="promise_in_bounds"),
                fields,
            )
            for owner, local, fields in zip(owners, locals_, carry)
        )

    blank = jnp.zeros((8, LANES), jnp.float32)
    gathered = lax.fori_loop(0, n, gather, (blank,) * groups, unroll=16)
    for group, fields in enumerate(gathered):
        sub_x, sub_y, cosine, sine, thrust = [fields[i : i + 1] for i in range(5)]
        cell_y = lax.broadcasted_iota(jnp.int32, (KY, LANES), 0).astype(jnp.float32)
        delta_y = cell_y + (0.5 - KY / 2.0) - sub_y
        for a in range(KX):
            delta_x = (a + 0.5 - KX / 2.0) - sub_x
            along = cosine * delta_x + sine * delta_y
            across = cosine * delta_y - sine * delta_x
            kernel = thrust * jnp.exp(
                -along * along / (2.0 * SIGMA_AXIAL * SIGMA_AXIAL)
                - across * across / (2.0 * SIGMA_RADIAL * SIGMA_RADIAL)
            )
            axial = along * (1.0 / (SIGMA_AXIAL * SIGMA_AXIAL))
            radial = across * (1.0 / (SIGMA_RADIAL * SIGMA_RADIAL))
            coef[0, group, a] = kernel * (axial * cosine - radial * sine)
            coef[1, group, a] = kernel * (axial * sine + radial * cosine)

    for copy in small:
        copy.wait()
    for group in range(groups):
        size = min(LANES, slots - group * LANES)
        part = pl.ds(group * LANES, size)
        first_x = jnp.minimum(corner[0:1, part], count - KX)
        first_y = jnp.minimum(corner[1:2, part], width - KY)
        first_z = jnp.minimum(corner[2:3, part], depth - KZ)
        place[group : group + 1, pl.ds(0, size)] = first_x * width + first_y
        place[groups + group : groups + group + 1, pl.ds(0, size)] = (
            lane[:, :size] - first_z
        ) & (LANES - 1)

    @pl.loop(0, count // BATCH)
    def _(i):
        pieces = []
        for j in range(BATCH):
            plane = q[0, i * BATCH + j]
            high = plane.astype(jnp.bfloat16)
            low = (plane - high.astype(jnp.float32)).astype(jnp.bfloat16)
            pieces.append(jnp.concatenate([high, low], axis=1))
        both = jnp.dot(
            jnp.concatenate(pieces, axis=0), profile[...], preferred_element_type=jnp.float32
        )
        rows = BATCH * width
        conv[pl.ds(pl.multiple_of(i * rows, 8), rows)] = both[:, :depth] + both[:, depth:]

    for copy in writes:
        copy.wait()


def weigh(state, table, slot_corner, turb_dev, sizes):
    _, count, width, depth = state.shape
    slots = slot_corner.shape[1]
    groups = -(-slots // LANES)
    vmem, hbm = pl.BlockSpec(memory_space=pltpu.VMEM), pl.BlockSpec(memory_space=pltpu.HBM)
    profile = jnp.asarray(z_weights(depth))
    return pl.pallas_call(
        functools.partial(weigh_kernel, sizes, turb_dev),
        out_shape=(
            jax.ShapeDtypeStruct(state.shape, jnp.float32),
            jax.ShapeDtypeStruct((count * width, depth), jnp.float32),
            jax.ShapeDtypeStruct((2, groups, KX, KY, LANES), jnp.float32),
            jax.ShapeDtypeStruct((2 * groups, LANES), jnp.int32),
        ),
        in_specs=[hbm, hbm, vmem, vmem],
        out_specs=(hbm, vmem, vmem, vmem),
        scratch_shapes=[
            pltpu.VMEM(slot_corner.shape, jnp.int32),
            pltpu.VMEM(profile.shape, jnp.bfloat16),
            pltpu.SemaphoreType.DMA((2,)),
            pltpu.SemaphoreType.DMA((8,)),
        ],
        compiler_params=pltpu.CompilerParams(vmem_limit_bytes=8 * 1024 * 1024),
        name="weigh",
    )(slot_corner, profile, table, state)


def plan_rows(sizes, moved_dev, table, plan):
    n = sizes[0] * sizes[1]
    me = lax.axis_index("gx") * sizes[1] + lax.axis_index("gy")
    lines = table[:, 7]
    lane = lax.broadcasted_iota(jnp.int32, lines.shape, 1)
    mine = jnp.where((lines == me.astype(jnp.float32)) & (lane < moved_dev), 1.0, 0.0)

    def earlier(size, row, col):
        less = lax.broadcasted_iota(jnp.int32, (size, size), row) < lax.broadcasted_iota(
            jnp.int32, (size, size), col
        )
        return jnp.where(less, 1.0, 0.0).astype(jnp.bfloat16)

    rank = jnp.sum(
        jnp.dot(
            earlier(n, 1, 0), mine.astype(jnp.bfloat16), preferred_element_type=jnp.float32
        ),
        axis=1,
        keepdims=True,
    ) + jnp.dot(
        mine.astype(jnp.bfloat16), earlier(LANES, 0, 1), preferred_element_type=jnp.float32
    )
    shifted = [jnp.ones_like(lines)]
    shifted += [pltpu.roll(lines, LANES - moved_dev * f, 1) for f in range(1, 7)]
    chosen = [jnp.where(rank == float(slot), mine, 0.0) for slot in range(RECV)]
    for i, values in enumerate(shifted):
        parts = [jnp.sum(pick * values, axis=0, keepdims=True) for pick in chosen]
        total = jnp.sum(jnp.concatenate(parts, axis=0), axis=1, keepdims=True)
        plan[i] = jnp.broadcast_to(total, (RECV, LANES))


def share_kernel(
    sizes,
    slots,
    width,
    moved_dev,
    conv,
    coef,
    place_vmem,
    table,
    out,
    plan,
    mine,
    every,
    place,
    place_sem,
    ssem,
    rsem,
):
    n, n_gy = sizes[0] * sizes[1], sizes[1]
    me = lax.axis_index("gx") * n_gy + lax.axis_index("gy")
    barrier = pltpu.get_barrier_semaphore()
    steps = n - 1 if n <= 32 else 1
    fetch = pltpu.make_async_copy(place_vmem, place, place_sem)
    fetch.start()

    def other(d):
        number = lax.rem(me + d, n)
        return lax.div(number, n_gy), lax.rem(number, n_gy)

    @pl.loop(1, n, unroll=steps)
    def _(d):
        pl.semaphore_signal(barrier, inc=1, device_id=other(d), device_id_type=MESH)

    fetch.wait()
    groups = -(-slots // LANES)
    lane = lax.broadcasted_iota(jnp.int32, (KY, LANES), 1)
    for group in range(groups):

        def collect(slot, blocks):
            base, shift = place[group, slot], place[groups + group, slot]
            here = lane == slot
            return tuple(
                jnp.where(here, pltpu.roll(conv[pl.ds(base + a * width, KY)], shift, 1), old)
                for a, old in enumerate(blocks)
            )

        size = min(LANES, slots - group * LANES)
        blank = jnp.zeros((KY, LANES), jnp.float32)
        blocks = lax.fori_loop(0, size, collect, (blank,) * KX, unroll=32)
        for i in range(2):
            total = blocks[0] * coef[i, group, 0]
            for a in range(1, KX):
                total = total + blocks[a] * coef[i, group, a]
            row = i * groups + group
            mine[row : row + 1] = jnp.sum(total, axis=0, keepdims=True)

    every[me] = mine[...]
    pl.semaphore_wait(barrier, n - 1)

    @pl.loop(1, n, unroll=steps)
    def _(d):
        pltpu.make_async_remote_copy(
            src_ref=mine,
            dst_ref=every.at[me],
            send_sem=ssem,
            recv_sem=rsem,
            device_id=other(d),
            device_id_type=MESH,
        ).start()

    plan_rows(sizes, moved_dev, table, plan)
    rest = every.at[pl.ds(0, n - 1)]
    total = pltpu.make_async_remote_copy(
        src_ref=rest,
        dst_ref=rest,
        send_sem=ssem,
        recv_sem=rsem,
        device_id=other(1),
        device_id_type=MESH,
    )
    total.wait()
    out[...] = every[...]


def finish_kernel(sizes, groups, every, table, plan, step_out, incoming):
    n = sizes[0] * sizes[1]
    me = lax.axis_index("gx") * sizes[1] + lax.axis_index("gy")
    turb_dev = step_out.shape[1]
    valid, wanted, sub_x, sub_y, cosine, sine, thrust = [plan[i] for i in range(7)]
    own = (
        me * turb_dev + lax.broadcasted_iota(jnp.int32, (turb_dev, LANES), 0)
    ).astype(jnp.float32)
    targets = jnp.concatenate([own, wanted], axis=0)

    def collect(d, carry):
        sum_x, sum_y = carry
        for group in range(groups):
            hit = targets == table[d, pl.ds(5 + group, 1)]
            sum_x = jnp.where(hit, every[d, pl.ds(group, 1)], sum_x)
            sum_y = jnp.where(hit, every[d, pl.ds(groups + group, 1)], sum_y)
        return sum_x, sum_y

    zero = jnp.zeros((turb_dev + RECV, LANES), jnp.float32)
    sums = lax.fori_loop(0, n, collect, (zero, zero), unroll=8)
    step = table[0, 0:1, LANES - 1 : LANES]
    taken = [
        jnp.clip(-step * jnp.sum(part, axis=1, keepdims=True), -0.5, 0.5) for part in sums
    ]
    flip = lax.broadcasted_iota(jnp.int32, (turb_dev, turb_dev), 0) == lax.broadcasted_iota(
        jnp.int32, (turb_dev, turb_dev), 1
    )
    for i in range(2):
        step_out[i : i + 1] = jnp.sum(
            jnp.where(flip, taken[i][:turb_dev], 0.0), axis=0, keepdims=True
        )
    cells = KX * KY * KZ
    cell = lax.broadcasted_iota(jnp.int32, (RECV, cells), 1)
    ex = (cell // (KY * KZ)).astype(jnp.float32) + 0.5 - KX / 2.0
    ey = lax.rem(cell // KZ, KY).astype(jnp.float32) + 0.5 - KY / 2.0
    ez = lax.rem(cell, KZ).astype(jnp.float32) + 0.5 - KZ / 2.0
    column = slice(0, 1)
    delta_x = ex - (sub_x[:, column] + taken[0][turb_dev:])
    delta_y = ey - (sub_y[:, column] + taken[1][turb_dev:])
    cosine, sine = cosine[:, column], sine[:, column]
    along = cosine * delta_x + sine * delta_y
    across = cosine * delta_y - sine * delta_x
    kernel = thrust[:, column] * jnp.exp(
        -along * along / (2.0 * SIGMA_AXIAL * SIGMA_AXIAL)
        - (across * across + ez * ez) / (2.0 * SIGMA_RADIAL * SIGMA_RADIAL)
    )
    incoming[...] = jnp.where(valid[:, column] > 0, kernel, 0.0).astype(jnp.bfloat16)


def finish(conv, coef, place, table, slots, width, turb_dev, moved_dev, sizes):
    n = sizes[0] * sizes[1]
    groups = -(-slots // LANES)
    vmem = pl.BlockSpec(memory_space=pltpu.VMEM)

    every, plan = pl.pallas_call(
        functools.partial(share_kernel, sizes, slots, width, moved_dev),
        out_shape=(
            jax.ShapeDtypeStruct((n, 2 * groups, LANES), jnp.float32),
            jax.ShapeDtypeStruct((7, RECV, LANES), jnp.float32),
        ),
        in_specs=[vmem] * 4,
        out_specs=(vmem, vmem),
        scratch_shapes=[
            pltpu.VMEM((2 * groups, LANES), jnp.float32),
            pltpu.VMEM((n, 2 * groups, LANES), jnp.float32),
            pltpu.SMEM(place.shape, jnp.int32),
            pltpu.SemaphoreType.DMA,
            pltpu.SemaphoreType.DMA,
            pltpu.SemaphoreType.DMA,
        ],
        compiler_params=pltpu.CompilerParams(
            collective_id=1, has_side_effects=True, vmem_limit_bytes=8 * 1024 * 1024
        ),
        name="share",
    )(conv, coef, place, table)
    return pl.pallas_call(
        functools.partial(finish_kernel, sizes, groups),
        out_shape=(
            jax.ShapeDtypeStruct((2, turb_dev), jnp.float32),
            jax.ShapeDtypeStruct((RECV, KX * KY * KZ), jnp.bfloat16),
        ),
        in_specs=[vmem, vmem, vmem],
        out_specs=(vmem, vmem),
        compiler_params=pltpu.CompilerParams(vmem_limit_bytes=8 * 1024 * 1024),
        name="finish",
    )(every, table, plan)


def body(
    sizes, adjoint, medium, rotors, step_size, slot_turbine, slot_corner, moved_rotors, new_brick
):
    turb_dev, slots = rotors.shape[1], slot_turbine.shape[0]
    state, table = relax(
        adjoint, medium, rotors, step_size, slot_turbine, moved_rotors, new_brick, sizes
    )
    state, conv, coef, place = weigh(state, table, slot_corner, turb_dev, sizes)
    step_taken, incoming = finish(
        conv,
        coef,
        place,
        table,
        slots,
        adjoint.shape[2],
        turb_dev,
        moved_rotors.shape[0],
        sizes,
    )
    return (state, step_taken, incoming)


def solution(mesh):
    sizes = (mesh.shape["gx"], mesh.shape["gy"])
    return jax.shard_map(
        functools.partial(body, sizes),
        mesh=mesh,
        in_specs=(
            P(None, "gx", "gy", None),
            P(None, "gx", "gy", None),
            P(None, ("gx", "gy")),
            P(),
            P(("gx", "gy")),
            P(None, ("gx", "gy")),
            P(("gx", "gy")),
            P(("gx", "gy"), None),
        ),
        out_specs=(P(None, "gx", "gy", None), P(None, ("gx", "gy")), P(("gx", "gy"), None)),
        check_vma=False,
    )
```
